32 devices in a mesh: site: 8 (over z, y), sp: 4 (over x, core).
Axes of the slice: x: 2, y: 2, z: 4, core: 2. Of those that a mesh axis runs over, the one named last changes fastest.
Arguments:
- counts: int32 [8, 5120, 2048], P('site', None, 'sp'), may hold values from 0 to 6
- factors: float32 [8, 16, 5120], P('site'), may hold values from -2.5 to 2.5
- loadings: float32 [2048, 16], P('sp'), may hold values from -0.4 to 0.4
- factor_momenta: float32 [8, 16, 5120], P('site'), may hold values from -6 to 6
- loading_momenta: float32 [2048, 16], P('sp'), may hold values from -6 to 6
- precision: float32 [16], replicated, may hold values from 0.5 to 4
- factor_step: float32 [1], replicated, may hold values from 0.03 to 0.07
- loading_step: float32 [1], replicated, may hold values from 0.0002 to 0.0008
Outputs:
- new_factors: float32 [8, 16, 5120], P('site')
- new_factor_momenta: float32 [8, 16, 5120], P('site')
- new_loadings: float32 [2048, 16], P('sp')
- new_loading_momenta: float32 [2048, 16], P('sp')
- energy: float32 [1], replicated
The draws below stay inside these ranges and needn't reach their ends.
All inputs are finite; a program needn't handle non-finite values.
Results may differ from the reference program's by a relative error of at most 0.0001.
Values sent between devices are 32-bit elements; how exact they have to be, the bound alone decides.
No kernel may reach another device: no remote copies, remote signals or barrier semaphores. Data moves between devices by JAX's collectives and lax.ppermute only.
A program may use at most 128 MiB of HBM per device.

```python
import math
import jax
import jax.numpy as jnp
from jax import lax

K = 16
TX = 80
TY = 64
TGY = 8
TGX = 1
CELLS = 5120
GX = 80
GY = 512
SPECIES = 2048
N_SITE = 8


def plant(drawn, rng, smallest, top_value):
    spot = [jax.random.randint(jax.random.fold_in(rng, axis), (), 0, length) for axis, length in enumerate(drawn.shape)]
    widest = drawn.shape.index(max(drawn.shape))
    beside = spot[:widest] + [(spot[widest] + 1) % drawn.shape[widest]] + spot[widest + 1:]
    return drawn.at[tuple(spot)].set(smallest).at[tuple(beside)].set(top_value)


def steps_of(key, dims, split, smallest, high):
    factor_of = 1.0
    for position, parts in split:
        steps = jax.random.uniform(jax.random.fold_in(jax.random.fold_in(key, 6), position), (parts,), jnp.float32, smallest / len(split), high / len(split))
        factor_of = factor_of * jnp.repeat(jnp.exp(steps), dims[position] // parts).reshape((-1,) + (1,) * (len(dims) - 1 - position))
    return factor_of


def centred(own_key, dims, spread, limit, cuts=(), dtype=jnp.bfloat16):
    entries = jax.random.normal(own_key, dims, jnp.float32) * spread
    if len(cuts) > 0:
        entries = steps_of(own_key, dims, cuts, -0.22, 0.18) * entries
    return jnp.clip(entries, min=-limit, max=limit).astype(dtype)


def setup_inputs(seed: int = 0) -> dict:
    arg_keys = jax.random.split(jax.random.key(seed), 9)
    return {
        "counts": plant(jax.random.randint(arg_keys[0], (N_SITE, CELLS, SPECIES), 0, 7), jax.random.fold_in(arg_keys[0], 1), 0, 6).astype(jnp.int32),
        "factors": centred(arg_keys[1], (N_SITE, K, CELLS), 1.0, 2.5, ((0, 8),), jnp.float32),
        "loadings": centred(arg_keys[2], (SPECIES, K), 0.15, 0.4, ((0, 4),), jnp.float32),
        "factor_momenta": centred(arg_keys[3], (N_SITE, K, CELLS), 1.0, 6.0, ((0, 8),), jnp.float32),
        "loading_momenta": centred(arg_keys[4], (SPECIES, K), 1.0, 6.0, ((0, 4),), jnp.float32),
        "precision": jnp.clip(jnp.exp(jax.random.uniform(arg_keys[5], (K,), jnp.float32, math.log(0.5), math.log(4.0))), 0.5, 4.0),
        "factor_step": jnp.clip(jax.random.uniform(arg_keys[6], (1,), jnp.float32, 0.03, 0.07), 0.03, 0.07),
        "loading_step": jnp.clip(jnp.exp(jax.random.uniform(arg_keys[7], (1,), jnp.float32, math.log(0.0002), math.log(0.0008))), 0.0002, 0.0008),
    }


kappa_sq = 0.25
highest = lax.Precision.HIGHEST


def to_grid(tiles):
    shaped = tiles.reshape(TGX, TGY, K, TX, TY)
    return shaped.transpose(2, 0, 3, 1, 4).reshape(K, TGX * TX, TGY * TY)


def from_grid(whole):
    shaped = whole.reshape(K, TGX, TX, TGY, TY)
    return shaped.transpose(1, 3, 0, 2, 4).reshape(N_SITE, K, TX * TY)


def to_strip(tiles):
    shaped = tiles.reshape(TGX, TGY, K, TX, TY)
    return shaped.transpose(2, 3, 0, 1, 4).reshape(K, TX, TGX * TGY * TY)


def from_strip(strip):
    shaped = strip.reshape(K, TX, TGX, TGY, TY)
    return shaped.transpose(2, 3, 0, 1, 4).reshape(N_SITE, K, TX * TY)


def apply_prior(tiles):
    whole = to_grid(tiles)
    padded = jnp.pad(whole, ((0, 0), (1, 1), (0, 0)))
    vertical = padded[:, 2:, :] + padded[:, :-2, :]
    strip = to_strip(tiles)
    padded_strip = jnp.pad(strip, ((0, 0), (0, 0), (1, 1)))
    horizontal = padded_strip[:, :, 2:] + padded_strip[:, :, :-2]
    beside = from_grid(vertical) + from_strip(horizontal)
    return (kappa_sq + 4.0) * tiles - beside


def poisson_terms(factors, loadings, counts):
    def one_tile(carry, tile_pair):
        tile, tile_counts = tile_pair
        counts_f = tile_counts.astype(jnp.float32)
        log_rate = lax.dot_general(tile, loadings, (((0,), (1,)), ((), ())), precision=highest, preferred_element_type=jnp.float32)
        intensity = jnp.exp(log_rate)
        residual = counts_f - intensity
        factor_part = lax.dot_general(loadings, residual, (((0,), (1,)), ((), ())), precision=highest, preferred_element_type=jnp.float32)
        loading_part = lax.dot_general(residual, tile, (((0,), (1,)), ((), ())), precision=highest, preferred_element_type=jnp.float32)
        loglik = jnp.sum(counts_f * log_rate - intensity)
        return (carry[0] + loading_part, carry[1] + loglik), factor_part

    start = (jnp.zeros((SPECIES, K), jnp.float32), jnp.zeros((), jnp.float32))
    (loading_part, loglik), factor_part = lax.scan(one_tile, start, (factors, counts))
    return factor_part, loading_part, loglik


def gradient(factors, loadings, counts, precision):
    factor_part, loading_part, loglik = poisson_terms(factors, loadings, counts)
    prior = apply_prior(factors)
    factor_grad = factor_part - precision[None, :, None] * prior
    loading_grad = loading_part - loadings
    return factor_grad, loading_grad, loglik, prior


def reference(counts, factors, loadings, factor_momenta, loading_momenta, precision, factor_step, loading_step):
    step_factor = factor_step[0]
    step_loading = loading_step[0]
    factor_grad, loading_grad, _, _ = gradient(factors, loadings, counts, precision)
    half_factor = factor_momenta + 0.5 * step_factor * factor_grad
    half_loading = loading_momenta + 0.5 * step_loading * loading_grad
    new_factors = factors + step_factor * half_factor
    new_loadings = loadings + step_loading * half_loading
    factor_grad, loading_grad, loglik, prior = gradient(new_factors, new_loadings, counts, precision)
    end_factor = half_factor + 0.5 * step_factor * factor_grad
    end_loading = half_loading + 0.5 * step_loading * loading_grad
    potential = -loglik + 0.5 * jnp.sum(precision[None, :, None] * new_factors * prior) + 0.5 * jnp.sum(new_loadings * new_loadings)
    kinetic = 0.5 * jnp.sum(end_factor * end_factor) + 0.5 * jnp.sum(end_loading * end_loading)
    energy = jnp.reshape((potential + kinetic) / (GX * GY * SPECIES), (1,))
    return new_factors, end_factor, new_loadings, end_loading, energy
```

```python
import functools

import jax
import jax.numpy as jnp
from jax import lax
from jax.experimental import pallas as pl
from jax.experimental.pallas import tpu as pltpu
from jax.sharding import PartitionSpec as P

TX = 80
TY = 64
TGY = 8
LANES = 128

kappa_sq = 0.25
LOG2E = 1.4426950408889634
LN2 = 0.6931471805599453
f32, bf16 = jnp.float32, jnp.bfloat16


VMEM = pl.BlockSpec(memory_space=pltpu.VMEM)
SMEM = pl.BlockSpec(memory_space=pltpu.SMEM)
ANY = pl.BlockSpec(memory_space=pl.ANY)


def swap(block, axis, mask):
    return lax.ppermute(block, axis, [(i, i ^ mask) for i in range(lax.axis_size(axis))])


def from_behind(block, axis, distance):
    devices = range(lax.axis_size(axis))
    route = [(i - distance, i) for i in devices if i - distance in devices]
    return lax.ppermute(block, axis, route)


def mask_groups(n):
    groups, stride = [], 1
    while stride < n:
        radix = 2 if stride == 1 or n // stride == 2 else 4
        groups.append([stride * g for g in range(1, radix)])
        stride *= radix
    return groups


def site_terms(block):
    groups = mask_groups(lax.axis_size("site"))
    terms = [block]
    for masks in groups:
        total = functools.reduce(lambda a, b: a + b, terms)
        terms = [total] + [swap(total, "site", m) for m in masks]
    return terms


def call(kernel, name, in_specs, outs, scratch=(), flops=100000):
    return pl.pallas_call(
        kernel,
        in_specs=in_specs,
        out_specs=[VMEM] * len(outs),
        out_shape=[jax.ShapeDtypeStruct(s, f32) for s in outs],
        scratch_shapes=list(scratch),
        name=name,
        compiler_params=pltpu.CompilerParams(vmem_limit_bytes=60 << 20),
    )


def core():
    return lax.rem(lax.axis_index("sp"), 2)


def split3(x):
    h = x.astype(bf16)
    r = x - h.astype(f32)
    m = r.astype(bf16)
    return h, m, (r - m.astype(f32)).astype(bf16)


def dotg(a, b, ca, cb):
    return lax.dot_general(a, b, (((ca,), (cb,)), ((), ())), preferred_element_type=f32)


def evaluate_block(zb, counts, ly, lg, k):
    h, m, l = split3(zb)
    y = dotg(jnp.concatenate([h, h, h, m, m, l], 0), ly, 0, 0)
    i = jnp.exp2(y)
    c = counts.astype(f32)
    r = c - i
    rh = r.astype(bf16)
    rl = (r - rh.astype(f32)).astype(bf16)
    a = dotg(lg, rh, 1, 1)
    b = dotg(lg[:k], rl, 1, 1)
    fac = a[:k] + a[k:] + b
    a = dotg(jnp.concatenate([h, m], 0), rh, 1, 0)
    b = dotg(h, rl, 1, 0)
    load = a[:k] + a[k:] + b
    return fac, load, c, y, i


def fill_loadings(lt, ly_ref, lg_ref):
    h, m, l = split3(lt * f32(LOG2E))
    ly_ref[...] = jnp.concatenate([h, m, l, h, m, h], 0)
    h, m, _ = split3(lt)
    lg_ref[...] = jnp.concatenate([h, m], 0)


def first_kernel(k, half, sub, z_ref, lt_ref, cnt_ref, fac_ref, load_ref, ly_ref, lg_ref, buf_ref, sem):
    c = core()
    steps = half // sub
    rows = cnt_ref.shape[2]

    def copy(i):
        rho = 1 - i // steps
        at = pl.multiple_of(lax.rem(rho + c, 2) * half + (i % steps) * sub, sub)
        return pltpu.make_async_copy(cnt_ref.at[0, pl.ds(at, sub)], buf_ref.at[pl.ds(i * sub, sub)], sem.at[i])

    for i in range(2 * steps):
        copy(i).start()
    fill_loadings(lt_ref[...], ly_ref, lg_ref)
    ly, lg = ly_ref[...], lg_ref[...]
    total = None
    for i in range(2 * steps):
        rho = 1 - i // steps
        at = pl.multiple_of(lax.rem(rho + c, 2) * half + (i % steps) * sub, sub)
        copy(i).wait()
        fac, load, _, _, _ = evaluate_block(z_ref[0, :, pl.ds(at, sub)], buf_ref[pl.ds(i * sub, sub), :], ly, lg, k)
        fac_ref[rho, :, pl.ds((i % steps) * sub, sub)] = fac
        total = load if total is None else total + load
    load_ref[...] = total


def second_kernel(
    k, half, sub, n_terms, *refs
):
    terms = refs[:n_terms]
    zown_ref, zoth_ref, lt_ref, lm_ref, sl_ref, cnt_ref, fac_ref, load_ref, newl_ref, halfl_ref, ly_ref, lg_ref, buf_ref, sem = refs[n_terms:]
    c = core()
    steps = half // sub

    def copy(i):
        rho = 1 - i // steps
        at = pl.multiple_of(lax.rem(rho + c, 2) * half + (i % steps) * sub, sub)
        return pltpu.make_async_copy(cnt_ref.at[0, pl.ds(at, sub)], buf_ref.at[pl.ds(i * sub, sub)], sem.at[i])

    for i in range(2 * steps):
        copy(i).start()
    step = sl_ref[0]
    grad = functools.reduce(lambda a, b: a + b, [t[...] for t in terms]) - lt_ref[...]
    halfl = lm_ref[...] + 0.5 * step * grad
    newl = lt_ref[...] + step * halfl
    halfl_ref[...] = halfl
    newl_ref[...] = newl
    fill_loadings(newl, ly_ref, lg_ref)
    ly, lg = ly_ref[...], lg_ref[...]
    total = None
    lik = None
    for i in range(2 * steps):
        rho = 1 - i // steps
        z_ref = zoth_ref if rho else zown_ref
        copy(i).wait()
        here = pl.ds((i % steps) * sub, sub)
        fac, load, cf, y, inten = evaluate_block(z_ref[:, here], buf_ref[pl.ds(i * sub, sub), :], ly, lg, k)
        fac_ref[rho, :, here] = fac
        total = load if total is None else total + load
        term = jnp.sum((inten - (cf * f32(LN2)) * y).reshape(sub // 8, 8, y.shape[1]), 0)
        lik = term if lik is None else lik + term
    load_ref[:k, :] = total
    load_ref[k:, :] = lik


def lane(shape):
    return lax.broadcasted_iota(jnp.int32, shape, len(shape) - 1)


def pack_rims(vregs, k):
    q = lax.rem(lane((k, LANES)), TY)
    first = jnp.zeros((k, LANES), f32)
    last = jnp.zeros((k, LANES), f32)
    for j, v in enumerate(vregs):
        first = jnp.where(q == j, pltpu.roll(v, j, 1) if j else v, first)
        last = jnp.where(q == j, pltpu.roll(v, (j - TY + 1) % LANES, 1), last)
    return first, last


def prior_of(vregs, lo, hi, left, right, upper, lower, k):
    q = lax.rem(lane((k, LANES)), TY)
    n = len(vregs)
    rows = LANES // TY
    wide = lane((k, LANES))
    out = []
    zero = jnp.zeros((k, LANES), f32)
    for j in range(lo, hi):
        v = vregs[j]
        back = pltpu.roll(v, 1, 1)
        ahead = pltpu.roll(v, LANES - 1, 1)
        lrim = pltpu.roll(left, (LANES - j) % LANES, 1) if j else left
        rrim = pltpu.roll(right, (TY - 1 - j) % LANES, 1)
        beside = jnp.where(q == 0, lrim, back) + jnp.where(q == TY - 1, rrim, ahead)
        prev = vregs[j - 1] if j else upper
        nxt = vregs[j + 1] if j + 1 < n else lower
        shift_down = pltpu.roll(v, TY, 1)
        above = jnp.where(wide < TY, pltpu.roll(prev, TY, 1), shift_down)
        below = jnp.where(wide >= LANES - TY, pltpu.roll(nxt, LANES - TY, 1), pltpu.roll(v, LANES - TY, 1))
        out.append((kappa_sq + 4.0) * v - (above + below + beside))
    return out


def vregs_of(array, k):
    return [array[:, j * LANES : (j + 1) * LANES] for j in range(array.shape[1] // LANES)]


def rims_kernel(k, z_ref, first_ref, last_ref):
    first_ref[...], last_ref[...] = pack_rims(vregs_of(z_ref[0], k), k)


def ahead_kernel(k, half, z_ref, mom_ref, left_ref, right_ref, upper_ref, lower_ref, gain_ref, sf_ref, a_ref, z_own_ref, s_ref):
    c = core()
    step = sf_ref[0]
    out = prior_of(
        vregs_of(z_ref[0], k), 0, 2 * half // LANES, left_ref[...], right_ref[...], upper_ref[...], lower_ref[...], k
    )
    n = half // LANES
    gain = gain_ref[...] * (0.5 * step)
    for j in range(n):
        at = pl.ds(j * LANES, LANES)
        own = jnp.where(c == 0, out[j], out[n + j])
        src = pl.ds(pl.multiple_of(c * half + j * LANES, LANES), LANES)
        a_ref[:, at] = mom_ref[0, :, src] - gain * own
        z_own_ref[:, at] = z_ref[0, :, src]
    s_ref[...] = jnp.full(s_ref.shape, step, f32)


def move_kernel(k, half, own_ref, other_ref, a_ref, z_ref, s_ref, half_ref, moved_ref):
    for j in range(half // LANES):
        at = pl.ds(j * LANES, LANES)
        h = a_ref[:, at] + (0.5 * s_ref[...]) * (own_ref[:, at] + other_ref[:, at])
        half_ref[:, at] = h
        moved_ref[:, at] = z_ref[:, at] + s_ref[...] * h


def join_kernel(k, half, own_ref, oth_ref, full_ref, first_ref, last_ref):
    c = core()
    n = half // LANES
    own, oth = vregs_of(own_ref[...], k), vregs_of(oth_ref[...], k)
    low = [jnp.where(c == 0, a, b) for a, b in zip(own, oth)]
    high = [jnp.where(c == 0, b, a) for a, b in zip(own, oth)]
    vregs = low + high
    for j, v in enumerate(vregs):
        full_ref[0, :, j * LANES : (j + 1) * LANES] = v
    first_ref[...], last_ref[...] = pack_rims(vregs, k)


def behind_kernel(k, half, z_ref, h_ref, left_ref, right_ref, upper_ref, lower_ref, gain_ref, s_ref, a_ref, e_ref):
    c = core()
    out = prior_of(
        vregs_of(z_ref[0], k), 0, 2 * half // LANES, left_ref[...], right_ref[...], upper_ref[...], lower_ref[...], k
    )
    n = half // LANES
    gain = gain_ref[...]
    energy = jnp.zeros((k, LANES), f32)
    for j in range(n):
        at = pl.ds(j * LANES, LANES)
        own = gain * jnp.where(c == 0, out[j], out[n + j])
        src = pl.ds(pl.multiple_of(c * half + j * LANES, LANES), LANES)
        energy = energy + z_ref[0, :, src] * own
        a_ref[:, at] = h_ref[:, at] - (0.5 * s_ref[...]) * own
    e_ref[...] = energy


def end_kernel(k, half, own_ref, other_ref, a_ref, s_ref, pe_ref, end_ref, b_ref):
    energy = pe_ref[...]
    for j in range(half // LANES):
        at = pl.ds(j * LANES, LANES)
        e = a_ref[:, at] + (0.5 * s_ref[...]) * (own_ref[:, at] + other_ref[:, at])
        end_ref[:, at] = e
        energy = energy + e * e
    b_ref[...] = 0.5 * sum(energy[g * 8 : (g + 1) * 8] for g in range(k // 8))


def pair_kernel(half, own_ref, oth_ref, full_ref):
    c = core()
    own, oth = own_ref[...], oth_ref[...]
    full_ref[0, :, :half] = jnp.where(c == 0, own, oth)
    full_ref[0, :, half:] = jnp.where(c == 0, oth, own)


def loading_end_kernel(k, n_terms, *refs):
    terms = refs[:n_terms]
    newl_ref, halfl_ref, sl_ref, end_ref, s_ref = refs[n_terms:]
    total = functools.reduce(lambda a, b: a + b, [t[...] for t in terms])
    newl = newl_ref[...]
    end = halfl_ref[...] + (0.5 * sl_ref[0]) * (total[:k] - newl)
    end_ref[...] = end
    squares = 0.5 * (end * end + newl * newl)
    energy = total[k:] + sum(squares[g * 8 : (g + 1) * 8] for g in range(k // 8))
    s_ref[...] = sum(energy[:, j * LANES : (j + 1) * LANES] for j in range(energy.shape[1] // LANES))


def local(
    counts, factors, loadings, factor_momenta, loading_momenta, precision, factor_step, loading_step
):
    k, cells = factors.shape[1:]
    species = loadings.shape[0]
    half = cells // 2
    sub = 640 if half % 640 == 0 else half
    n_site, n_sp = lax.axis_size("site"), lax.axis_size("sp")
    lt, lm = loadings.T, loading_momenta.T
    gain = jnp.broadcast_to(precision[:, None], (k, LANES))
    zero_rim = jnp.zeros((k, LANES), f32)

    def rims_from(first, last, full):
        left = from_behind(last, "site", 1)
        right = from_behind(first, "site", -1)
        if n_site > TGY:
            low, high = full[0, :, :TY], full[0, :, cells - TY :]
            lead = jnp.zeros((k, LANES - TY), f32)
            upper = jnp.concatenate([lead, from_behind(high, "site", TGY)], 1)
            lower = jnp.concatenate([from_behind(low, "site", -TGY), lead], 1)
        else:
            upper, lower = zero_rim, zero_rim
        return left, right, upper, lower

    def share(fac):
        own = fac[0] + swap(fac[1], "sp", 1)
        terms = [own]
        for masks in mask_groups(n_sp)[1:]:
            total = functools.reduce(lambda a, b: a + b, terms)
            terms = [total] + [swap(total, "sp", m) for m in masks]
        return terms[0], functools.reduce(lambda a, b: a + b, terms[1:])

    scratch = [
        pltpu.VMEM((6 * k, species), bf16),
        pltpu.VMEM((2 * k, species), bf16),
        pltpu.VMEM((cells, species), jnp.int32),
        pltpu.SemaphoreType.DMA((cells // sub,)),
    ]
    fac, load = call(
        functools.partial(first_kernel, k, half, sub), "first", [VMEM, VMEM, ANY], [(2, k, half), (k, species)], scratch
    )(factors, lt, counts)
    load_terms = site_terms(load)
    own, other = share(fac)

    first, last = call(functools.partial(rims_kernel, k), "rims", [VMEM], [(k, LANES)] * 2)(factors)
    a1, z_own, svec = call(
        functools.partial(ahead_kernel, k, half), "ahead", [VMEM] * 7 + [SMEM], [(k, half), (k, half), (k, LANES)]
    )(factors, factor_momenta, *rims_from(first, last, factors), gain, factor_step)
    half_own, moved_own = call(
        functools.partial(move_kernel, k, half), "move", [VMEM] * 5, [(k, half)] * 2
    )(own, other, a1, z_own, svec)
    moved_oth = swap(moved_own, "sp", 1)
    new_factors, first, last = call(
        functools.partial(join_kernel, k, half), "join", [VMEM] * 2, [(1, k, cells), (k, LANES), (k, LANES)]
    )(moved_own, moved_oth)

    fac, load, newl, halfl = call(
        functools.partial(second_kernel, k, half, sub, len(load_terms)),
        "second",
        [VMEM] * (len(load_terms) + 4) + [SMEM, ANY],
        [(2, k, half), (k + 8, species), (k, species), (k, species)],
        scratch,
    )(*load_terms, moved_own, moved_oth, lt, lm, loading_step, counts)
    load_terms = site_terms(load)
    own, other = share(fac)

    a2, prior_energy = call(
        functools.partial(behind_kernel, k, half), "behind", [VMEM] * 8, [(k, half), (k, LANES)]
    )(new_factors, half_own, *rims_from(first, last, new_factors), gain, svec)
    end_own, b_part = call(
        functools.partial(end_kernel, k, half), "end", [VMEM] * 5, [(k, half), (8, LANES)]
    )(own, other, a2, svec, prior_energy)
    end_oth = swap(end_own, "sp", 1)
    (new_momenta,) = call(functools.partial(pair_kernel, half), "pair", [VMEM] * 2, [(1, k, cells)])(end_own, end_oth)

    endl, s_part = call(
        functools.partial(loading_end_kernel, k, len(load_terms)),
        "loading_end",
        [VMEM] * (len(load_terms) + 2) + [SMEM],
        [(k, species), (8, LANES)],
    )(*load_terms, newl, halfl, loading_step)
    for masks in mask_groups(n_sp)[1:]:
        s_part = functools.reduce(lambda a, b: a + b, [s_part] + [swap(s_part, "sp", m) for m in masks])
    total = s_part + functools.reduce(lambda a, b: a + b, site_terms(b_part))
    total = total + swap(total, "sp", 1)
    entries = n_site * cells * n_sp * species
    energy = jnp.reshape(jnp.sum(total) / entries, (1,))
    return new_factors, new_momenta, newl.T, endl.T, energy


def solution(mesh):
    placed = (
        P("site", None, "sp"),
        P("site", None, None),
        P("sp", None),
        P("site", None, None),
        P("sp", None),
        P(),
        P(),
        P(),
    )
    return jax.shard_map(
        local,
        mesh=mesh,
        in_specs=placed,
        out_specs=(P("site", None, None), P("site", None, None), P("sp", None), P("sp", None), P()),
        check_vma=False,
    )
```

```python
import functools

import jax
import jax.numpy as jnp
from jax import lax
from jax.experimental import pallas as pl
from jax.experimental.pallas import tpu as pltpu
from jax.sharding import PartitionSpec as P


TY = 64
TGY = 8
LANES = 128

kappa_sq = 0.25
LOG2E = 1.4426950408889634
LN2 = 0.6931471805599453
f32, bf16 = jnp.float32, jnp.bfloat16


VMEM = pl.BlockSpec(memory_space=pltpu.VMEM)
SMEM = pl.BlockSpec(memory_space=pltpu.SMEM)
HBM = pl.BlockSpec(memory_space=pltpu.HBM)


def swap(block, axis, mask):
    return lax.ppermute(block, axis, [(i, i ^ mask) for i in range(lax.axis_size(axis))])


def from_behind(block, axis, distance):
    devices = range(lax.axis_size(axis))
    route = [(i - distance, i) for i in devices if i - distance in devices]
    return lax.ppermute(block, axis, route)


def mask_groups(n):
    groups, stride = [], 1
    while stride < n:
        radix = 2 if stride == 1 or n // stride == 2 else 4
        groups.append([stride * g for g in range(1, radix)])
        stride *= radix
    return groups


def add(terms):
    return functools.reduce(lambda a, b: a + b, terms)


def sum_terms(block, axis, groups):
    terms = [block]
    for masks in groups:
        total = add(terms)
        terms = [total] + [swap(total, axis, m) for m in masks]
    return terms


def call(kernel, in_specs, outs, scratch=(), limit=4, held=()):
    return pl.pallas_call(
        kernel,
        in_specs=in_specs,
        out_specs=[VMEM] * (len(outs) + len(held)),
        out_shape=[jax.ShapeDtypeStruct(s, f32) for s in outs]
        + [jax.ShapeDtypeStruct(s, jnp.int32) for s in held],
        scratch_shapes=list(scratch),
        compiler_params=pltpu.CompilerParams(vmem_limit_bytes=limit << 20),
    )


def core():
    return lax.rem(lax.axis_index("sp"), 2)


def split3(x):
    h = x.astype(bf16)
    r = x - h.astype(f32)
    m = r.astype(bf16)
    return h, m, (r - m.astype(f32)).astype(bf16)


def dotg(a, b, ca, cb):
    return lax.dot_general(a, b, (((ca,), (cb,)), ((), ())), preferred_element_type=f32)


def evaluate_block(zb, counts, ly, lg, k):
    h, m, l = split3(zb)
    y = dotg(jnp.concatenate([h, h, h, m, m, l], 0), ly, 0, 0)
    i = jnp.exp2(y)
    c = counts.astype(f32)
    r = c - i
    rh = r.astype(bf16)
    rl = (r - rh.astype(f32)).astype(bf16)
    a = dotg(lg, rh, 1, 1)
    b = dotg(lg[:k], rl, 1, 1)
    fac = a[:k] + a[k:] + b
    a = dotg(jnp.concatenate([h, m], 0), rh, 1, 0)
    b = dotg(h, rl, 1, 0)
    load = a[:k] + a[k:] + b
    return fac, load, c, y, i


def fill_loadings(lt, ly_ref, lg_ref):
    h, m, l = split3(lt * f32(LOG2E))
    ly_ref[...] = jnp.concatenate([h, m, l, h, m, h], 0)
    h, m, _ = split3(lt)
    lg_ref[...] = jnp.concatenate([h, m], 0)


def first_kernel(k, half, sub, z_ref, lt_ref, cnt_ref, own_ref, oth_ref, load_ref, buf_ref, ly_ref, lg_ref, sem):
    c = core()
    steps = half // sub

    def copy(i):
        rho = 1 - i // steps
        at = pl.multiple_of(lax.rem(rho + c, 2) * half + (i % steps) * sub, sub)
        return pltpu.make_async_copy(cnt_ref.at[0, pl.ds(at, sub)], buf_ref.at[pl.ds(i * sub, sub)], sem.at[i])

    for i in range(2 * steps):
        copy(i).start()
    fill_loadings(lt_ref[...], ly_ref, lg_ref)
    ly, lg = ly_ref[...], lg_ref[...]
    total = None
    for i in range(2 * steps):
        rho = 1 - i // steps
        at = pl.multiple_of(lax.rem(rho + c, 2) * half + (i % steps) * sub, sub)
        copy(i).wait()
        fac, load, _, _, _ = evaluate_block(z_ref[0, :, pl.ds(at, sub)], buf_ref[pl.ds(i * sub, sub), :], ly, lg, k)
        (oth_ref if rho else own_ref)[:, pl.ds((i % steps) * sub, sub)] = fac
        total = load if total is None else total + load
    load_ref[...] = total


def second_kernel(k, half, sub, n_terms, *refs):
    terms = refs[:n_terms]
    zown_ref, zoth_ref, lt_ref, lm_ref, sl_ref, cnt_ref = refs[n_terms : n_terms + 6]
    own_ref, oth_ref, load_ref, newl_ref, halfl_ref, ly_ref, lg_ref = refs[n_terms + 6 :]
    steps = half // sub
    step = sl_ref[0]
    grad = add([t[...] for t in terms]) - lt_ref[...]
    halfl = lm_ref[...] + 0.5 * step * grad
    newl = lt_ref[...] + step * halfl
    halfl_ref[...] = halfl
    newl_ref[...] = newl
    fill_loadings(newl, ly_ref, lg_ref)
    ly, lg = ly_ref[...], lg_ref[...]
    total = None
    lik = None
    for i in range(2 * steps):
        rho = 1 - i // steps
        z_ref = zoth_ref if rho else zown_ref
        here = pl.ds((i % steps) * sub, sub)
        fac, load, cf, y, inten = evaluate_block(z_ref[:, here], cnt_ref[pl.ds(i * sub, sub), :], ly, lg, k)
        (oth_ref if rho else own_ref)[:, here] = fac
        total = load if total is None else total + load
        term = jnp.sum((inten - (cf * f32(LN2)) * y).reshape(sub // 8, 8, y.shape[1]), 0)
        lik = term if lik is None else lik + term
    load_ref[:k, :] = total
    load_ref[k:, :] = lik


def lane(shape):
    return lax.broadcasted_iota(jnp.int32, shape, len(shape) - 1)


def pack_rims(vregs, k):
    q = lax.rem(lane((k, LANES)), TY)
    first = jnp.zeros((k, LANES), f32)
    last = jnp.zeros((k, LANES), f32)
    for j, v in enumerate(vregs):
        first = jnp.where(q == j, pltpu.roll(v, j, 1) if j else v, first)
        last = jnp.where(q == j, pltpu.roll(v, (j - TY + 1) % LANES, 1), last)
    return first, last


def prior_of(vregs, lo, hi, left, right, upper, lower, k):
    q = lax.rem(lane((k, LANES)), TY)
    n = len(vregs)
    wide = lane((k, LANES))
    out = []
    zero = jnp.zeros((k, LANES), f32)
    for j in range(lo, hi):
        v = vregs[j]
        back = pltpu.roll(v, 1, 1)
        ahead = pltpu.roll(v, LANES - 1, 1)
        lrim = pltpu.roll(left, (LANES - j) % LANES, 1) if j else left
        rrim = pltpu.roll(right, (TY - 1 - j) % LANES, 1)
        beside = jnp.where(q == 0, lrim, back) + jnp.where(q == TY - 1, rrim, ahead)
        prev = vregs[j - 1] if j else upper
        nxt = vregs[j + 1] if j + 1 < n else lower
        shift_down = pltpu.roll(v, TY, 1)
        above = jnp.where(wide < TY, pltpu.roll(prev, TY, 1), shift_down)
        below = jnp.where(wide >= LANES - TY, pltpu.roll(nxt, LANES - TY, 1), pltpu.roll(v, LANES - TY, 1))
        out.append((kappa_sq + 4.0) * v - (above + below + beside))
    return out


def vregs_of(array):
    return [array[:, j * LANES : (j + 1) * LANES] for j in range(array.shape[1] // LANES)]


def rims_kernel(k, z_ref, first_ref, last_ref):
    first_ref[...], last_ref[...] = pack_rims(vregs_of(z_ref[0]), k)


def ahead_kernel(k, half, z_ref, mom_ref, left_ref, right_ref, upper_ref, lower_ref, gain_ref, sf_ref, a_ref, z_own_ref, s_ref):
    c = core()
    step = sf_ref[0]
    out = prior_of(
        vregs_of(z_ref[0]), 0, 2 * half // LANES, left_ref[...], right_ref[...], upper_ref[...], lower_ref[...], k
    )
    n = half // LANES
    gain = gain_ref[...] * (0.5 * step)
    for j in range(n):
        at = pl.ds(j * LANES, LANES)
        own = jnp.where(c == 0, out[j], out[n + j])
        src = pl.ds(pl.multiple_of(c * half + j * LANES, LANES), LANES)
        a_ref[:, at] = mom_ref[0, :, src] - gain * own
        z_own_ref[:, at] = z_ref[0, :, src]
    s_ref[...] = jnp.full(s_ref.shape, step, f32)


def move_kernel(half, own_ref, other_ref, a_ref, z_ref, s_ref, half_ref, moved_ref):
    for j in range(half // LANES):
        at = pl.ds(j * LANES, LANES)
        h = a_ref[:, at] + (0.5 * s_ref[...]) * (own_ref[:, at] + other_ref[:, at])
        half_ref[:, at] = h
        moved_ref[:, at] = z_ref[:, at] + s_ref[...] * h


def join_kernel(k, own_ref, oth_ref, full_ref, first_ref, last_ref):
    c = core()
    own, oth = vregs_of(own_ref[...]), vregs_of(oth_ref[...])
    low = [jnp.where(c == 0, a, b) for a, b in zip(own, oth)]
    high = [jnp.where(c == 0, b, a) for a, b in zip(own, oth)]
    vregs = low + high
    for j, v in enumerate(vregs):
        full_ref[0, :, j * LANES : (j + 1) * LANES] = v
    first_ref[...], last_ref[...] = pack_rims(vregs, k)


def behind_kernel(k, half, z_ref, h_ref, left_ref, right_ref, upper_ref, lower_ref, gain_ref, s_ref, a_ref, e_ref):
    c = core()
    out = prior_of(
        vregs_of(z_ref[0]), 0, 2 * half // LANES, left_ref[...], right_ref[...], upper_ref[...], lower_ref[...], k
    )
    n = half // LANES
    gain = gain_ref[...]
    energy = jnp.zeros((k, LANES), f32)
    for j in range(n):
        at = pl.ds(j * LANES, LANES)
        own = gain * jnp.where(c == 0, out[j], out[n + j])
        src = pl.ds(pl.multiple_of(c * half + j * LANES, LANES), LANES)
        energy = energy + z_ref[0, :, src] * own
        a_ref[:, at] = h_ref[:, at] - (0.5 * s_ref[...]) * own
    e_ref[...] = energy


def end_kernel(k, half, own_ref, other_ref, a_ref, s_ref, pe_ref, end_ref, b_ref):
    energy = pe_ref[...]
    for j in range(half // LANES):
        at = pl.ds(j * LANES, LANES)
        e = a_ref[:, at] + (0.5 * s_ref[...]) * (own_ref[:, at] + other_ref[:, at])
        end_ref[:, at] = e
        energy = energy + e * e
    b_ref[...] = 0.5 * sum(energy[g * 8 : (g + 1) * 8] for g in range(k // 8))


def pair_kernel(half, own_ref, oth_ref, full_ref):
    c = core()
    own, oth = own_ref[...], oth_ref[...]
    full_ref[0, :, :half] = jnp.where(c == 0, own, oth)
    full_ref[0, :, half:] = jnp.where(c == 0, oth, own)


def loading_end_kernel(k, n_terms, *refs):
    terms = refs[:n_terms]
    newl_ref, halfl_ref, sl_ref, end_ref, s_ref = refs[n_terms:]
    total = add([t[...] for t in terms])
    newl = newl_ref[...]
    end = halfl_ref[...] + (0.5 * sl_ref[0]) * (total[:k] - newl)
    end_ref[...] = end
    squares = 0.5 * (end * end + newl * newl)
    energy = total[k:] + sum(squares[g * 8 : (g + 1) * 8] for g in range(k // 8))
    s_ref[...] = sum(energy[:, j * LANES : (j + 1) * LANES] for j in range(energy.shape[1] // LANES))


def local(
    counts, factors, loadings, factor_momenta, loading_momenta, precision, factor_step, loading_step
):
    k, cells = factors.shape[1:]
    species = loadings.shape[0]
    half = cells // 2
    sub = 640 if half % 640 == 0 else half
    n_site, n_sp = lax.axis_size("site"), lax.axis_size("sp")
    site, chips = mask_groups(n_site), mask_groups(n_sp)[1:]
    lt, lm = loadings.T, loading_momenta.T
    gain = jnp.broadcast_to(precision[:, None], (k, LANES))
    zero_rim = jnp.zeros((k, LANES), f32)

    def rims_from(first, last, full):
        left = from_behind(last, "site", 1)
        right = from_behind(first, "site", -1)
        if n_site > TGY:
            low, high = full[0, :, :TY], full[0, :, cells - TY :]
            lead = jnp.zeros((k, LANES - TY), f32)
            upper = jnp.concatenate([lead, from_behind(high, "site", TGY)], 1)
            lower = jnp.concatenate([from_behind(low, "site", -TGY), lead], 1)
        else:
            upper, lower = zero_rim, zero_rim
        return left, right, upper, lower

    def share(own, oth):
        terms = sum_terms(own + swap(oth, "sp", 1), "sp", chips)
        return terms[0], add(terms[1:])

    loadings_scratch = [pltpu.VMEM((6 * k, species), bf16), pltpu.VMEM((2 * k, species), bf16)]
    own, oth, load, held = call(
        functools.partial(first_kernel, k, half, sub),
        [VMEM, VMEM, HBM],
        [(k, half), (k, half), (k, species)],
        loadings_scratch
        + [pltpu.SemaphoreType.DMA((cells // sub,))],
        16,
        [(cells, species)],
    )(factors, lt, pltpu.with_memory_space_constraint(counts, pltpu.HBM))
    load_terms = sum_terms(load, "site", site)
    own, other = share(own, oth)

    first, last = call(functools.partial(rims_kernel, k), [VMEM], [(k, LANES)] * 2)(factors)
    a1, z_own, svec = call(
        functools.partial(ahead_kernel, k, half), [VMEM] * 7 + [SMEM], [(k, half), (k, half), (k, LANES)]
    )(factors, factor_momenta, *rims_from(first, last, factors), gain, factor_step)
    half_own, moved_own = call(
        functools.partial(move_kernel, half), [VMEM] * 5, [(k, half)] * 2
    )(own, other, a1, z_own, svec)
    moved_oth = swap(moved_own, "sp", 1)
    new_factors, first, last = call(
        functools.partial(join_kernel, k), [VMEM] * 2, [(1, k, cells), (k, LANES), (k, LANES)]
    )(moved_own, moved_oth)

    own, oth, load, newl, halfl = call(
        functools.partial(second_kernel, k, half, sub, len(load_terms)),
        [VMEM] * (len(load_terms) + 4) + [SMEM, VMEM],
        [(k, half), (k, half), (k + 8, species), (k, species), (k, species)],
        loadings_scratch,
        20,
    )(*load_terms, moved_own, moved_oth, lt, lm, loading_step, held)
    load_terms = sum_terms(load, "site", site)
    own, other = share(own, oth)

    a2, prior_energy = call(
        functools.partial(behind_kernel, k, half), [VMEM] * 8, [(k, half), (k, LANES)]
    )(new_factors, half_own, *rims_from(first, last, new_factors), gain, svec)
    end_own, b_part = call(
        functools.partial(end_kernel, k, half), [VMEM] * 5, [(k, half), (8, LANES)]
    )(own, other, a2, svec, prior_energy)
    end_oth = swap(end_own, "sp", 1)
    (new_momenta,) = call(functools.partial(pair_kernel, half), [VMEM] * 2, [(1, k, cells)])(end_own, end_oth)

    endl, s_part = call(
        functools.partial(loading_end_kernel, k, len(load_terms)),
        [VMEM] * (len(load_terms) + 2) + [SMEM],
        [(k, species), (8, LANES)],
    )(*load_terms, newl, halfl, loading_step)
    total = add(sum_terms(s_part, "sp", chips) + sum_terms(b_part, "site", site))
    total = total + swap(total, "sp", 1)
    entries = n_site * cells * n_sp * species
    energy = jnp.reshape(jnp.sum(total) / entries, (1,))
    return new_factors, new_momenta, newl.T, endl.T, energy


def solution(mesh):
    placed = (
        P("site", None, "sp"),
        P("site", None, None),
        P("sp", None),
        P("site", None, None),
        P("sp", None),
        P(),
        P(),
        P(),
    )

    return jax.shard_map(
        local,
        mesh=mesh,
        in_specs=placed,
        out_specs=(P("site", None, None), P("site", None, None), P("sp", None), P("sp", None), P()),
        check_vma=False,
    )
```

```python
import functools

import jax
import jax.numpy as jnp
from jax import lax
from jax.experimental import pallas as pl
from jax.experimental.pallas import tpu as pltpu
from jax.sharding import PartitionSpec as P


TY = 64
TGY = 8
LANES = 128

kappa_sq = 0.25
LOG2E = 1.4426950408889634
LN2 = 0.6931471805599453
f32, bf16 = jnp.float32, jnp.bfloat16


VMEM = pl.BlockSpec(memory_space=pltpu.VMEM)
SMEM = pl.BlockSpec(memory_space=pltpu.SMEM)
HBM = pl.BlockSpec(memory_space=pltpu.HBM)


def swap(block, axis, mask):
    return lax.ppermute(block, axis, [(i, i ^ mask) for i in range(lax.axis_size(axis))])


def from_behind(block, axis, distance):
    devices = range(lax.axis_size(axis))
    route = [(i - distance, i) for i in devices if i - distance in devices]
    return lax.ppermute(block, axis, route)


def paired(block, axis, first):
    n = lax.axis_size(axis)
    return lax.ppermute(block, axis, [(i, (i + 1 if (i - first) % 2 == 0 else i - 1) % n) for i in range(n)])


def mask_groups(n):
    groups, stride = [], 1
    while stride < n:
        radix = 2 if stride == 1 or n // stride == 2 else 4
        groups.append([stride * g for g in range(1, radix)])
        stride *= radix
    return groups


def add(terms):
    return functools.reduce(lambda a, b: a + b, terms)


def sum_terms(block, axis, groups):
    terms = [block]
    for masks in groups:
        total = add(terms)
        terms = [total] + [swap(total, axis, m) for m in masks]
    return terms


def call(kernel, in_specs, outs, scratch=(), limit=4, held=()):
    return pl.pallas_call(
        kernel,
        in_specs=in_specs,
        out_specs=[VMEM] * (len(outs) + len(held)),
        out_shape=[jax.ShapeDtypeStruct(s, f32) for s in outs]
        + [jax.ShapeDtypeStruct(s, jnp.int32) for s in held],
        scratch_shapes=list(scratch),
        compiler_params=pltpu.CompilerParams(vmem_limit_bytes=limit << 20),
    )


def core():
    return lax.rem(lax.axis_index("sp"), 2)


def split3(x):
    h = x.astype(bf16)
    r = x - h.astype(f32)
    m = r.astype(bf16)
    return h, m, (r - m.astype(f32)).astype(bf16)


def dotg(a, b, ca, cb):
    return lax.dot_general(a, b, (((ca,), (cb,)), ((), ())), preferred_element_type=f32)


def evaluate_block(zb, counts, ly, lg, k):
    h, m, l = split3(zb)
    y = dotg(jnp.concatenate([h, h, h, m, m, l], 0), ly, 0, 0)
    i = jnp.exp2(y)
    c = counts.astype(f32)
    r = c - i
    rh = r.astype(bf16)
    rl = (r - rh.astype(f32)).astype(bf16)
    a = dotg(lg, rh, 1, 1)
    b = dotg(lg[:k], rl, 1, 1)
    fac = a[:k] + a[k:] + b
    a = dotg(jnp.concatenate([h, m], 0), rh, 1, 0)
    b = dotg(h, rl, 1, 0)
    load = a[:k] + a[k:] + b
    return fac, load, c, y, i


def fill_loadings(lt, ly_ref, lg_ref):
    h, m, l = split3(lt * f32(LOG2E))
    ly_ref[...] = jnp.concatenate([h, m, l, h, m, h], 0)
    h, m, _ = split3(lt)
    lg_ref[...] = jnp.concatenate([h, m], 0)


def first_kernel(
    k, half, sub, z_hbm, lt_hbm, cnt_ref, own_ref, oth_ref, load_ref, buf_ref, ly_ref, lg_ref, z_ref, lt_ref, sem, sems
):
    c = core()
    steps = half // sub

    def copy(i):
        rho = 1 - i // steps
        at = pl.multiple_of(lax.rem(rho + c, 2) * half + (i % steps) * sub, sub)
        return pltpu.make_async_copy(cnt_ref.at[0, pl.ds(at, sub)], buf_ref.at[pl.ds(i * sub, sub)], sem.at[i])

    small = [
        pltpu.make_async_copy(lt_hbm, lt_ref, sems.at[0]),
        pltpu.make_async_copy(z_hbm, z_ref, sems.at[1]),
    ]
    for job in small:
        job.start()
    for i in range(2 * steps):
        copy(i).start()
    small[0].wait()
    fill_loadings(lt_ref[...], ly_ref, lg_ref)
    small[1].wait()
    ly, lg = ly_ref[...], lg_ref[...]
    total = None
    for i in range(2 * steps):
        rho = 1 - i // steps
        at = pl.multiple_of(lax.rem(rho + c, 2) * half + (i % steps) * sub, sub)
        copy(i).wait()
        fac, load, _, _, _ = evaluate_block(z_ref[0, :, pl.ds(at, sub)], buf_ref[pl.ds(i * sub, sub), :], ly, lg, k)
        (oth_ref if rho else own_ref)[:, pl.ds((i % steps) * sub, sub)] = fac
        total = load if total is None else total + load
    load_ref[...] = total


def second_kernel(k, half, sub, n_terms, *refs):
    terms = refs[:n_terms]
    zown_ref, zoth_ref, lt_ref, lm_ref, sl_ref, cnt_ref = refs[n_terms : n_terms + 6]
    own_ref, oth_ref, load_ref, out_ref, newl_ref, halfl_ref, ly_ref, lg_ref = refs[n_terms + 6 :]
    steps = half // sub
    step = sl_ref[0]
    grad = add([t[...] for t in terms]) - lt_ref[...]
    halfl = lm_ref[...] + 0.5 * step * grad
    newl = lt_ref[...] + step * halfl
    halfl_ref[...] = halfl
    newl_ref[...] = newl
    out_ref[...] = newl
    fill_loadings(newl, ly_ref, lg_ref)
    ly, lg = ly_ref[...], lg_ref[...]
    total = None
    lik = None
    for i in range(2 * steps):
        rho = 1 - i // steps
        z_ref = zoth_ref if rho else zown_ref
        here = pl.ds((i % steps) * sub, sub)
        fac, load, cf, y, inten = evaluate_block(z_ref[:, here], cnt_ref[pl.ds(i * sub, sub), :], ly, lg, k)
        (oth_ref if rho else own_ref)[:, here] = fac
        total = load if total is None else total + load
        term = jnp.sum((inten - (cf * f32(LN2)) * y).reshape(sub // 8, 8, y.shape[1]), 0)
        lik = term if lik is None else lik + term
    load_ref[:k, :] = total
    load_ref[k:, :] = lik


def lane(shape):
    return lax.broadcasted_iota(jnp.int32, shape, len(shape) - 1)


def pack_rims(vregs, k):
    q = lax.rem(lane((k, LANES)), TY)
    first = jnp.zeros((k, LANES), f32)
    last = jnp.zeros((k, LANES), f32)
    for j, v in enumerate(vregs):
        first = jnp.where(q == j, pltpu.roll(v, j, 1) if j else v, first)
        last = jnp.where(q == j, pltpu.roll(v, (j - TY + 1) % LANES, 1), last)
    return first, last


def prior_of(vregs, lo, hi, left, right, upper, lower, k):
    q = lax.rem(lane((k, LANES)), TY)
    n = len(vregs)
    wide = lane((k, LANES))
    out = []
    zero = jnp.zeros((k, LANES), f32)
    for j in range(lo, hi):
        v = vregs[j]
        back = pltpu.roll(v, 1, 1)
        ahead = pltpu.roll(v, LANES - 1, 1)
        lrim = pltpu.roll(left, (LANES - j) % LANES, 1) if j else left
        rrim = pltpu.roll(right, (TY - 1 - j) % LANES, 1)
        beside = jnp.where(q == 0, lrim, back) + jnp.where(q == TY - 1, rrim, ahead)
        prev = vregs[j - 1] if j else upper
        nxt = vregs[j + 1] if j + 1 < n else lower
        shift_down = pltpu.roll(v, TY, 1)
        above = jnp.where(wide < TY, pltpu.roll(prev, TY, 1), shift_down)
        below = jnp.where(wide >= LANES - TY, pltpu.roll(nxt, LANES - TY, 1), pltpu.roll(v, LANES - TY, 1))
        out.append((kappa_sq + 4.0) * v - (above + below + beside))
    return out


def sides(near, far):
    me, n = lax.axis_index("site"), lax.axis_size("site")
    even = lax.rem(me, 2) == 0
    left = jnp.where(me == 0, 0.0, jnp.where(even, far, near))
    right = jnp.where(me == n - 1, 0.0, jnp.where(even, near, far))
    return left, right


def rims_of(vregs, k):
    first, last = pack_rims(vregs, k)
    even = lax.rem(lax.axis_index("site"), 2) == 0
    return jnp.where(even, last, first), jnp.where(even, first, last)


def vregs_of(array):
    return [array[:, j * LANES : (j + 1) * LANES] for j in range(array.shape[1] // LANES)]


def rims_kernel(k, z_ref, near_ref, far_ref):
    near_ref[...], far_ref[...] = rims_of(vregs_of(z_ref[0]), k)


def ahead_kernel(k, half, z_ref, mom_ref, near_ref, far_ref, upper_ref, lower_ref, gain_ref, sf_ref, a_ref, z_own_ref, s_ref):
    c = core()
    step = sf_ref[0]
    left, right = sides(near_ref[...], far_ref[...])
    out = prior_of(vregs_of(z_ref[0]), 0, 2 * half // LANES, left, right, upper_ref[...], lower_ref[...], k)
    n = half // LANES
    gain = gain_ref[...] * (0.5 * step)
    for j in range(n):
        at = pl.ds(j * LANES, LANES)
        own = jnp.where(c == 0, out[j], out[n + j])
        src = pl.ds(pl.multiple_of(c * half + j * LANES, LANES), LANES)
        a_ref[:, at] = mom_ref[0, :, src] - gain * own
        z_own_ref[:, at] = z_ref[0, :, src]
    s_ref[...] = jnp.full(s_ref.shape, step, f32)


def move_kernel(half, own_ref, other_ref, a_ref, z_ref, s_ref, half_ref, moved_ref):
    for j in range(half // LANES):
        at = pl.ds(j * LANES, LANES)
        h = a_ref[:, at] + (0.5 * s_ref[...]) * (own_ref[:, at] + other_ref[:, at])
        half_ref[:, at] = h
        moved_ref[:, at] = z_ref[:, at] + s_ref[...] * h


def in_order(own, oth):
    first = core() == 0
    own, oth = vregs_of(own), vregs_of(oth)
    return [jnp.where(first, a, b) for a, b in zip(own, oth)] + [jnp.where(first, b, a) for a, b in zip(own, oth)]


def join_kernel(k, own_ref, oth_ref, near_ref, far_ref):
    near_ref[...], far_ref[...] = rims_of(in_order(own_ref[...], oth_ref[...]), k)


def behind_kernel(k, half, own_ref, oth_ref, h_ref, near_ref, far_ref, upper_ref, lower_ref, gain_ref, s_ref, a_ref, e_ref):
    c = core()
    left, right = sides(near_ref[...], far_ref[...])
    z = in_order(own_ref[...], oth_ref[...])
    out = prior_of(z, 0, 2 * half // LANES, left, right, upper_ref[...], lower_ref[...], k)
    n = half // LANES
    gain = gain_ref[...]
    energy = jnp.zeros((k, LANES), f32)
    for j in range(n):
        at = pl.ds(j * LANES, LANES)
        own = gain * jnp.where(c == 0, out[j], out[n + j])
        energy = energy + own_ref[:, at] * own
        a_ref[:, at] = h_ref[:, at] - (0.5 * s_ref[...]) * own
    e_ref[...] = energy


def end_kernel(k, half, own_ref, other_ref, a_ref, s_ref, pe_ref, end_ref, b_ref):
    energy = pe_ref[...]
    for j in range(half // LANES):
        at = pl.ds(j * LANES, LANES)
        e = a_ref[:, at] + (0.5 * s_ref[...]) * (own_ref[:, at] + other_ref[:, at])
        end_ref[:, at] = e
        energy = energy + e * e
    b_ref[...] = 0.5 * sum(energy[g * 8 : (g + 1) * 8] for g in range(k // 8))


def pair_kernel(half, own_ref, oth_ref, full_ref):
    c = core()
    own, oth = own_ref[...], oth_ref[...]
    full_ref[0, :, :half] = jnp.where(c == 0, own, oth)
    full_ref[0, :, half:] = jnp.where(c == 0, oth, own)


def loading_end_kernel(k, n_terms, *refs):
    terms = refs[:n_terms]
    newl_ref, halfl_ref, sl_ref, end_ref, s_ref = refs[n_terms:]
    total = add([t[...] for t in terms])
    newl = newl_ref[...]
    end = halfl_ref[...] + (0.5 * sl_ref[0]) * (total[:k] - newl)
    end_ref[...] = end
    squares = 0.5 * (end * end + newl * newl)
    energy = total[k:] + sum(squares[g * 8 : (g + 1) * 8] for g in range(k // 8))
    s_ref[...] = sum(energy[:, j * LANES : (j + 1) * LANES] for j in range(energy.shape[1] // LANES))


def local(
    counts, factors, loadings, factor_momenta, loading_momenta, precision, factor_step, loading_step
):
    k, cells = factors.shape[1:]
    species = loadings.shape[0]
    half = cells // 2
    sub = 640 if half % 640 == 0 else half
    n_site, n_sp = lax.axis_size("site"), lax.axis_size("sp")
    site, chips = mask_groups(n_site), mask_groups(n_sp)[1:]
    lt, lm = loadings.T, loading_momenta.T
    gain = jnp.broadcast_to(precision[:, None], (k, LANES))
    zero_rim = jnp.zeros((k, LANES), f32)

    def rims_from(near, far, low, high):
        near = paired(near, "site", 0)
        far = paired(far, "site", 1)
        if n_site > TGY:
            lead = jnp.zeros((k, LANES - TY), f32)
            upper = jnp.concatenate([lead, from_behind(high, "site", TGY)], 1)
            lower = jnp.concatenate([from_behind(low, "site", -TGY), lead], 1)
        else:
            upper, lower = zero_rim, zero_rim
        return near, far, upper, lower

    def share(own, oth):
        terms = sum_terms(own + swap(oth, "sp", 1), "sp", chips)
        return terms[0], add(terms[1:])

    loadings_scratch = [pltpu.VMEM((6 * k, species), bf16), pltpu.VMEM((2 * k, species), bf16)]
    own, oth, load, held = call(
        functools.partial(first_kernel, k, half, sub),
        [HBM, HBM, HBM],
        [(k, half), (k, half), (k, species)],
        loadings_scratch
        + [
            pltpu.VMEM((1, k, cells), f32),
            pltpu.VMEM((k, species), f32),
            pltpu.SemaphoreType.DMA((cells // sub,)),
            pltpu.SemaphoreType.DMA((2,)),
        ],
        16,
        [(cells, species)],
    )(*[pltpu.with_memory_space_constraint(x, pltpu.HBM) for x in (factors, lt, counts)])
    load_terms = sum_terms(load, "site", site)
    own, other = share(own, oth)

    near, far = call(functools.partial(rims_kernel, k), [VMEM], [(k, LANES)] * 2)(factors)
    a1, z_own, svec = call(
        functools.partial(ahead_kernel, k, half), [VMEM] * 7 + [SMEM], [(k, half), (k, half), (k, LANES)]
    )(factors, factor_momenta, *rims_from(near, far, factors[0, :, :TY], factors[0, :, cells - TY :]), gain, factor_step)
    half_own, moved_own = call(
        functools.partial(move_kernel, half), [VMEM] * 5, [(k, half)] * 2
    )(own, other, a1, z_own, svec)
    moved_oth = swap(moved_own, "sp", 1)
    near, far = call(functools.partial(join_kernel, k), [VMEM] * 2, [(k, LANES)] * 2)(moved_own, moved_oth)
    (new_factors,) = call(functools.partial(pair_kernel, half), [VMEM] * 2, [(1, k, cells)])(moved_own, moved_oth)

    own, oth, load, new_loadings, newl, halfl = call(
        functools.partial(second_kernel, k, half, sub, len(load_terms)),
        [VMEM] * (len(load_terms) + 4) + [SMEM, VMEM],
        [(k, half), (k, half), (k + 8, species)] + [(k, species)] * 3,
        loadings_scratch,
        20,
    )(*load_terms, moved_own, moved_oth, lt, lm, loading_step, held)
    load_terms = sum_terms(load, "site", site)
    own, other = share(own, oth)

    edges = new_factors[0, :, :TY], new_factors[0, :, cells - TY :]
    a2, prior_energy = call(
        functools.partial(behind_kernel, k, half), [VMEM] * 9, [(k, half), (k, LANES)]
    )(moved_own, moved_oth, half_own, *rims_from(near, far, *edges), gain, svec)
    end_own, b_part = call(
        functools.partial(end_kernel, k, half), [VMEM] * 5, [(k, half), (8, LANES)]
    )(own, other, a2, svec, prior_energy)
    end_oth = swap(end_own, "sp", 1)
    (new_momenta,) = call(functools.partial(pair_kernel, half), [VMEM] * 2, [(1, k, cells)])(end_own, end_oth)

    endl, s_part = call(
        functools.partial(loading_end_kernel, k, len(load_terms)),
        [VMEM] * (len(load_terms) + 2) + [SMEM],
        [(k, species), (8, LANES)],
    )(*load_terms, newl, halfl, loading_step)
    total = add(sum_terms(s_part, "sp", chips) + sum_terms(b_part, "site", site))
    total = total + swap(total, "sp", 1)
    entries = n_site * cells * n_sp * species
    energy = jnp.reshape(jnp.sum(total) / entries, (1,))
    return new_factors, new_momenta, new_loadings.T, endl.T, energy


def solution(mesh):
    placed = (
        P("site", None, "sp"),
        P("site", None, None),
        P("sp", None),
        P("site", None, None),
        P("sp", None),
        P(),
        P(),
        P(),
    )

    return jax.shard_map(
        local,
        mesh=mesh,
        in_specs=placed,
        out_specs=(P("site", None, None), P("site", None, None), P("sp", None), P("sp", None), P()),
        check_vma=False,
    )
```

```python
import functools

import jax
import jax.numpy as jnp
from jax import lax
from jax.experimental import pallas as pl
from jax.experimental.pallas import tpu as pltpu
from jax.sharding import PartitionSpec as P


TY = 64
TGY = 8
LANES = 128

kappa_sq = 0.25
LOG2E = 1.4426950408889634
LN2 = 0.6931471805599453
f32, bf16 = jnp.float32, jnp.bfloat16


VMEM = pl.BlockSpec(memory_space=pltpu.VMEM)
SMEM = pl.BlockSpec(memory_space=pltpu.SMEM)
HBM = pl.BlockSpec(memory_space=pltpu.HBM)


def swap(block, axis, mask):
    return lax.ppermute(block, axis, [(i, i ^ mask) for i in range(lax.axis_size(axis))])


def from_behind(block, axis, distance):
    devices = range(lax.axis_size(axis))
    route = [(i - distance, i) for i in devices if i - distance in devices]
    return lax.ppermute(block, axis, route)


def paired(block, axis, first):
    n = lax.axis_size(axis)
    route = [(i, i + 1 if (i - first) % 2 == 0 else i - 1) for i in range(n)]
    return lax.ppermute(block, axis, [(i, j) for i, j in route if 0 <= j < n])


def mask_groups(n):
    groups, stride = [], 1
    while stride < n:
        radix = 2 if stride == 1 or n // stride == 2 else 4
        groups.append([stride * g for g in range(1, radix)])
        stride *= radix
    return groups


def add(terms):
    return functools.reduce(lambda a, b: a + b, terms)


def sum_terms(block, axis, groups):
    terms = [block]
    for masks in groups:
        total = add(terms)
        terms = [total] + [swap(total, axis, m) for m in masks]
    return terms


def call(kernel, in_specs, outs, scratch=(), limit=4, packed=()):
    return pl.pallas_call(
        kernel,
        in_specs=in_specs,
        out_specs=[VMEM] * len(outs),
        out_shape=[jax.ShapeDtypeStruct(s, bf16 if i in packed else f32) for i, s in enumerate(outs)],
        scratch_shapes=list(scratch),
        compiler_params=pltpu.CompilerParams(vmem_limit_bytes=limit << 20),
    )


def core():
    return lax.rem(lax.axis_index("sp"), 2)


def split3(x):
    h = x.astype(bf16)
    r = x - h.astype(f32)
    m = r.astype(bf16)
    return h, m, (r - m.astype(f32)).astype(bf16)


def dotg(a, b, ca, cb):
    return lax.dot_general(a, b, (((ca,), (cb,)), ((), ())), preferred_element_type=f32)


def residuals(zb, c, ly):
    h, m, l = split3(zb)
    y = dotg(jnp.concatenate([h, h, h, m, m, l], 0), ly, 0, 0)
    i = jnp.exp2(y)
    r = c - i
    rh = r.astype(bf16)
    return y, i, rh, (r - rh.astype(f32)).astype(bf16), h, m


def factor_terms(rh, rl, lg, k):
    a = dotg(lg, rh, 1, 1)
    return a[:k] + a[k:] + dotg(lg[k:], rl, 1, 1)


def loading_terms(h, m, rh, rl, k):
    a = dotg(jnp.concatenate([m, h], 0), rh, 1, 0)
    return a[:k] + a[k:] + dotg(h, rl, 1, 0)


def fill_loadings(lt, ly_ref, lg_ref):
    h, m, l = split3(lt * f32(LOG2E))
    ly_ref[...] = jnp.concatenate([h, m, l, h, m, h], 0)
    h, m, _ = split3(lt)
    lg_ref[...] = jnp.concatenate([m, h], 0)


def rows_to_8(x):
    return jnp.sum(x.reshape(x.shape[0] // 8, 8, x.shape[1]), 0)


DEPTH = 3


def first_kernel(
    k, half, sub, z_hbm, lt_hbm, cnt_ref, load_ref, lg_ref, held_ref, rh_ref, rl_ref, ly_ref, z_ref, lt_ref, buf_ref, sem, sems
):
    c = core()
    steps = half // sub
    slots = DEPTH + 1

    def place(i):
        return pl.multiple_of(lax.rem((1 - i // steps) + c, 2) * half + (i % steps) * sub, sub)

    def copy(i):
        return pltpu.make_async_copy(
            cnt_ref.at[0, pl.ds(place(i), sub)], buf_ref.at[pl.ds((i % slots) * sub, sub)], sem.at[i]
        )

    small = [
        pltpu.make_async_copy(lt_hbm, lt_ref, sems.at[0]),
        pltpu.make_async_copy(z_hbm, z_ref, sems.at[1]),
    ]
    for job in small:
        job.start()
    for i in range(min(DEPTH, 2 * steps)):
        copy(i).start()
    small[0].wait()
    fill_loadings(lt_ref[...], ly_ref, lg_ref)
    small[1].wait()
    ly = ly_ref[...]
    loads = []
    for i in range(2 * steps):
        copy(i).wait()
        if i + DEPTH < 2 * steps:
            copy(i + DEPTH).start()
        cf = buf_ref[pl.ds((i % slots) * sub, sub), :].astype(f32)
        rows = pl.ds(i * sub, sub)
        held_ref[rows, :] = cf
        _, _, rh, rl, h, m = residuals(z_ref[0, :, pl.ds(place(i), sub)], cf, ly)
        rh_ref[rows, :] = rh
        rl_ref[rows, :] = rl
        loads.append(loading_terms(h, m, rh, rl, k))
    load_ref[...] = add(loads)


def factor_kernel(k, half, sub, start, lg_ref, rh_ref, rl_ref, fac_ref):
    lg = lg_ref[...]
    for i in range(half // sub):
        rows = pl.ds(start + i * sub, sub)
        fac_ref[:, i * sub : (i + 1) * sub] = factor_terms(rh_ref[rows, :], rl_ref[rows, :], lg, k)


def move_loadings_kernel(n_terms, *refs):
    terms = refs[:n_terms]
    lt_ref, lm_ref, sl_ref, out_ref, newl_ref, halfl_ref, ly_ref, lg_ref = refs[n_terms:]
    step = sl_ref[0]
    halfl = lm_ref[...] + 0.5 * step * (add([t[...] for t in terms]) - lt_ref[...])
    newl = lt_ref[...] + step * halfl
    halfl_ref[...] = halfl
    newl_ref[...] = newl
    out_ref[...] = newl
    fill_loadings(newl, ly_ref, lg_ref)


def second_kernel(k, half, sub, start, z_ref, ly_ref, lg_ref, cnt_ref, fac_ref, lik_ref, rh_ref, rl_ref):
    ly, lg = ly_ref[...], lg_ref[...]
    likes, sums = [], []
    for i in range(half // sub):
        rows = pl.ds(i * sub, sub)
        cf = cnt_ref[pl.ds(start + i * sub, sub), :]
        y, inten, rh, rl, _, _ = residuals(z_ref[:, rows], cf, ly)
        rh_ref[rows, :] = rh
        rl_ref[rows, :] = rl
        fac_ref[:, rows] = factor_terms(rh, rl, lg, k)
        likes.append(rows_to_8(cf * y))
        sums.append(rows_to_8(inten))
    lik_ref[...] = add(sums) - f32(LN2) * add(likes)


def loading_kernel(k, half, sub, zo_ref, rho_ref, rlo_ref, zw_ref, rhw_ref, rlw_ref, liko_ref, likw_ref, load_ref):
    loads = []
    for z_ref, rh_ref, rl_ref in ((zo_ref, rho_ref, rlo_ref), (zw_ref, rhw_ref, rlw_ref)):
        for i in range(half // sub):
            rows = pl.ds(i * sub, sub)
            h, m, _ = split3(z_ref[:, rows])
            loads.append(loading_terms(h, m, rh_ref[rows, :], rl_ref[rows, :], k))
    load_ref[:k, :] = add(loads)
    load_ref[k:, :] = liko_ref[...] + likw_ref[...]


def lane(shape):
    return lax.broadcasted_iota(jnp.int32, shape, len(shape) - 1)


def pack_rims(vregs, k):
    q = lax.rem(lane((k, LANES)), TY)
    first = jnp.zeros((k, LANES), f32)
    last = jnp.zeros((k, LANES), f32)
    for j, v in enumerate(vregs):
        first = jnp.where(q == j, pltpu.roll(v, j, 1) if j else v, first)
        last = jnp.where(q == j, pltpu.roll(v, (j - TY + 1) % LANES, 1), last)
    return first, last


def prior_of(vregs, lo, hi, left, right, upper, lower, k):
    q = lax.rem(lane((k, LANES)), TY)
    n = len(vregs)
    wide = lane((k, LANES))
    out = []
    zero = jnp.zeros((k, LANES), f32)
    for j in range(lo, hi):
        v = vregs[j]
        back = pltpu.roll(v, 1, 1)
        ahead = pltpu.roll(v, LANES - 1, 1)
        lrim = pltpu.roll(left, (LANES - j) % LANES, 1) if j else left
        rrim = pltpu.roll(right, (TY - 1 - j) % LANES, 1)
        beside = jnp.where(q == 0, lrim, back) + jnp.where(q == TY - 1, rrim, ahead)
        prev = vregs[j - 1] if j else upper
        nxt = vregs[j + 1] if j + 1 < n else lower
        shift_down = pltpu.roll(v, TY, 1)
        above = jnp.where(wide < TY, pltpu.roll(prev, TY, 1), shift_down)
        below = jnp.where(wide >= LANES - TY, pltpu.roll(nxt, LANES - TY, 1), pltpu.roll(v, LANES - TY, 1))
        out.append((kappa_sq + 4.0) * v - (above + below + beside))
    return out


def sides(near, far):
    me, n = lax.axis_index("site"), lax.axis_size("site")
    even = lax.rem(me, 2) == 0
    left = jnp.where(me == 0, 0.0, jnp.where(even, far, near))
    right = jnp.where(me == n - 1, 0.0, jnp.where(even, near, far))
    return left, right


def rims_of(vregs, k):
    first, last = pack_rims(vregs, k)
    even = lax.rem(lax.axis_index("site"), 2) == 0
    return jnp.where(even, last, first), jnp.where(even, first, last)


def vregs_of(array):
    return [array[:, j * LANES : (j + 1) * LANES] for j in range(array.shape[1] // LANES)]


def rims_kernel(k, z_ref, near_ref, far_ref):
    near_ref[...], far_ref[...] = rims_of(vregs_of(z_ref[0]), k)


def ahead_kernel(k, half, z_ref, mom_ref, near_ref, far_ref, upper_ref, lower_ref, gain_ref, sf_ref, a_ref, z_own_ref, s_ref):
    c = core()
    step = sf_ref[0]
    left, right = sides(near_ref[...], far_ref[...])
    out = prior_of(vregs_of(z_ref[0]), 0, 2 * half // LANES, left, right, upper_ref[...], lower_ref[...], k)
    n = half // LANES
    gain = gain_ref[...] * (0.5 * step)
    for j in range(n):
        at = pl.ds(j * LANES, LANES)
        own = jnp.where(c == 0, out[j], out[n + j])
        src = pl.ds(pl.multiple_of(c * half + j * LANES, LANES), LANES)
        a_ref[:, at] = mom_ref[0, :, src] - gain * own
        z_own_ref[:, at] = z_ref[0, :, src]
    s_ref[...] = jnp.full(s_ref.shape, step, f32)


def move_kernel(half, own_ref, other_ref, a_ref, z_ref, s_ref, half_ref, moved_ref):
    for j in range(half // LANES):
        at = pl.ds(j * LANES, LANES)
        h = a_ref[:, at] + (0.5 * s_ref[...]) * (own_ref[:, at] + other_ref[:, at])
        half_ref[:, at] = h
        moved_ref[:, at] = z_ref[:, at] + s_ref[...] * h


def in_order(own, oth):
    first = core() == 0
    own, oth = vregs_of(own), vregs_of(oth)
    return [jnp.where(first, a, b) for a, b in zip(own, oth)] + [jnp.where(first, b, a) for a, b in zip(own, oth)]


def join_kernel(k, own_ref, oth_ref, near_ref, far_ref):
    near_ref[...], far_ref[...] = rims_of(in_order(own_ref[...], oth_ref[...]), k)


def behind_kernel(k, half, own_ref, oth_ref, h_ref, near_ref, far_ref, upper_ref, lower_ref, gain_ref, s_ref, a_ref, e_ref):
    c = core()
    left, right = sides(near_ref[...], far_ref[...])
    z = in_order(own_ref[...], oth_ref[...])
    out = prior_of(z, 0, 2 * half // LANES, left, right, upper_ref[...], lower_ref[...], k)
    n = half // LANES
    gain = gain_ref[...]
    energy = jnp.zeros((k, LANES), f32)
    for j in range(n):
        at = pl.ds(j * LANES, LANES)
        own = gain * jnp.where(c == 0, out[j], out[n + j])
        energy = energy + own_ref[:, at] * own
        a_ref[:, at] = h_ref[:, at] - (0.5 * s_ref[...]) * own
    e_ref[...] = energy


def end_kernel(k, half, own_ref, other_ref, a_ref, s_ref, pe_ref, end_ref, b_ref):
    energy = pe_ref[...]
    for j in range(half // LANES):
        at = pl.ds(j * LANES, LANES)
        e = a_ref[:, at] + (0.5 * s_ref[...]) * (own_ref[:, at] + other_ref[:, at])
        end_ref[:, at] = e
        energy = energy + e * e
    b_ref[...] = 0.5 * sum(energy[g * 8 : (g + 1) * 8] for g in range(k // 8))


def pair_kernel(half, own_ref, oth_ref, full_ref):
    c = core()
    own, oth = own_ref[...], oth_ref[...]
    full_ref[0, :, :half] = jnp.where(c == 0, own, oth)
    full_ref[0, :, half:] = jnp.where(c == 0, oth, own)


def loading_end_kernel(k, n_terms, *refs):
    terms = refs[:n_terms]
    newl_ref, halfl_ref, sl_ref, end_ref, s_ref = refs[n_terms:]
    total = add([t[...] for t in terms])
    newl = newl_ref[...]
    end = halfl_ref[...] + (0.5 * sl_ref[0]) * (total[:k] - newl)
    end_ref[...] = end
    squares = 0.5 * (end * end + newl * newl)
    energy = total[k:] + sum(squares[g * 8 : (g + 1) * 8] for g in range(k // 8))
    s_ref[...] = sum(energy[:, j * LANES : (j + 1) * LANES] for j in range(energy.shape[1] // LANES))


def local(
    counts, factors, loadings, factor_momenta, loading_momenta, precision, factor_step, loading_step
):
    k, cells = factors.shape[1:]
    species = loadings.shape[0]
    half = cells // 2
    sub = 640 if half % 640 == 0 else half
    n_site, n_sp = lax.axis_size("site"), lax.axis_size("sp")
    site, chips = mask_groups(n_site), mask_groups(n_sp)[1:]
    lt, lm = loadings.T, loading_momenta.T
    gain = jnp.broadcast_to(precision[:, None], (k, LANES))
    zero_rim = jnp.zeros((k, LANES), f32)

    def rims_from(near, far, low, high):
        near = paired(near, "site", 0)
        far = paired(far, "site", 1)
        if n_site > TGY:
            lead = jnp.zeros((k, LANES - TY), f32)
            upper = jnp.concatenate([lead, from_behind(high, "site", TGY)], 1)
            lower = jnp.concatenate([from_behind(low, "site", -TGY), lead], 1)
        else:
            upper, lower = zero_rim, zero_rim
        return near, far, upper, lower

    def share(own, oth):
        terms = sum_terms(own + swap(oth, "sp", 1), "sp", chips)
        return terms[0], add(terms[1:])

    rates, grads = (6 * k, species), (2 * k, species)
    load, lg, held, rh, rl = call(
        functools.partial(first_kernel, k, half, sub),
        [HBM, HBM, HBM],
        [(k, species), grads, (cells, species), (cells, species), (cells, species)],
        [
            pltpu.VMEM(rates, bf16),
            pltpu.VMEM((1, k, cells), f32),
            pltpu.VMEM((k, species), f32),
            pltpu.VMEM(((DEPTH + 1) * sub, species), jnp.int32),
            pltpu.SemaphoreType.DMA((cells // sub,)),
            pltpu.SemaphoreType.DMA((2,)),
        ],
        12,
        (1, 3, 4),
    )(*[pltpu.with_memory_space_constraint(x, pltpu.HBM) for x in (factors, lt, counts)])
    load_terms = sum_terms(load, "site", site)
    oth, own = [
        call(functools.partial(factor_kernel, k, half, sub, start), [VMEM] * 3, [(k, half)])(lg, rh, rl)[0]
        for start in (0, half)
    ]
    own, other = share(own, oth)

    near, far = call(functools.partial(rims_kernel, k), [VMEM], [(k, LANES)] * 2)(factors)
    a1, z_own, svec = call(
        functools.partial(ahead_kernel, k, half), [VMEM] * 7 + [SMEM], [(k, half), (k, half), (k, LANES)]
    )(factors, factor_momenta, *rims_from(near, far, factors[0, :, :TY], factors[0, :, cells - TY :]), gain, factor_step)
    half_own, moved_own = call(
        functools.partial(move_kernel, half), [VMEM] * 5, [(k, half)] * 2
    )(own, other, a1, z_own, svec)
    moved_oth = swap(moved_own, "sp", 1)
    near, far = call(functools.partial(join_kernel, k), [VMEM] * 2, [(k, LANES)] * 2)(moved_own, moved_oth)
    (new_factors,) = call(functools.partial(pair_kernel, half), [VMEM] * 2, [(1, k, cells)])(moved_own, moved_oth)

    new_loadings, newl, halfl, ly, lg = call(
        functools.partial(move_loadings_kernel, len(load_terms)),
        [VMEM] * (len(load_terms) + 2) + [SMEM],
        [(k, species)] * 3 + [rates, grads],
        packed=(3, 4),
    )(*load_terms, lt, lm, loading_step)
    (oth, lik_oth, *parts_oth), (own, lik_own, *parts_own) = [
        call(
            functools.partial(second_kernel, k, half, sub, start),
            [VMEM] * 4,
            [(k, half), (8, species), (half, species), (half, species)],
            limit=8,
            packed=(2, 3),
        )(z, ly, lg, held)
        for start, z in ((0, moved_oth), (half, moved_own))
    ]
    (load,) = call(functools.partial(loading_kernel, k, half, sub), [VMEM] * 8, [(k + 8, species)])(
        moved_oth, *parts_oth, moved_own, *parts_own, lik_oth, lik_own
    )
    load_terms = sum_terms(load, "site", site)
    own, other = share(own, oth)

    edges = new_factors[0, :, :TY], new_factors[0, :, cells - TY :]
    a2, prior_energy = call(
        functools.partial(behind_kernel, k, half), [VMEM] * 9, [(k, half), (k, LANES)]
    )(moved_own, moved_oth, half_own, *rims_from(near, far, *edges), gain, svec)
    end_own, b_part = call(
        functools.partial(end_kernel, k, half), [VMEM] * 5, [(k, half), (8, LANES)]
    )(own, other, a2, svec, prior_energy)
    end_oth = swap(end_own, "sp", 1)
    (new_momenta,) = call(functools.partial(pair_kernel, half), [VMEM] * 2, [(1, k, cells)])(end_own, end_oth)

    endl, s_part = call(
        functools.partial(loading_end_kernel, k, len(load_terms)),
        [VMEM] * (len(load_terms) + 2) + [SMEM],
        [(k, species), (8, LANES)],
    )(*load_terms, newl, halfl, loading_step)
    total = add(sum_terms(s_part, "sp", chips) + sum_terms(b_part, "site", site))
    total = total + swap(total, "sp", 1)
    entries = n_site * cells * n_sp * species
    energy = jnp.reshape(jnp.sum(total) / entries, (1,))
    return new_factors, new_momenta, new_loadings.T, endl.T, energy


def solution(mesh):
    placed = (
        P("site", None, "sp"),
        P("site", None, None),
        P("sp", None),
        P("site", None, None),
        P("sp", None),
        P(),
        P(),
        P(),
    )

    return jax.shard_map(
        local,
        mesh=mesh,
        in_specs=placed,
        out_specs=(P("site", None, None), P("site", None, None), P("sp", None), P("sp", None), P()),
        check_vma=False,
    )
```

```python
import functools

import jax
import jax.numpy as jnp
from jax import lax
from jax.experimental import pallas as pl
from jax.experimental.pallas import tpu as pltpu
from jax.sharding import PartitionSpec as P


TY = 64
TGY = 8
LANES = 128

kappa_sq = 0.25
LOG2E = 1.4426950408889634
LN2 = 0.6931471805599453
f32, bf16 = jnp.float32, jnp.bfloat16


VMEM = pl.BlockSpec(memory_space=pltpu.VMEM)
SMEM = pl.BlockSpec(memory_space=pltpu.SMEM)
HBM = pl.BlockSpec(memory_space=pltpu.HBM)


def swap(block, axis, mask):
    return lax.ppermute(block, axis, [(i, i ^ mask) for i in range(lax.axis_size(axis))])


def from_behind(block, axis, distance):
    devices = range(lax.axis_size(axis))
    route = [(i - distance, i) for i in devices if i - distance in devices]
    return lax.ppermute(block, axis, route)


def paired(block, axis, first):
    n = lax.axis_size(axis)
    route = [(i, i + 1 if (i - first) % 2 == 0 else i - 1) for i in range(n)]
    return lax.ppermute(block, axis, [(i, j) for i, j in route if 0 <= j < n])


def mask_groups(n):
    groups, stride = [], 1
    while stride < n:
        radix = 2 if stride == 1 or n // stride == 2 else 4
        groups.append([stride * g for g in range(1, radix)])
        stride *= radix
    return groups


def add(terms):
    return functools.reduce(lambda a, b: a + b, terms)


def sum_terms(block, axis, groups):
    terms = [block]
    for masks in groups:
        total = add(terms)
        terms = [total] + [swap(total, axis, m) for m in masks]
    return terms


def call(kernel, in_specs, outs, scratch=(), limit=4, packed=()):
    return pl.pallas_call(
        kernel,
        in_specs=in_specs,
        out_specs=[VMEM] * len(outs),
        out_shape=[jax.ShapeDtypeStruct(s, bf16 if i in packed else f32) for i, s in enumerate(outs)],
        scratch_shapes=list(scratch),
        compiler_params=pltpu.CompilerParams(vmem_limit_bytes=limit << 20),
    )


def core():
    return lax.rem(lax.axis_index("sp"), 2)


def split3(x):
    h = x.astype(bf16)
    r = x - h.astype(f32)
    m = r.astype(bf16)
    return h, m, (r - m.astype(f32)).astype(bf16)


def dotg(a, b, ca, cb):
    return lax.dot_general(a, b, (((ca,), (cb,)), ((), ())), preferred_element_type=f32)


def residuals(zb, c, ly):
    h, m, l = split3(zb)
    y = dotg(jnp.concatenate([h, h, h, m, m, l], 0), ly, 0, 0)
    i = jnp.exp2(y)
    r = c - i
    rh = r.astype(bf16)
    return y, i, rh, (r - rh.astype(f32)).astype(bf16), h, m


def factor_terms(rh, rl, lg, k):
    a = dotg(lg, rh, 1, 1)
    return a[:k] + a[k:] + dotg(lg[k:], rl, 1, 1)


def loading_terms(h, m, rh, rl, k):
    a = dotg(jnp.concatenate([m, h], 0), rh, 1, 0)
    return a[:k] + a[k:] + dotg(h, rl, 1, 0)


def fill_loadings(lt, ly_ref, lg_ref):
    h, m, l = split3(lt * f32(LOG2E))
    ly_ref[...] = jnp.concatenate([h, m, l, h, m, h], 0)
    h, m, _ = split3(lt)
    lg_ref[...] = jnp.concatenate([m, h], 0)


def rows_to_8(x):
    return jnp.sum(x.reshape(x.shape[0] // 8, 8, x.shape[1]), 0)


DEPTH = 3


def first_kernel(
    k, half, sub, z_hbm, lt_hbm, cnt_ref, load_ref, oth_ref, lg_ref, held_ref, rh_ref, rl_ref,
    ly_ref, z_ref, lt_ref, buf_ref, sem, sems
):
    c = core()
    steps = half // sub
    slots = DEPTH + 1

    def place(i):
        return pl.multiple_of(lax.rem((1 - i // steps) + c, 2) * half + (i % steps) * sub, sub)

    def copy(i):
        return pltpu.make_async_copy(
            cnt_ref.at[0, pl.ds(place(i), sub)], buf_ref.at[pl.ds((i % slots) * sub, sub)], sem.at[i]
        )

    small = [
        pltpu.make_async_copy(lt_hbm, lt_ref, sems.at[0]),
        pltpu.make_async_copy(z_hbm, z_ref, sems.at[1]),
    ]
    for job in small:
        job.start()
    for i in range(min(DEPTH, 2 * steps)):
        copy(i).start()
    small[0].wait()
    fill_loadings(lt_ref[...], ly_ref, lg_ref)
    small[1].wait()
    load_ref[:, -2 * LANES : -LANES], load_ref[:, -LANES:] = pack_rims(vregs_of(z_ref[0]), k)
    ly, lg = ly_ref[...], lg_ref[...]
    loads = []
    for i in range(2 * steps):
        copy(i).wait()
        if i + DEPTH < 2 * steps:
            copy(i + DEPTH).start()
        cf = buf_ref[pl.ds((i % slots) * sub, sub), :].astype(f32)
        rows = pl.ds(i * sub, sub)
        held_ref[rows, :] = cf
        _, _, rh, rl, h, m = residuals(z_ref[0, :, pl.ds(place(i), sub)], cf, ly)
        loads.append(loading_terms(h, m, rh, rl, k))
        if i < steps:
            oth_ref[:, i * sub : (i + 1) * sub] = factor_terms(rh, rl, lg, k)
        else:
            rows = pl.ds((i - steps) * sub, sub)
            rh_ref[rows, :] = rh
            rl_ref[rows, :] = rl
    load_ref[:, : -2 * LANES] = add(loads)


def factor_kernel(k, half, sub, lg_ref, rh_ref, rl_ref, fac_ref):
    lg = lg_ref[...]
    for i in range(half // sub):
        rows = pl.ds(i * sub, sub)
        fac_ref[:, i * sub : (i + 1) * sub] = factor_terms(rh_ref[rows, :], rl_ref[rows, :], lg, k)


def move_loadings_kernel(n_terms, *refs):
    terms = refs[:n_terms]
    lt_ref, lm_ref, sl_ref, out_ref, newl_ref, halfl_ref, ly_ref, lg_ref = refs[n_terms:]
    step = sl_ref[0]
    halfl = lm_ref[...] + 0.5 * step * (add([t[:, : lt_ref.shape[1]] for t in terms]) - lt_ref[...])
    newl = lt_ref[...] + step * halfl
    halfl_ref[...] = halfl
    newl_ref[...] = newl
    out_ref[...] = newl
    fill_loadings(newl, ly_ref, lg_ref)


def second_kernel(k, half, sub, start, z_ref, ly_ref, lg_ref, cnt_ref, fac_ref, lik_ref, rh_ref, rl_ref):
    ly, lg = ly_ref[...], lg_ref[...]
    likes, sums = [], []
    for i in range(half // sub):
        rows = pl.ds(i * sub, sub)
        cf = cnt_ref[pl.ds(start + i * sub, sub), :]
        y, inten, rh, rl, _, _ = residuals(z_ref[:, rows], cf, ly)
        rh_ref[rows, :] = rh
        rl_ref[rows, :] = rl
        fac_ref[:, rows] = factor_terms(rh, rl, lg, k)
        likes.append(rows_to_8(cf * y))
        sums.append(rows_to_8(inten))
    lik_ref[...] = add(sums) - f32(LN2) * add(likes)


def loading_kernel(k, half, sub, zo_ref, rho_ref, rlo_ref, zw_ref, rhw_ref, rlw_ref, liko_ref, likw_ref, load_ref):
    loads = []
    for z_ref, rh_ref, rl_ref in ((zo_ref, rho_ref, rlo_ref), (zw_ref, rhw_ref, rlw_ref)):
        for i in range(half // sub):
            rows = pl.ds(i * sub, sub)
            h, m, _ = split3(z_ref[:, rows])
            loads.append(loading_terms(h, m, rh_ref[rows, :], rl_ref[rows, :], k))
    load_ref[:k, : -2 * LANES] = add(loads)
    load_ref[k:, : -2 * LANES] = liko_ref[...] + likw_ref[...]
    load_ref[k:, -2 * LANES :] = jnp.zeros((load_ref.shape[0] - k, 2 * LANES), f32)
    rims = pack_rims(in_order(zw_ref[...], zo_ref[...]), k)
    load_ref[:k, -2 * LANES : -LANES], load_ref[:k, -LANES:] = rims


def lane(shape):
    return lax.broadcasted_iota(jnp.int32, shape, len(shape) - 1)


def pack_rims(vregs, k):
    q = lax.rem(lane((k, LANES)), TY)
    first = jnp.zeros((k, LANES), f32)
    last = jnp.zeros((k, LANES), f32)
    for j, v in enumerate(vregs):
        first = jnp.where(q == j, pltpu.roll(v, j, 1) if j else v, first)
        last = jnp.where(q == j, pltpu.roll(v, (j - TY + 1) % LANES, 1), last)
    return first, last


def prior_of(vregs, lo, hi, left, right, upper, lower, k):
    q = lax.rem(lane((k, LANES)), TY)
    n = len(vregs)
    wide = lane((k, LANES))
    out = []
    zero = jnp.zeros((k, LANES), f32)
    for j in range(lo, hi):
        v = vregs[j]
        back = pltpu.roll(v, 1, 1)
        ahead = pltpu.roll(v, LANES - 1, 1)
        lrim = pltpu.roll(left, (LANES - j) % LANES, 1) if j else left
        rrim = pltpu.roll(right, (TY - 1 - j) % LANES, 1)
        beside = jnp.where(q == 0, lrim, back) + jnp.where(q == TY - 1, rrim, ahead)
        prev = vregs[j - 1] if j else upper
        nxt = vregs[j + 1] if j + 1 < n else lower
        shift_down = pltpu.roll(v, TY, 1)
        above = jnp.where(wide < TY, pltpu.roll(prev, TY, 1), shift_down)
        below = jnp.where(wide >= LANES - TY, pltpu.roll(nxt, LANES - TY, 1), pltpu.roll(v, LANES - TY, 1))
        out.append((kappa_sq + 4.0) * v - (above + below + beside))
    return out


def sides(ride, refs, k):
    me, n = lax.axis_index("site"), lax.axis_size("site")
    even = lax.rem(me, 2) == 0
    if ride:
        pair, one, three = refs
        near = jnp.where(even, pair[:k, -2 * LANES : -LANES], pair[:k, -LANES:])
        row = me // 2
        close = (lax.rem(row, 2) == 1) == even
        first = jnp.where(close, one[:k, -2 * LANES : -LANES], three[:k, -2 * LANES : -LANES])
        last = jnp.where(close, one[:k, -LANES:], three[:k, -LANES:])
        far = jnp.where(even, last, first)
    else:
        near, far = refs[0][...], refs[1][...]
    left = jnp.where(me == 0, 0.0, jnp.where(even, far, near))
    right = jnp.where(me == n - 1, 0.0, jnp.where(even, near, far))
    return left, right


def rims_of(vregs, k):
    first, last = pack_rims(vregs, k)
    even = lax.rem(lax.axis_index("site"), 2) == 0
    return jnp.where(even, last, first), jnp.where(even, first, last)


def vregs_of(array):
    return [array[:, j * LANES : (j + 1) * LANES] for j in range(array.shape[1] // LANES)]


def rims_kernel(k, z_ref, near_ref, far_ref):
    near_ref[...], far_ref[...] = rims_of(vregs_of(z_ref[0]), k)


def stage_kernel(own_ref, got_ref, out_ref):
    own, got = own_ref[...], got_ref[...]
    out_ref[:, : -2 * LANES] = own[:, : -2 * LANES] + got[:, : -2 * LANES]
    even = lax.rem(lax.axis_index("site"), 2) == 0
    out_ref[:, -2 * LANES : -LANES] = jnp.where(even, own[:, -2 * LANES : -LANES], got[:, -2 * LANES : -LANES])
    out_ref[:, -LANES:] = jnp.where(even, got[:, -LANES:], own[:, -LANES:])


def ahead_kernel(
    ride, k, half, z_ref, mom_ref, upper_ref, lower_ref, gain_ref, sf_ref, *refs
):
    *halo, a_ref, z_own_ref, s_ref = refs
    c = core()
    step = sf_ref[0]
    left, right = sides(ride, halo, k)
    out = prior_of(vregs_of(z_ref[0]), 0, 2 * half // LANES, left, right, upper_ref[...], lower_ref[...], k)
    n = half // LANES
    gain = gain_ref[...] * (0.5 * step)
    for j in range(n):
        at = pl.ds(j * LANES, LANES)
        own = jnp.where(c == 0, out[j], out[n + j])
        src = pl.ds(pl.multiple_of(c * half + j * LANES, LANES), LANES)
        a_ref[:, at] = mom_ref[0, :, src] - gain * own
        z_own_ref[:, at] = z_ref[0, :, src]
    s_ref[...] = jnp.full(s_ref.shape, step, f32)


def move_kernel(half, own_ref, other_ref, a_ref, z_ref, s_ref, half_ref, moved_ref):
    for j in range(half // LANES):
        at = pl.ds(j * LANES, LANES)
        h = a_ref[:, at] + (0.5 * s_ref[...]) * (own_ref[:, at] + other_ref[:, at])
        half_ref[:, at] = h
        moved_ref[:, at] = z_ref[:, at] + s_ref[...] * h


def in_order(own, oth):
    first = core() == 0
    own, oth = vregs_of(own), vregs_of(oth)
    return [jnp.where(first, a, b) for a, b in zip(own, oth)] + [jnp.where(first, b, a) for a, b in zip(own, oth)]


def join_kernel(k, own_ref, oth_ref, near_ref, far_ref):
    near_ref[...], far_ref[...] = rims_of(in_order(own_ref[...], oth_ref[...]), k)


def behind_kernel(ride, k, half, own_ref, oth_ref, h_ref, upper_ref, lower_ref, gain_ref, s_ref, *refs):
    *halo, a_ref, e_ref = refs
    c = core()
    left, right = sides(ride, halo, k)
    z = in_order(own_ref[...], oth_ref[...])
    out = prior_of(z, 0, 2 * half // LANES, left, right, upper_ref[...], lower_ref[...], k)
    n = half // LANES
    gain = gain_ref[...]
    energy = jnp.zeros((k, LANES), f32)
    for j in range(n):
        at = pl.ds(j * LANES, LANES)
        own = gain * jnp.where(c == 0, out[j], out[n + j])
        energy = energy + own_ref[:, at] * own
        a_ref[:, at] = h_ref[:, at] - (0.5 * s_ref[...]) * own
    e_ref[...] = energy


def end_kernel(k, half, own_ref, other_ref, a_ref, s_ref, pe_ref, end_ref, b_ref):
    energy = pe_ref[...]
    for j in range(half // LANES):
        at = pl.ds(j * LANES, LANES)
        e = a_ref[:, at] + (0.5 * s_ref[...]) * (own_ref[:, at] + other_ref[:, at])
        end_ref[:, at] = e
        energy = energy + e * e
    b_ref[...] = 0.5 * sum(energy[g * 8 : (g + 1) * 8] for g in range(k // 8))


def pair_kernel(half, own_ref, oth_ref, full_ref):
    c = core()
    own, oth = own_ref[...], oth_ref[...]
    full_ref[0, :, :half] = jnp.where(c == 0, own, oth)
    full_ref[0, :, half:] = jnp.where(c == 0, oth, own)


def loading_end_kernel(k, n_terms, *refs):
    terms = refs[:n_terms]
    newl_ref, halfl_ref, sl_ref, end_ref, s_ref = refs[n_terms:]
    newl = newl_ref[...]
    total = add([t[:, : newl.shape[1]] for t in terms])
    end = halfl_ref[...] + (0.5 * sl_ref[0]) * (total[:k] - newl)
    end_ref[...] = end
    squares = 0.5 * (end * end + newl * newl)
    energy = total[k:] + sum(squares[g * 8 : (g + 1) * 8] for g in range(k // 8))
    s_ref[...] = sum(energy[:, j * LANES : (j + 1) * LANES] for j in range(energy.shape[1] // LANES))


def local(
    counts, factors, loadings, factor_momenta, loading_momenta, precision, factor_step, loading_step
):
    k, cells = factors.shape[1:]
    species = loadings.shape[0]
    half = cells // 2
    sub = 640 if half % 640 == 0 else half
    n_site, n_sp = lax.axis_size("site"), lax.axis_size("sp")
    site, chips = mask_groups(n_site), mask_groups(n_sp)[1:]
    lt, lm = loadings.T, loading_momenta.T
    gain = jnp.broadcast_to(precision[:, None], (k, LANES))
    zero_rim = jnp.zeros((k, LANES), f32)

    ride = site == [[1], [2, 4, 6]]

    def exchange(load):
        if not ride:
            return sum_terms(load, "site", site), ()
        got = swap(load, "site", 1)
        (total,) = call(stage_kernel, [VMEM] * 2, [load.shape])(load, got)
        terms = [total] + [swap(total, "site", m) for m in site[1]]
        return terms, (got, terms[1], terms[3])

    def upright(low, high):
        if n_site <= TGY:
            return zero_rim, zero_rim
        lead = jnp.zeros((k, LANES - TY), f32)
        upper = jnp.concatenate([lead, from_behind(high, "site", TGY)], 1)
        return upper, jnp.concatenate([from_behind(low, "site", -TGY), lead], 1)

    def sideways(kernel, halo, *arrays):
        if ride:
            return halo
        near, far = call(functools.partial(kernel, k), [VMEM] * len(arrays), [(k, LANES)] * 2)(*arrays)
        return paired(near, "site", 0), paired(far, "site", 1)

    def share(own, oth):
        terms = sum_terms(own + swap(oth, "sp", 1), "sp", chips)
        return terms[0], add(terms[1:])

    rates, grads = (6 * k, species), (2 * k, species)
    load, oth, lg, held, rh, rl = call(
        functools.partial(first_kernel, k, half, sub),
        [HBM, HBM, HBM],
        [(k, species + 2 * LANES), (k, half), grads, (cells, species), (half, species), (half, species)],
        [
            pltpu.VMEM(rates, bf16),
            pltpu.VMEM((1, k, cells), f32),
            pltpu.VMEM((k, species), f32),
            pltpu.VMEM(((DEPTH + 1) * sub, species), jnp.int32),
            pltpu.SemaphoreType.DMA((cells // sub,)),
            pltpu.SemaphoreType.DMA((2,)),
        ],
        12,
        (2, 4, 5),
    )(*[pltpu.with_memory_space_constraint(x, pltpu.HBM) for x in (factors, lt, counts)])
    load_terms, halo = exchange(load)
    (own,) = call(functools.partial(factor_kernel, k, half, sub), [VMEM] * 3, [(k, half)])(lg, rh, rl)
    own, other = share(own, oth)

    halo = sideways(rims_kernel, halo, factors)
    edges = upright(factors[0, :, :TY], factors[0, :, cells - TY :])
    a1, z_own, svec = call(
        functools.partial(ahead_kernel, ride, k, half),
        [VMEM] * 5 + [SMEM] + [VMEM] * len(halo),
        [(k, half), (k, half), (k, LANES)],
    )(factors, factor_momenta, *edges, gain, factor_step, *halo)
    half_own, moved_own = call(
        functools.partial(move_kernel, half), [VMEM] * 5, [(k, half)] * 2
    )(own, other, a1, z_own, svec)
    moved_oth = swap(moved_own, "sp", 1)
    (new_factors,) = call(functools.partial(pair_kernel, half), [VMEM] * 2, [(1, k, cells)])(moved_own, moved_oth)

    new_loadings, newl, halfl, ly, lg = call(
        functools.partial(move_loadings_kernel, len(load_terms)),
        [VMEM] * (len(load_terms) + 2) + [SMEM],
        [(k, species)] * 3 + [rates, grads],
        packed=(3, 4),
    )(*load_terms, lt, lm, loading_step)
    (own, lik_own, *parts_own), (oth, lik_oth, *parts_oth) = [
        call(
            functools.partial(second_kernel, k, half, sub, start),
            [VMEM] * 4,
            [(k, half), (8, species), (half, species), (half, species)],
            limit=8,
            packed=(2, 3),
        )(z, ly, lg, held)
        for start, z in ((half, moved_own), (0, moved_oth))
    ]
    (load,) = call(functools.partial(loading_kernel, k, half, sub), [VMEM] * 8, [(k + 8, species + 2 * LANES)])(
        moved_oth, *parts_oth, moved_own, *parts_own, lik_oth, lik_own
    )
    load_terms, halo = exchange(load)
    own, other = share(own, oth)

    halo = sideways(join_kernel, halo, moved_own, moved_oth)
    edges = upright(new_factors[0, :, :TY], new_factors[0, :, cells - TY :])
    a2, prior_energy = call(
        functools.partial(behind_kernel, ride, k, half), [VMEM] * (7 + len(halo)), [(k, half), (k, LANES)]
    )(moved_own, moved_oth, half_own, *edges, gain, svec, *halo)
    end_own, b_part = call(
        functools.partial(end_kernel, k, half), [VMEM] * 5, [(k, half), (8, LANES)]
    )(own, other, a2, svec, prior_energy)
    end_oth = swap(end_own, "sp", 1)
    (new_momenta,) = call(functools.partial(pair_kernel, half), [VMEM] * 2, [(1, k, cells)])(end_own, end_oth)

    endl, s_part = call(
        functools.partial(loading_end_kernel, k, len(load_terms)),
        [VMEM] * (len(load_terms) + 2) + [SMEM],
        [(k, species), (8, LANES)],
    )(*load_terms, newl, halfl, loading_step)
    total = add(sum_terms(s_part, "sp", chips) + sum_terms(b_part, "site", site))
    total = total + swap(total, "sp", 1)
    entries = n_site * cells * n_sp * species
    energy = jnp.reshape(jnp.sum(total) / entries, (1,))
    return new_factors, new_momenta, new_loadings.T, endl.T, energy


def solution(mesh):
    placed = (
        P("site", None, "sp"),
        P("site", None, None),
        P("sp", None),
        P("site", None, None),
        P("sp", None),
        P(),
        P(),
        P(),
    )

    return jax.shard_map(
        local,
        mesh=mesh,
        in_specs=placed,
        out_specs=(P("site", None, None), P("site", None, None), P("sp", None), P("sp", None), P()),
        check_vma=False,
    )
```

```python
import functools

import jax
import jax.numpy as jnp
from jax import lax
from jax.experimental import pallas as pl
from jax.experimental.pallas import tpu as pltpu
from jax.sharding import PartitionSpec as P


TY = 64
TGY = 8
LANES = 128

kappa_sq = 0.25
LOG2E = 1.4426950408889634
LN2 = 0.6931471805599453
f32, bf16 = jnp.float32, jnp.bfloat16


VMEM = pl.BlockSpec(memory_space=pltpu.VMEM)
SMEM = pl.BlockSpec(memory_space=pltpu.SMEM)
HBM = pl.BlockSpec(memory_space=pltpu.HBM)


def swap(block, axis, mask):
    return lax.ppermute(block, axis, [(i, i ^ mask) for i in range(lax.axis_size(axis))])


def from_behind(block, axis, distance):
    devices = range(lax.axis_size(axis))
    route = [(i - distance, i) for i in devices if i - distance in devices]
    return lax.ppermute(block, axis, route)


def paired(block, axis, first):
    n = lax.axis_size(axis)
    route = [(i, i + 1 if (i - first) % 2 == 0 else i - 1) for i in range(n)]
    return lax.ppermute(block, axis, [(i, j) for i, j in route if 0 <= j < n])


def mask_groups(n):
    groups, stride = [], 1
    while stride < n:
        radix = 2 if stride == 1 or n // stride == 2 else 4
        groups.append([stride * g for g in range(1, radix)])
        stride *= radix
    return groups


def rides(n_site):
    return n_site == 8 == TGY


def add(terms):
    return functools.reduce(lambda a, b: a + b, terms)


def sum_terms(block, axis, groups):
    terms = [block]
    for masks in groups:
        total = add(terms)
        terms = [total] + [swap(total, axis, m) for m in masks]
    return terms


def call(kernel, in_specs, outs, scratch=(), limit=4, packed=()):
    return pl.pallas_call(
        kernel,
        in_specs=in_specs,
        out_specs=[VMEM] * len(outs),
        out_shape=[jax.ShapeDtypeStruct(s, bf16 if i in packed else f32) for i, s in enumerate(outs)],
        scratch_shapes=list(scratch),
        compiler_params=pltpu.CompilerParams(vmem_limit_bytes=limit << 20),
    )


def core():
    return lax.rem(lax.axis_index("sp"), 2)


def split3(x):
    h = x.astype(bf16)
    r = x - h.astype(f32)
    m = r.astype(bf16)
    return h, m, (r - m.astype(f32)).astype(bf16)


def dotg(a, b, ca, cb):
    return lax.dot_general(a, b, (((ca,), (cb,)), ((), ())), preferred_element_type=f32)


def residuals(zb, c, ly):
    h, m, l = split3(zb)
    y = dotg(jnp.concatenate([h, h, h, m, m, l], 0), ly, 0, 0)
    i = jnp.exp2(y)
    r = c - i
    rh = r.astype(bf16)
    return y, i, rh, (r - rh.astype(f32)).astype(bf16), h, m


def factor_terms(rh, rl, lg, k):
    a = dotg(lg, rh, 1, 1)
    return a[:k] + a[k:] + dotg(lg[k:], rl, 1, 1)


def loading_terms(h, m, rh, rl, k):
    a = dotg(jnp.concatenate([m, h], 0), rh, 1, 0)
    return a[:k] + a[k:] + dotg(h, rl, 1, 0)


def fill_loadings(lt, ly_ref, lg_ref):
    h, m, l = split3(lt * f32(LOG2E))
    ly_ref[...] = jnp.concatenate([h, m, l, h, m, h], 0)
    h, m, _ = split3(lt)
    lg_ref[...] = jnp.concatenate([m, h], 0)


def rows_to_8(x):
    return jnp.sum(x.reshape(x.shape[0] // 8, 8, x.shape[1]), 0)


DEPTH = 3


def first_kernel(
    k, half, sub, z_hbm, lt_hbm, cnt_ref, load_ref, lg_ref, held_ref, rho_ref, rlo_ref, rhw_ref, rlw_ref,
    ly_ref, z_ref, lt_ref, buf_ref, sem, sems
):
    c = core()
    steps = half // sub
    slots = DEPTH + 1

    def place(i):
        return pl.multiple_of(lax.rem((1 - i // steps) + c, 2) * half + (i % steps) * sub, sub)

    def copy(i):
        return pltpu.make_async_copy(
            cnt_ref.at[0, pl.ds(place(i), sub)], buf_ref.at[pl.ds((i % slots) * sub, sub)], sem.at[i]
        )

    small = [
        pltpu.make_async_copy(lt_hbm, lt_ref, sems.at[0]),
        pltpu.make_async_copy(z_hbm, z_ref, sems.at[1]),
    ]
    for job in small:
        job.start()
    for i in range(min(DEPTH, 2 * steps)):
        copy(i).start()
    small[0].wait()
    fill_loadings(lt_ref[...], ly_ref, lg_ref)
    small[1].wait()
    load_ref[:, -2 * LANES : -LANES], load_ref[:, -LANES:] = pack_rims(vregs_of(z_ref[0]), k)
    ly = ly_ref[...]
    loads = []
    for i in range(2 * steps):
        copy(i).wait()
        if i + DEPTH < 2 * steps:
            copy(i + DEPTH).start()
        cf = buf_ref[pl.ds((i % slots) * sub, sub), :].astype(f32)
        rows = pl.ds(i * sub, sub)
        held_ref[rows, :] = cf
        _, _, rh, rl, h, m = residuals(z_ref[0, :, pl.ds(place(i), sub)], cf, ly)
        loads.append(loading_terms(h, m, rh, rl, k))
        rh_ref, rl_ref = (rho_ref, rlo_ref) if i < steps else (rhw_ref, rlw_ref)
        rows = pl.ds((i % steps) * sub, sub)
        rh_ref[rows, :] = rh
        rl_ref[rows, :] = rl
    load_ref[:, : -2 * LANES] = add(loads)


def factor_kernel(k, half, sub, lg_ref, rh_ref, rl_ref, fac_ref):
    lg = lg_ref[...]
    for i in range(half // sub):
        rows = pl.ds(i * sub, sub)
        fac_ref[:, i * sub : (i + 1) * sub] = factor_terms(rh_ref[rows, :], rl_ref[rows, :], lg, k)


def move_loadings_kernel(n_terms, *refs):
    terms = refs[:n_terms]
    lt_ref, lm_ref, sl_ref, newl_ref, halfl_ref, ly_ref, lg_ref = refs[n_terms:]
    step = sl_ref[0]
    halfl = lm_ref[...] + 0.5 * step * (add([t[:, : lt_ref.shape[1]] for t in terms]) - lt_ref[...])
    newl = lt_ref[...] + step * halfl
    halfl_ref[...] = halfl
    newl_ref[...] = newl
    fill_loadings(newl, ly_ref, lg_ref)


def second_kernel(k, half, sub, start, z_ref, ly_ref, lg_ref, cnt_ref, fac_ref, lik_ref, rh_ref, rl_ref):
    ly, lg = ly_ref[...], lg_ref[...]
    likes, sums = [], []
    for i in range(half // sub):
        rows = pl.ds(i * sub, sub)
        cf = cnt_ref[pl.ds(start + i * sub, sub), :]
        y, inten, rh, rl, _, _ = residuals(z_ref[:, rows], cf, ly)
        rh_ref[rows, :] = rh
        rl_ref[rows, :] = rl
        fac_ref[:, rows] = factor_terms(rh, rl, lg, k)
        likes.append(rows_to_8(cf * y))
        sums.append(rows_to_8(inten))
    lik_ref[...] = add(sums) - f32(LN2) * add(likes)


def loading_kernel(k, half, sub, zo_ref, rho_ref, rlo_ref, zw_ref, rhw_ref, rlw_ref, liko_ref, likw_ref, load_ref):
    loads = []
    for z_ref, rh_ref, rl_ref in ((zo_ref, rho_ref, rlo_ref), (zw_ref, rhw_ref, rlw_ref)):
        for i in range(half // sub):
            rows = pl.ds(i * sub, sub)
            h, m, _ = split3(z_ref[:, rows])
            loads.append(loading_terms(h, m, rh_ref[rows, :], rl_ref[rows, :], k))
    load_ref[:k, : -2 * LANES] = add(loads)
    load_ref[k:, : -2 * LANES] = liko_ref[...] + likw_ref[...]
    load_ref[k:, -2 * LANES :] = jnp.zeros((load_ref.shape[0] - k, 2 * LANES), f32)
    rims = pack_rims(in_order(zw_ref[...], zo_ref[...]), k)
    load_ref[:k, -2 * LANES : -LANES], load_ref[:k, -LANES:] = rims


def lane(shape):
    return lax.broadcasted_iota(jnp.int32, shape, len(shape) - 1)


def pack_rims(vregs, k):
    q = lax.rem(lane((k, LANES)), TY)
    first = jnp.zeros((k, LANES), f32)
    last = jnp.zeros((k, LANES), f32)
    for j, v in enumerate(vregs):
        first = jnp.where(q == j, pltpu.roll(v, j, 1) if j else v, first)
        last = jnp.where(q == j, pltpu.roll(v, (j - TY + 1) % LANES, 1), last)
    return first, last


def prior_of(vregs, upper, lower, k):
    q = lax.rem(lane((k, LANES)), TY)
    wide = lane((k, LANES))
    n = len(vregs)
    out = []
    for j, v in enumerate(vregs):
        back = jnp.where(q == 0, 0.0, pltpu.roll(v, 1, 1))
        ahead = jnp.where(q == TY - 1, 0.0, pltpu.roll(v, LANES - 1, 1))
        prev = vregs[j - 1] if j else upper
        nxt = vregs[j + 1] if j + 1 < n else lower
        above = jnp.where(wide < TY, pltpu.roll(prev, TY, 1), pltpu.roll(v, TY, 1))
        below = jnp.where(wide >= LANES - TY, pltpu.roll(nxt, LANES - TY, 1), pltpu.roll(v, LANES - TY, 1))
        out.append((kappa_sq + 4.0) * v - (above + below + (back + ahead)))
    return out


def beside_of(left, right, half, k):
    q = lax.rem(lane((k, LANES)), TY)
    n = half // LANES
    low = core() == 0
    left = jnp.where(low, left, pltpu.roll(left, (LANES - n) % LANES, 1))
    right = jnp.where(low, right, pltpu.roll(right, (LANES - n) % LANES, 1))
    out = []
    for j in range(n):
        lrim = pltpu.roll(left, LANES - j, 1) if j else left
        rrim = pltpu.roll(right, (TY - 1 - j) % LANES, 1)
        out.append(jnp.where(q == 0, lrim, 0.0) + jnp.where(q == TY - 1, rrim, 0.0))
    return out


def sides(ride, refs, k):
    me, n = lax.axis_index("site"), lax.axis_size("site")
    even = lax.rem(me, 2) == 0
    if ride:
        pair, one, three = refs
        near = jnp.where(even, pair[:k, -2 * LANES : -LANES], pair[:k, -LANES:])
        row = me // 2
        close = (lax.rem(row, 2) == 1) == even
        far = jnp.where(close, one[:k, -LANES:], three[:k, -LANES:])
    else:
        near, far = refs[0][...], refs[1][...]
    left = jnp.where(me == 0, 0.0, jnp.where(even, far, near))
    right = jnp.where(me == n - 1, 0.0, jnp.where(even, near, far))
    return left, right


def rims_of(vregs, k):
    first, last = pack_rims(vregs, k)
    even = lax.rem(lax.axis_index("site"), 2) == 0
    return jnp.where(even, last, first), jnp.where(even, first, last)


def vregs_of(array):
    return [array[:, j * LANES : (j + 1) * LANES] for j in range(array.shape[1] // LANES)]


def rims_kernel(k, z_ref, near_ref, far_ref):
    near_ref[...], far_ref[...] = rims_of(vregs_of(z_ref[0]), k)


def stage_kernel(near, own_ref, got_ref, *refs):
    *sums, out_ref = refs
    a, b = sums if sums else (own_ref, got_ref)
    width = own_ref.shape[1] - 2 * LANES
    out_ref[:, :width] = a[:, :width] + b[:, :width]
    site = lax.axis_index("site")
    even = lax.rem(site, 2) == 0
    first = jnp.where(even, own_ref[:, -2 * LANES : -LANES], got_ref[:, -2 * LANES : -LANES])
    last = jnp.where(even, got_ref[:, -LANES:], own_ref[:, -LANES:])
    out_ref[:, width:] = jnp.where((lax.rem(site // 2, 2) == 0) == near, last, first)


def ahead_kernel(k, half, z_ref, mom_ref, upper_ref, lower_ref, gain_ref, sf_ref, a_ref, z_own_ref, s_ref):
    c = core()
    step = sf_ref[0]
    out = prior_of(vregs_of(z_ref[0]), upper_ref[...], lower_ref[...], k)
    n = half // LANES
    gain = gain_ref[...] * (0.5 * step)
    for j in range(n):
        at = pl.ds(j * LANES, LANES)
        own = jnp.where(c == 0, out[j], out[n + j])
        src = pl.ds(pl.multiple_of(c * half + j * LANES, LANES), LANES)
        a_ref[:, at] = mom_ref[0, :, src] - gain * own
        z_own_ref[:, at] = z_ref[0, :, src]
    s_ref[...] = jnp.full(s_ref.shape, step, f32)


def move_kernel(ride, k, half, own_ref, other_ref, a_ref, z_ref, s_ref, gain_ref, *refs):
    *halo, half_ref, moved_ref = refs
    beside = beside_of(*sides(ride, halo, k), half, k)
    step, gain = s_ref[...], gain_ref[...]
    for j in range(half // LANES):
        at = pl.ds(j * LANES, LANES)
        h = a_ref[:, at] + (0.5 * step) * ((own_ref[:, at] + other_ref[:, at]) + gain * beside[j])
        half_ref[:, at] = h
        moved_ref[:, at] = z_ref[:, at] + step * h


def in_order(own, oth):
    first = core() == 0
    own, oth = vregs_of(own), vregs_of(oth)
    return [jnp.where(first, a, b) for a, b in zip(own, oth)] + [jnp.where(first, b, a) for a, b in zip(own, oth)]


def join_kernel(k, own_ref, oth_ref, near_ref, far_ref):
    near_ref[...], far_ref[...] = rims_of(in_order(own_ref[...], oth_ref[...]), k)


def behind_kernel(k, half, own_ref, oth_ref, h_ref, upper_ref, lower_ref, gain_ref, s_ref, a_ref, e_ref):
    c = core()
    out = prior_of(in_order(own_ref[...], oth_ref[...]), upper_ref[...], lower_ref[...], k)
    n = half // LANES
    gain = gain_ref[...]
    energy = jnp.zeros((k, LANES), f32)
    for j in range(n):
        at = pl.ds(j * LANES, LANES)
        own = gain * jnp.where(c == 0, out[j], out[n + j])
        energy = energy + own_ref[:, at] * own
        a_ref[:, at] = h_ref[:, at] - (0.5 * s_ref[...]) * own
    e_ref[...] = energy


def end_kernel(ride, k, half, own_ref, other_ref, a_ref, z_ref, s_ref, gain_ref, pe_ref, *refs):
    *halo, end_ref, b_ref = refs
    beside = beside_of(*sides(ride, halo, k), half, k)
    step, gain = s_ref[...], gain_ref[...]
    energy = pe_ref[...]
    for j in range(half // LANES):
        at = pl.ds(j * LANES, LANES)
        rim = gain * beside[j]
        e = a_ref[:, at] + (0.5 * step) * ((own_ref[:, at] + other_ref[:, at]) + rim)
        end_ref[:, at] = e
        energy = energy + (e * e - z_ref[:, at] * rim)
    b_ref[...] = 0.5 * sum(energy[g * 8 : (g + 1) * 8] for g in range(k // 8))


def pair_kernel(half, own_ref, oth_ref, loadings_ref, full_ref, out_ref):
    c = core()
    own, oth = own_ref[...], oth_ref[...]
    full_ref[0, :, :half] = jnp.where(c == 0, own, oth)
    full_ref[0, :, half:] = jnp.where(c == 0, oth, own)
    out_ref[...] = loadings_ref[...]


def energy_kernel(entries, own_ref, got_ref, out_ref):
    out_ref[0] = jnp.sum(own_ref[...] + got_ref[...]) / entries


def loading_end_kernel(k, n_terms, *refs):
    terms = refs[:n_terms]
    newl_ref, halfl_ref, sl_ref, end_ref, s_ref = refs[n_terms:]
    newl = newl_ref[...]
    total = add([t[:, : newl.shape[1]] for t in terms])
    end = halfl_ref[...] + (0.5 * sl_ref[0]) * (total[:k] - newl)
    end_ref[...] = end
    squares = 0.5 * (end * end + newl * newl)
    energy = total[k:] + sum(squares[g * 8 : (g + 1) * 8] for g in range(k // 8))
    s_ref[...] = sum(energy[:, j * LANES : (j + 1) * LANES] for j in range(energy.shape[1] // LANES))


def local(
    counts, factors, loadings, factor_momenta, loading_momenta, precision, factor_step, loading_step
):
    k, cells = factors.shape[1:]
    species = loadings.shape[0]
    half = cells // 2
    sub = 640 if half % 640 == 0 else half
    n_site, n_sp = lax.axis_size("site"), lax.axis_size("sp")
    site, chips = mask_groups(n_site), mask_groups(n_sp)[1:]
    lt, lm = loadings.T, loading_momenta.T
    gain = jnp.broadcast_to(precision[:, None], (k, LANES))
    zero_rim = jnp.zeros((k, LANES), f32)

    ride = rides(n_site)

    def exchange(load):
        if not ride:
            return sum_terms(load, "site", site), ()
        shape = (load.shape[0], species + LANES)

        def stage(near, *args):
            kernel = functools.partial(stage_kernel, near)
            return call(kernel, [VMEM] * len(args), [shape])(*args)[0]

        got = swap(load, "site", 1)
        two = stage(True, load, got)
        got_two = swap(two, "site", 2)
        four = stage(False, load, got, two, got_two)
        got_four = swap(four, "site", 6)
        return [four, got_four], (got, got_two, got_four)

    def upright(low, high):
        if n_site <= TGY:
            return zero_rim, zero_rim
        lead = jnp.zeros((k, LANES - TY), f32)
        upper = jnp.concatenate([lead, from_behind(high, "site", TGY)], 1)
        return upper, jnp.concatenate([from_behind(low, "site", -TGY), lead], 1)

    def sideways(kernel, halo, *arrays):
        if ride:
            return halo
        near, far = call(functools.partial(kernel, k), [VMEM] * len(arrays), [(k, LANES)] * 2)(*arrays)
        return paired(near, "site", 0), paired(far, "site", 1)

    def share(own, oth):
        terms = sum_terms(own + swap(oth, "sp", 1), "sp", chips)
        return terms[0], add(terms[1:])

    rates, grads = (6 * k, species), (2 * k, species)
    load, lg, held, rho, rlo, rhw, rlw = call(
        functools.partial(first_kernel, k, half, sub),
        [HBM, HBM, HBM],
        [(k, species + 2 * LANES), grads, (cells, species)] + [(half, species)] * 4,
        [
            pltpu.VMEM(rates, bf16),
            pltpu.VMEM((1, k, cells), f32),
            pltpu.VMEM((k, species), f32),
            pltpu.VMEM(((DEPTH + 1) * sub, species), jnp.int32),
            pltpu.SemaphoreType.DMA((cells // sub,)),
            pltpu.SemaphoreType.DMA((2,)),
        ],
        12,
        (1, 3, 4, 5, 6),
    )(*[pltpu.with_memory_space_constraint(x, pltpu.HBM) for x in (factors, lt, counts)])
    load_terms, halo = exchange(load)
    (oth,), (own,) = [
        call(functools.partial(factor_kernel, k, half, sub), [VMEM] * 3, [(k, half)])(lg, rh, rl)
        for rh, rl in ((rho, rlo), (rhw, rlw))
    ]
    own, other = share(own, oth)

    halo = sideways(rims_kernel, halo, factors)
    edges = upright(factors[0, :, :TY], factors[0, :, cells - TY :])
    a1, z_own, svec = call(
        functools.partial(ahead_kernel, k, half), [VMEM] * 5 + [SMEM], [(k, half), (k, half), (k, LANES)]
    )(factors, factor_momenta, *edges, gain, factor_step)
    half_own, moved_own = call(
        functools.partial(move_kernel, ride, k, half), [VMEM] * (6 + len(halo)), [(k, half)] * 2
    )(own, other, a1, z_own, svec, gain, *halo)
    moved_oth = swap(moved_own, "sp", 1)

    newl, halfl, ly, lg = call(
        functools.partial(move_loadings_kernel, len(load_terms)),
        [VMEM] * (len(load_terms) + 2) + [SMEM],
        [(k, species)] * 2 + [rates, grads],
        packed=(2, 3),
    )(*load_terms, lt, lm, loading_step)
    new_factors, new_loadings = call(
        functools.partial(pair_kernel, half), [VMEM] * 3, [(1, k, cells), (k, species)]
    )(moved_own, moved_oth, newl)
    (own, lik_own, *parts_own), (oth, lik_oth, *parts_oth) = [
        call(
            functools.partial(second_kernel, k, half, sub, start),
            [VMEM] * 4,
            [(k, half), (8, species), (half, species), (half, species)],
            limit=8,
            packed=(2, 3),
        )(z, ly, lg, held)
        for start, z in ((half, moved_own), (0, moved_oth))
    ]
    (load,) = call(functools.partial(loading_kernel, k, half, sub), [VMEM] * 8, [(k + 8, species + 2 * LANES)])(
        moved_oth, *parts_oth, moved_own, *parts_own, lik_oth, lik_own
    )
    load_terms, halo = exchange(load)
    own, other = share(own, oth)

    halo = sideways(join_kernel, halo, moved_own, moved_oth)
    edges = upright(new_factors[0, :, :TY], new_factors[0, :, cells - TY :])
    a2, prior_energy = call(
        functools.partial(behind_kernel, k, half), [VMEM] * 7, [(k, half), (k, LANES)]
    )(moved_own, moved_oth, half_own, *edges, gain, svec)
    end_own, b_part = call(
        functools.partial(end_kernel, ride, k, half), [VMEM] * (7 + len(halo)), [(k, half), (8, LANES)]
    )(own, other, a2, moved_own, svec, gain, prior_energy, *halo)
    end_oth = swap(end_own, "sp", 1)
    endl, s_part = call(
        functools.partial(loading_end_kernel, k, len(load_terms)),
        [VMEM] * (len(load_terms) + 2) + [SMEM],
        [(k, species), (8, LANES)],
    )(*load_terms, newl, halfl, loading_step)
    new_momenta, end_loadings = call(
        functools.partial(pair_kernel, half), [VMEM] * 3, [(1, k, cells), (k, species)]
    )(end_own, end_oth, endl)
    total = add(sum_terms(s_part, "sp", chips) + sum_terms(b_part, "site", site))
    energy = pl.pallas_call(
        functools.partial(energy_kernel, n_site * cells * n_sp * species),
        in_specs=[VMEM] * 2,
        out_specs=SMEM,
        out_shape=jax.ShapeDtypeStruct((1,), f32),
        name="energy",
        compiler_params=pltpu.CompilerParams(vmem_limit_bytes=1 << 20),
    )(total, swap(total, "sp", 1))
    return new_factors, new_momenta, new_loadings.T, end_loadings.T, energy


def solution(mesh):
    placed = (
        P("site", None, "sp"),
        P("site", None, None),
        P("sp", None),
        P("site", None, None),
        P("sp", None),
        P(),
        P(),
        P(),
    )

    return jax.shard_map(
        local,
        mesh=mesh,
        in_specs=placed,
        out_specs=(P("site", None, None), P("site", None, None), P("sp", None), P("sp", None), P()),
        check_vma=False,
    )
```

```python
import functools

import jax
import jax.numpy as jnp
from jax import lax
from jax.experimental import pallas as pl
from jax.experimental.pallas import tpu as pltpu
from jax.sharding import PartitionSpec as P


TY = 64
TGY = 8
LANES = 128

kappa_sq = 0.25
LOG2E = 1.4426950408889634
LN2 = 0.6931471805599453
f32, bf16 = jnp.float32, jnp.bfloat16


VMEM = pl.BlockSpec(memory_space=pltpu.VMEM)
SMEM = pl.BlockSpec(memory_space=pltpu.SMEM)
HBM = pl.BlockSpec(memory_space=pltpu.HBM)


def swap(block, axis, mask):
    return lax.ppermute(block, axis, [(i, i ^ mask) for i in range(lax.axis_size(axis))])


def from_behind(block, axis, distance):
    devices = range(lax.axis_size(axis))
    route = [(i - distance, i) for i in devices if i - distance in devices]
    return lax.ppermute(block, axis, route)


def paired(block, axis, first):
    n = lax.axis_size(axis)
    route = [(i, i + 1 if (i - first) % 2 == 0 else i - 1) for i in range(n)]
    return lax.ppermute(block, axis, [(i, j) for i, j in route if 0 <= j < n])


def mask_groups(n):
    groups, stride = [], 1
    while stride < n:
        radix = 2 if stride == 1 or n // stride == 2 else 4
        groups.append([stride * g for g in range(1, radix)])
        stride *= radix
    return groups


def rides(n_site):
    return n_site == 8 == TGY


def add(terms):
    return functools.reduce(lambda a, b: a + b, terms)


def sum_terms(block, axis, groups):
    terms = [block]
    for masks in groups:
        total = add(terms)
        terms = [total] + [swap(total, axis, m) for m in masks]
    return terms


def call(kernel, in_specs, outs, scratch=(), limit=4, packed=()):
    return pl.pallas_call(
        kernel,
        in_specs=in_specs,
        out_specs=[SMEM if s == (1,) else VMEM for s in outs],
        out_shape=[jax.ShapeDtypeStruct(s, bf16 if i in packed else f32) for i, s in enumerate(outs)],
        scratch_shapes=list(scratch),
        compiler_params=pltpu.CompilerParams(vmem_limit_bytes=limit << 20),
    )


def core():
    return lax.rem(lax.axis_index("sp"), 2)


def split3(x):
    h = x.astype(bf16)
    r = x - h.astype(f32)
    m = r.astype(bf16)
    return h, m, (r - m.astype(f32)).astype(bf16)


def dotg(a, b, ca, cb):
    return lax.dot_general(a, b, (((ca,), (cb,)), ((), ())), preferred_element_type=f32)


def residuals(zb, c, ly):
    h, m, l = split3(zb)
    y = dotg(jnp.concatenate([h, h, h, m, m, l], 0), ly, 0, 0)
    i = jnp.exp2(y)
    r = c - i
    rh = r.astype(bf16)
    return y, i, rh, (r - rh.astype(f32)).astype(bf16), h, m


def factor_terms(rh, rl, lg, k):
    a = dotg(lg, rh, 1, 1)
    return a[:k] + a[k:] + dotg(lg[k:], rl, 1, 1)


def loading_terms(h, m, rh, rl, k):
    a = dotg(jnp.concatenate([m, h], 0), rh, 1, 0)
    return a[:k] + a[k:] + dotg(h, rl, 1, 0)


def fill_loadings(lt, ly_ref, lg_ref):
    h, m, l = split3(lt * f32(LOG2E))
    ly_ref[...] = jnp.concatenate([h, m, l, h, m, h], 0)
    h, m, _ = split3(lt)
    lg_ref[...] = jnp.concatenate([m, h], 0)


def fold_lanes(x):
    return add([x[:, j * LANES : (j + 1) * LANES] for j in range(x.shape[1] // LANES)])


def rows_to_8(x):
    return jnp.sum(x.reshape(x.shape[0] // 8, 8, x.shape[1]), 0)


DEPTH = 3


def first_kernel(
    k, half, sub, z_hbm, lt_hbm, cnt_ref, load_ref, lg_ref, held_ref, rho_ref, rlo_ref, rhw_ref, rlw_ref,
    ly_ref, z_ref, lt_ref, buf_ref, sem, sems
):
    c = core()
    pieces = [(rho, at) for rho in (1, 0) for at in range(0, half, sub)]

    def place(i):
        rho, at = pieces[i]
        return pl.multiple_of(lax.rem(rho + c, 2) * half + at, LANES)

    def kept(i):
        return pl.ds(i * sub, sub)

    def copy(i):
        return pltpu.make_async_copy(cnt_ref.at[0, pl.ds(place(i), sub)], buf_ref.at[kept(i)], sem.at[i])

    small = [
        pltpu.make_async_copy(lt_hbm, lt_ref, sems.at[0]),
        pltpu.make_async_copy(z_hbm, z_ref, sems.at[1]),
    ]
    for job in small:
        job.start()
    for i in range(min(DEPTH, len(pieces))):
        copy(i).start()
    small[0].wait()
    fill_loadings(lt_ref[...], ly_ref, lg_ref)
    small[1].wait()
    load_ref[:, -2 * LANES : -LANES], load_ref[:, -LANES:] = pack_rims(vregs_of(z_ref[0]), k)
    ly = ly_ref[...]
    loads = []
    for i, (rho, at) in enumerate(pieces):
        copy(i).wait()
        if i + DEPTH < len(pieces):
            copy(i + DEPTH).start()
        cf = buf_ref[kept(i), :].astype(f32)
        held_ref[kept(i), :] = cf
        _, _, rh, rl, h, m = residuals(z_ref[0, :, pl.ds(place(i), sub)], cf, ly)
        loads.append(loading_terms(h, m, rh, rl, k))
        rh_ref, rl_ref = (rho_ref, rlo_ref) if rho else (rhw_ref, rlw_ref)
        rh_ref[pl.ds(at, sub), :] = rh
        rl_ref[pl.ds(at, sub), :] = rl
    load_ref[:, : -2 * LANES] = add(loads)


def factor_kernel(k, half, sub, lg_ref, rh_ref, rl_ref, fac_ref):
    lg = lg_ref[...]
    for i in range(half // sub):
        rows = pl.ds(i * sub, sub)
        fac_ref[:, i * sub : (i + 1) * sub] = factor_terms(rh_ref[rows, :], rl_ref[rows, :], lg, k)


def move_loadings_kernel(n_terms, *refs):
    terms = refs[:n_terms]
    lt_ref, lm_ref, sl_ref, newl_ref, halfl_ref, ly_ref, lg_ref = refs[n_terms:]
    step = jnp.tile(sl_ref[...], (1, lt_ref.shape[1] // LANES))
    halfl = lm_ref[...] + 0.5 * step * (add([t[:, : lt_ref.shape[1]] for t in terms]) - lt_ref[...])
    newl = lt_ref[...] + step * halfl
    halfl_ref[...] = halfl
    newl_ref[...] = newl
    fill_loadings(newl, ly_ref, lg_ref)


def second_kernel(k, half, sub, start, z_ref, ly_ref, lg_ref, cnt_ref, fac_ref, lik_ref, rh_ref, rl_ref):
    ly, lg = ly_ref[...], lg_ref[...]
    likes, sums = [], []
    for i in range(half // sub):
        rows = pl.ds(i * sub, sub)
        cf = cnt_ref[pl.ds(start + i * sub, sub), :]
        y, inten, rh, rl, _, _ = residuals(z_ref[:, rows], cf, ly)
        rh_ref[rows, :] = rh
        rl_ref[rows, :] = rl
        fac_ref[:, rows] = factor_terms(rh, rl, lg, k)
        likes.append(rows_to_8(cf * y))
        sums.append(rows_to_8(inten))
    lik_ref[...] = add(sums) - f32(LN2) * add(likes)


def loading_kernel(k, half, sub, zo_ref, rho_ref, rlo_ref, zw_ref, rhw_ref, rlw_ref, liko_ref, likw_ref, load_ref):
    loads = []
    for z_ref, rh_ref, rl_ref in ((zo_ref, rho_ref, rlo_ref), (zw_ref, rhw_ref, rlw_ref)):
        for i in range(half // sub):
            rows = pl.ds(i * sub, sub)
            h, m, _ = split3(z_ref[:, rows])
            loads.append(loading_terms(h, m, rh_ref[rows, :], rl_ref[rows, :], k))
    load_ref[:, : -2 * LANES] = add(loads)
    first, load_ref[:, -LANES:] = pack_rims(in_order(zw_ref[...], zo_ref[...]), k)
    like = jnp.sum(fold_lanes(liko_ref[...] + likw_ref[...]), 1, keepdims=True)
    like = jnp.concatenate([like, jnp.zeros((k - 8, 1), f32)], 0)
    load_ref[:, -2 * LANES : -LANES] = jnp.where(lane(first.shape) == SPARE, like, first)


def lane(shape):
    return lax.broadcasted_iota(jnp.int32, shape, len(shape) - 1)


SPARE = TY - 1


def pack_rims(vregs, k):
    assert len(vregs) < TY
    q = lax.rem(lane((k, LANES)), TY)
    first = jnp.zeros((k, LANES), f32)
    last = jnp.zeros((k, LANES), f32)
    for j, v in enumerate(vregs):
        first = jnp.where(q == j, pltpu.roll(v, j, 1) if j else v, first)
        last = jnp.where(q == j, pltpu.roll(v, (j - TY + 1) % LANES, 1), last)
    return first, last


def prior_of(vregs, upper, lower, k):
    q = lax.rem(lane((k, LANES)), TY)
    wide = lane((k, LANES))
    n = len(vregs)
    out = []
    for j, v in enumerate(vregs):
        back = jnp.where(q == 0, 0.0, pltpu.roll(v, 1, 1))
        ahead = jnp.where(q == TY - 1, 0.0, pltpu.roll(v, LANES - 1, 1))
        prev = vregs[j - 1] if j else upper
        nxt = vregs[j + 1] if j + 1 < n else lower
        above = jnp.where(wide < TY, pltpu.roll(prev, TY, 1), pltpu.roll(v, TY, 1))
        below = jnp.where(wide >= LANES - TY, pltpu.roll(nxt, LANES - TY, 1), pltpu.roll(v, LANES - TY, 1))
        out.append((kappa_sq + 4.0) * v - (above + below + (back + ahead)))
    return out


def beside_of(left, right, half, k):
    q = lax.rem(lane((k, LANES)), TY)
    n = half // LANES
    low = core() == 0
    left = jnp.where(low, left, pltpu.roll(left, (LANES - n) % LANES, 1))
    right = jnp.where(low, right, pltpu.roll(right, (LANES - n) % LANES, 1))
    out = []
    for j in range(n):
        lrim = pltpu.roll(left, LANES - j, 1) if j else left
        rrim = pltpu.roll(right, (TY - 1 - j) % LANES, 1)
        out.append(jnp.where(q == 0, lrim, 0.0) + jnp.where(q == TY - 1, rrim, 0.0))
    return out


def sides(ride, refs):
    me, n = lax.axis_index("site"), lax.axis_size("site")
    even = lax.rem(me, 2) == 0
    if ride:
        pair, one, two = refs
        near = jnp.where(even, pair[:, -2 * LANES : -LANES], pair[:, -LANES:])
        row = me // 2
        close = (lax.rem(row, 2) == 1) == even
        far = jnp.where(close, one[:, -2 * LANES : -LANES], two[:, -LANES:])
    else:
        near, far = refs[0][...], refs[1][...]
    left = jnp.where(me == 0, 0.0, jnp.where(even, far, near))
    right = jnp.where(me == n - 1, 0.0, jnp.where(even, near, far))
    return left, right


def rims_of(vregs, k):
    first, last = pack_rims(vregs, k)
    even = lax.rem(lax.axis_index("site"), 2) == 0
    return jnp.where(even, last, first), jnp.where(even, first, last)


def vregs_of(array):
    return [array[:, j * LANES : (j + 1) * LANES] for j in range(array.shape[1] // LANES)]


def rims_kernel(k, z_ref, near_ref, far_ref):
    near_ref[...], far_ref[...] = rims_of(vregs_of(z_ref[0]), k)


def pair_stage_kernel(own_ref, got_ref, out_ref):
    site = lax.axis_index("site")
    out_ref[:, : -2 * LANES] = own_ref[:, : -2 * LANES] + got_ref[:, : -2 * LANES]
    even = lax.rem(site, 2) == 0
    own_first, got_first = own_ref[:, -2 * LANES : -LANES], got_ref[:, -2 * LANES : -LANES]
    first = jnp.where(even, own_first, got_first)
    last = jnp.where(even, got_ref[:, -LANES:], own_ref[:, -LANES:])
    low = lax.rem(site // 2, 2) == 0
    spare = lane(first.shape) == SPARE
    out_ref[:, -2 * LANES : -LANES] = jnp.where(spare, own_first + got_first, jnp.where(low, last, first))
    out_ref[:, -LANES:] = jnp.where(low, first, last)


def row_stage_kernel(own_ref, got_ref, out_ref):
    wide = slice(None), slice(0, own_ref.shape[1] - LANES)
    both = own_ref[wide] + got_ref[wide]
    out_ref[:, :-LANES] = both[:, :-LANES]
    rim = both[:, -LANES:]
    out_ref[:, -LANES:] = jnp.where(lane(rim.shape) == SPARE, rim, got_ref[:, -LANES:])


def ahead_kernel(k, half, z_ref, mom_ref, upper_ref, lower_ref, gain_ref, sf_ref, sl_ref, a_ref, z_own_ref, s_ref, l_ref):
    c = core()
    step = sf_ref[0]
    out = prior_of(vregs_of(z_ref[0]), upper_ref[...], lower_ref[...], k)
    n = half // LANES
    gain = gain_ref[...] * (0.5 * step)
    for j in range(n):
        at = pl.ds(j * LANES, LANES)
        own = jnp.where(c == 0, out[j], out[n + j])
        src = pl.ds(pl.multiple_of(c * half + j * LANES, LANES), LANES)
        a_ref[:, at] = mom_ref[0, :, src] - gain * own
        z_own_ref[:, at] = z_ref[0, :, src]
    s_ref[...] = jnp.full(s_ref.shape, step, f32)
    l_ref[...] = jnp.full(l_ref.shape, sl_ref[0], f32)


def move_kernel(ride, k, half, own_ref, other_ref, a_ref, z_ref, s_ref, gain_ref, *refs):
    *halo, half_ref, moved_ref = refs
    beside = beside_of(*sides(ride, halo), half, k)
    step, gain = s_ref[...], gain_ref[...]
    for j in range(half // LANES):
        at = pl.ds(j * LANES, LANES)
        h = a_ref[:, at] + (0.5 * step) * ((own_ref[:, at] + other_ref[:, at]) + gain * beside[j])
        half_ref[:, at] = h
        moved_ref[:, at] = z_ref[:, at] + step * h


def in_order(own, oth):
    first = core() == 0
    own, oth = vregs_of(own), vregs_of(oth)
    return [jnp.where(first, a, b) for a, b in zip(own, oth)] + [jnp.where(first, b, a) for a, b in zip(own, oth)]


def join_kernel(k, own_ref, oth_ref, near_ref, far_ref):
    near_ref[...], far_ref[...] = rims_of(in_order(own_ref[...], oth_ref[...]), k)


def behind_kernel(k, half, own_ref, oth_ref, h_ref, upper_ref, lower_ref, gain_ref, s_ref, a_ref, e_ref):
    c = core()
    out = prior_of(in_order(own_ref[...], oth_ref[...]), upper_ref[...], lower_ref[...], k)
    n = half // LANES
    gain = gain_ref[...]
    energy = jnp.zeros((k, LANES), f32)
    for j in range(n):
        at = pl.ds(j * LANES, LANES)
        own = gain * jnp.where(c == 0, out[j], out[n + j])
        energy = energy + own_ref[:, at] * own
        a_ref[:, at] = h_ref[:, at] - (0.5 * s_ref[...]) * own
    e_ref[...] = energy


def finish_kernel(ride, k, half, n_terms, shares, *refs):
    terms = refs[:n_terms]
    own_ref, other_ref, a_ref, z_ref, s_ref, gain_ref, pe_ref, newl_ref, halfl_ref, sl_ref = refs[n_terms : n_terms + 10]
    *halo, end_ref, endl_ref, share_ref = refs[n_terms + 10 :]
    beside = beside_of(*sides(ride, halo), half, k)
    step, gain = s_ref[...], gain_ref[...]
    energy = pe_ref[...]
    for j in range(half // LANES):
        at = pl.ds(j * LANES, LANES)
        rim = gain * beside[j]
        e = a_ref[:, at] + (0.5 * step) * ((own_ref[:, at] + other_ref[:, at]) + rim)
        end_ref[:, at] = e
        energy = energy + (e * e - z_ref[:, at] * rim)
    newl = newl_ref[...]
    species = newl.shape[1]
    load = add([t[:, :species] for t in terms])
    step = jnp.tile(sl_ref[...], (1, species // LANES))
    endl = halfl_ref[...] + (0.5 * step) * (load - newl)
    endl_ref[...] = endl
    rim = add([t[:, species : species + LANES] for t in terms])
    loadings = 0.5 * fold_lanes(endl * endl + newl * newl) + jnp.where(lane(rim.shape) == SPARE, rim, 0.0)
    share = jnp.sum((0.5 / shares[0]) * energy + (1.0 / shares[1]) * loadings, 0, keepdims=True)
    share_ref[...] = jnp.broadcast_to(share, share_ref.shape)


def output_kernel(half, own_ref, oth_ref, loadings_ref, full_ref, out_ref):
    c = core()
    own, oth = own_ref[...], oth_ref[...]
    full_ref[0, :, :half] = jnp.where(c == 0, own, oth)
    full_ref[0, :, half:] = jnp.where(c == 0, oth, own)
    out_ref[...] = loadings_ref[...]


def last_kernel(half, entries, own_ref, oth_ref, loadings_ref, shares_ref, full_ref, out_ref, energy_ref):
    output_kernel(half, own_ref, oth_ref, loadings_ref, full_ref, out_ref)
    energy_ref[0] = jnp.sum(shares_ref[...]) / entries


def local(
    counts, factors, loadings, factor_momenta, loading_momenta, precision, factor_step, loading_step
):
    k, cells = factors.shape[1:]
    species = loadings.shape[0]
    half = cells // 2
    sub = 640 if half % 640 == 0 else half
    n_site, n_sp = lax.axis_size("site"), lax.axis_size("sp")
    site, chips = mask_groups(n_site), mask_groups(n_sp)[1:]
    lt, lm = loadings.T, loading_momenta.T
    gain = jnp.broadcast_to(precision[:, None], (k, LANES))
    zero_rim = jnp.zeros((k, LANES), f32)

    ride = rides(n_site)

    def exchange(load):
        if not ride:
            return sum_terms(load, "site", site), ()
        got = swap(load, "site", 1)
        (two,) = call(pair_stage_kernel, [VMEM] * 2, [load.shape])(load, got)
        got_two = swap(two, "site", 2)
        (four,) = call(row_stage_kernel, [VMEM] * 2, [(k, species + LANES)])(two, got_two)
        got_four = swap(four, "site", 4)
        return [four, got_four], (got, got_two, got_four)

    def upright(low, high):
        if n_site <= TGY:
            return zero_rim, zero_rim
        lead = jnp.zeros((k, LANES - TY), f32)
        upper = jnp.concatenate([lead, from_behind(high, "site", TGY)], 1)
        return upper, jnp.concatenate([from_behind(low, "site", -TGY), lead], 1)

    def sideways(kernel, halo, *arrays):
        if ride:
            return halo
        near, far = call(functools.partial(kernel, k), [VMEM] * len(arrays), [(k, LANES)] * 2)(*arrays)
        return paired(near, "site", 0), paired(far, "site", 1)

    def share(own, oth):
        terms = sum_terms(own + swap(oth, "sp", 1), "sp", chips)
        return terms[0], add(terms[1:])

    rates, grads = (6 * k, species), (2 * k, species)
    load, lg, held, rho, rlo, rhw, rlw = call(
        functools.partial(first_kernel, k, half, sub),
        [HBM, HBM, HBM],
        [(k, species + 2 * LANES), grads, (cells, species)] + [(half, species)] * 4,
        [
            pltpu.VMEM(rates, bf16),
            pltpu.VMEM((1, k, cells), f32),
            pltpu.VMEM((k, species), f32),
            pltpu.VMEM((cells, species), jnp.int32),
            pltpu.SemaphoreType.DMA((cells // sub,)),
            pltpu.SemaphoreType.DMA((2,)),
        ],
        16,
        (1, 3, 4, 5, 6),
    )(*[pltpu.with_memory_space_constraint(x, pltpu.HBM) for x in (factors, lt, counts)])
    load_terms, halo = exchange(load)
    (oth,), (own,) = [
        call(functools.partial(factor_kernel, k, half, sub), [VMEM] * 3, [(k, half)])(lg, rh, rl)
        for rh, rl in ((rho, rlo), (rhw, rlw))
    ]
    own, other = share(own, oth)

    halo = sideways(rims_kernel, halo, factors)
    edges = upright(factors[0, :, :TY], factors[0, :, cells - TY :])
    a1, z_own, svec, lvec = call(
        functools.partial(ahead_kernel, k, half),
        [VMEM] * 5 + [SMEM] * 2,
        [(k, half), (k, half), (k, LANES), (k, LANES)],
    )(factors, factor_momenta, *edges, gain, factor_step, loading_step)
    half_own, moved_own = call(
        functools.partial(move_kernel, ride, k, half), [VMEM] * (6 + len(halo)), [(k, half)] * 2
    )(own, other, a1, z_own, svec, gain, *halo)
    moved_oth = swap(moved_own, "sp", 1)

    newl, halfl, ly, lg = call(
        functools.partial(move_loadings_kernel, len(load_terms)),
        [VMEM] * (len(load_terms) + 3),
        [(k, species)] * 2 + [rates, grads],
        packed=(2, 3),
    )(*load_terms, lt, lm, lvec)
    new_factors, new_loadings = call(
        functools.partial(output_kernel, half), [VMEM] * 3, [(1, k, cells), (k, species)]
    )(moved_own, moved_oth, newl)
    (own, lik_own, *parts_own), (oth, lik_oth, *parts_oth) = [
        call(
            functools.partial(second_kernel, k, half, sub, start),
            [VMEM] * 4,
            [(k, half), (8, species), (half, species), (half, species)],
            limit=8,
            packed=(2, 3),
        )(z, ly, lg, held)
        for start, z in ((half, moved_own), (0, moved_oth))
    ]
    (load,) = call(functools.partial(loading_kernel, k, half, sub), [VMEM] * 8, [(k, species + 2 * LANES)])(
        moved_oth, *parts_oth, moved_own, *parts_own, lik_oth, lik_own
    )
    load_terms, halo = exchange(load)
    own, other = share(own, oth)

    halo = sideways(join_kernel, halo, moved_own, moved_oth)
    edges = upright(new_factors[0, :, :TY], new_factors[0, :, cells - TY :])
    a2, prior_energy = call(
        functools.partial(behind_kernel, k, half), [VMEM] * 7, [(k, half), (k, LANES)]
    )(moved_own, moved_oth, half_own, *edges, gain, svec)
    n_devices = n_site * n_sp
    end_own, endl, shares = call(
        functools.partial(finish_kernel, ride, k, half, len(load_terms), (n_sp // 2, n_site)),
        [VMEM] * (len(load_terms) + 10 + len(halo)),
        [(k, half), (k, species), (n_devices, LANES)],
    )(*load_terms, own, other, a2, moved_own, svec, gain, prior_energy, newl, halfl, lvec, *halo)
    end_oth = swap(end_own, "sp", 1)
    shares = lax.all_to_all(shares, ("site", "sp"), 0, 0, tiled=True)
    new_momenta, end_loadings, energy = call(
        functools.partial(last_kernel, half, n_site * cells * n_sp * species),
        [VMEM] * 4,
        [(1, k, cells), (k, species), (1,)],
    )(end_own, end_oth, endl, shares)
    return new_factors, new_momenta, new_loadings.T, end_loadings.T, energy


def solution(mesh):
    placed = (
        P("site", None, "sp"),
        P("site", None, None),
        P("sp", None),
        P("site", None, None),
        P("sp", None),
        P(),
        P(),
        P(),
    )

    return jax.shard_map(
        local,
        mesh=mesh,
        in_specs=placed,
        out_specs=(P("site", None, None), P("site", None, None), P("sp", None), P("sp", None), P()),
        check_vma=False,
    )
```

```python
import functools

import jax
import jax.numpy as jnp
from jax import lax
from jax.experimental import pallas as pl
from jax.experimental.pallas import tpu as pltpu
from jax.sharding import PartitionSpec as P


TY = 64
TGY = 8
LANES = 128

kappa_sq = 0.25
LOG2E = 1.4426950408889634
LN2 = 0.6931471805599453
f32, bf16 = jnp.float32, jnp.bfloat16


VMEM = pl.BlockSpec(memory_space=pltpu.VMEM)
SMEM = pl.BlockSpec(memory_space=pltpu.SMEM)
HBM = pl.BlockSpec(memory_space=pltpu.HBM)


def swap(block, axis, mask):
    return lax.ppermute(block, axis, [(i, i ^ mask) for i in range(lax.axis_size(axis))])


def from_behind(block, axis, distance):
    devices = range(lax.axis_size(axis))
    route = [(i - distance, i) for i in devices if i - distance in devices]
    return lax.ppermute(block, axis, route)


def paired(block, axis, first):
    n = lax.axis_size(axis)
    route = [(i, i + 1 if (i - first) % 2 == 0 else i - 1) for i in range(n)]
    return lax.ppermute(block, axis, [(i, j) for i, j in route if 0 <= j < n])


def mask_groups(n):
    groups, stride = [], 1
    while stride < n:
        radix = 2 if stride == 1 or n // stride == 2 else 4
        groups.append([stride * g for g in range(1, radix)])
        stride *= radix
    return groups


def rides(n_site):
    return n_site == 8 == TGY


def add(terms):
    return functools.reduce(lambda a, b: a + b, terms)


def sum_terms(block, axis, groups):
    terms = [block]
    for masks in groups:
        total = add(terms)
        terms = [total] + [swap(total, axis, m) for m in masks]
    return terms


def call(kernel, in_specs, outs, scratch=(), limit=4, packed=()):
    return pl.pallas_call(
        kernel,
        in_specs=in_specs,
        out_specs=[SMEM if s == (1,) else VMEM for s in outs],
        out_shape=[jax.ShapeDtypeStruct(s, bf16 if i in packed else f32) for i, s in enumerate(outs)],
        scratch_shapes=list(scratch),
        compiler_params=pltpu.CompilerParams(vmem_limit_bytes=limit << 20),
    )


def core():
    return lax.rem(lax.axis_index("sp"), 2)


def split3(x):
    h = x.astype(bf16)
    r = x - h.astype(f32)
    m = r.astype(bf16)
    return h, m, (r - m.astype(f32)).astype(bf16)


def dotg(a, b, ca, cb):
    return lax.dot_general(a, b, (((ca,), (cb,)), ((), ())), preferred_element_type=f32)


def residuals(zb, c, ly):
    h, m, l = split3(zb)
    y = dotg(jnp.concatenate([h, h, h, m, m, l], 0), ly, 0, 0)
    i = jnp.exp2(y)
    r = c - i
    rh = r.astype(bf16)
    return y, i, rh, (r - rh.astype(f32)).astype(bf16), h, m


def factor_terms(rh, rl, lg, k):
    a = dotg(lg, rh, 1, 1)
    return a[:k] + a[k:] + dotg(lg[k:], rl, 1, 1)


def loading_terms(h, m, rh, rl, k):
    a = dotg(jnp.concatenate([m, h], 0), rh, 1, 0)
    return a[:k] + a[k:] + dotg(h, rl, 1, 0)


def fill_loadings(lt, ly_ref, lg_ref):
    h, m, l = split3(lt * f32(LOG2E))
    ly_ref[...] = jnp.concatenate([h, m, l, h, m, h], 0)
    h, m, _ = split3(lt)
    lg_ref[...] = jnp.concatenate([m, h], 0)


def fold_lanes(x):
    return add([x[:, j * LANES : (j + 1) * LANES] for j in range(x.shape[1] // LANES)])


def rows_to_8(x):
    return jnp.sum(x.reshape(x.shape[0] // 8, 8, x.shape[1]), 0)


DEPTH = 3


def first_kernel(
    k, half, sub, z_hbm, lt_hbm, cnt_ref, load_ref, lg_ref, held_ref, rho_ref, rlo_ref, rhw_ref, rlw_ref,
    ly_ref, z_ref, lt_ref, buf_ref, sem, sems
):
    c = core()
    pieces = [(rho, at) for rho in (1, 0) for at in range(0, half, sub)]

    def place(i):
        rho, at = pieces[i]
        return pl.multiple_of(lax.rem(rho + c, 2) * half + at, LANES)

    def kept(i):
        return pl.ds(i * sub, sub)

    def copy(i):
        return pltpu.make_async_copy(cnt_ref.at[0, pl.ds(place(i), sub)], buf_ref.at[kept(i)], sem.at[i])

    small = [
        pltpu.make_async_copy(lt_hbm, lt_ref, sems.at[0]),
        pltpu.make_async_copy(z_hbm, z_ref, sems.at[1]),
    ]
    for job in small:
        job.start()
    for i in range(min(DEPTH, len(pieces))):
        copy(i).start()
    small[0].wait()
    fill_loadings(lt_ref[...], ly_ref, lg_ref)
    small[1].wait()
    load_ref[:, -2 * LANES : -LANES], load_ref[:, -LANES:] = pack_rims(vregs_of(z_ref[0]), k)
    ly = ly_ref[...]
    loads = []
    for i, (rho, at) in enumerate(pieces):
        copy(i).wait()
        if i + DEPTH < len(pieces):
            copy(i + DEPTH).start()
        cf = buf_ref[kept(i), :].astype(f32)
        held_ref[kept(i), :] = cf
        _, _, rh, rl, h, m = residuals(z_ref[0, :, pl.ds(place(i), sub)], cf, ly)
        loads.append(loading_terms(h, m, rh, rl, k))
        rh_ref, rl_ref = (rho_ref, rlo_ref) if rho else (rhw_ref, rlw_ref)
        rh_ref[pl.ds(at, sub), :] = rh
        rl_ref[pl.ds(at, sub), :] = rl
    load_ref[:, : -2 * LANES] = add(loads)


def factor_kernel(k, half, sub, lg_ref, rh_ref, rl_ref, fac_ref):
    lg = lg_ref[...]
    for i in range(half // sub):
        rows = pl.ds(i * sub, sub)
        fac_ref[:, i * sub : (i + 1) * sub] = factor_terms(rh_ref[rows, :], rl_ref[rows, :], lg, k)


def move_loadings_kernel(n_terms, *refs):
    terms = refs[:n_terms]
    lt_ref, lm_ref, sl_ref, newl_ref, halfl_ref, ly_ref, lg_ref = refs[n_terms:]
    step = jnp.tile(sl_ref[...], (1, lt_ref.shape[1] // LANES))
    halfl = lm_ref[...] + 0.5 * step * (add([t[:, : lt_ref.shape[1]] for t in terms]) - lt_ref[...])
    newl = lt_ref[...] + step * halfl
    halfl_ref[...] = halfl
    newl_ref[...] = newl
    fill_loadings(newl, ly_ref, lg_ref)


def second_kernel(k, half, sub, start, z_ref, ly_ref, lg_ref, cnt_ref, fac_ref, lik_ref, rh_ref, rl_ref):
    ly, lg = ly_ref[...], lg_ref[...]
    likes, sums = [], []
    for i in range(half // sub):
        rows = pl.ds(i * sub, sub)
        cf = cnt_ref[pl.ds(start + i * sub, sub), :]
        y, inten, rh, rl, _, _ = residuals(z_ref[:, rows], cf, ly)
        rh_ref[rows, :] = rh
        rl_ref[rows, :] = rl
        fac_ref[:, rows] = factor_terms(rh, rl, lg, k)
        likes.append(rows_to_8(cf * y))
        sums.append(rows_to_8(inten))
    lik_ref[...] = add(sums) - f32(LN2) * add(likes)


def loading_kernel(k, half, sub, zo_ref, rho_ref, rlo_ref, zw_ref, rhw_ref, rlw_ref, load_ref):
    loads = []
    for z_ref, rh_ref, rl_ref in ((zo_ref, rho_ref, rlo_ref), (zw_ref, rhw_ref, rlw_ref)):
        for i in range(half // sub):
            rows = pl.ds(i * sub, sub)
            h, m, _ = split3(z_ref[:, rows])
            loads.append(loading_terms(h, m, rh_ref[rows, :], rl_ref[rows, :], k))
    load_ref[:, : -2 * LANES] = add(loads)
    load_ref[:, -2 * LANES : -LANES], load_ref[:, -LANES:] = pack_rims(in_order(zw_ref[...], zo_ref[...]), k)


def lane(shape):
    return lax.broadcasted_iota(jnp.int32, shape, len(shape) - 1)


def pack_rims(vregs, k):
    assert len(vregs) <= TY
    q = lax.rem(lane((k, LANES)), TY)
    first = jnp.zeros((k, LANES), f32)
    last = jnp.zeros((k, LANES), f32)
    for j, v in enumerate(vregs):
        first = jnp.where(q == j, pltpu.roll(v, j, 1) if j else v, first)
        last = jnp.where(q == j, pltpu.roll(v, (j - TY + 1) % LANES, 1), last)
    return first, last


def prior_of(vregs, upper, lower, k):
    q = lax.rem(lane((k, LANES)), TY)
    wide = lane((k, LANES))
    n = len(vregs)
    out = []
    for j, v in enumerate(vregs):
        back = jnp.where(q == 0, 0.0, pltpu.roll(v, 1, 1))
        ahead = jnp.where(q == TY - 1, 0.0, pltpu.roll(v, LANES - 1, 1))
        prev = vregs[j - 1] if j else upper
        nxt = vregs[j + 1] if j + 1 < n else lower
        above = jnp.where(wide < TY, pltpu.roll(prev, TY, 1), pltpu.roll(v, TY, 1))
        below = jnp.where(wide >= LANES - TY, pltpu.roll(nxt, LANES - TY, 1), pltpu.roll(v, LANES - TY, 1))
        out.append((kappa_sq + 4.0) * v - (above + below + (back + ahead)))
    return out


def beside_of(left, right, half, k):
    q = lax.rem(lane((k, LANES)), TY)
    n = half // LANES
    low = core() == 0
    left = jnp.where(low, left, pltpu.roll(left, (LANES - n) % LANES, 1))
    right = jnp.where(low, right, pltpu.roll(right, (LANES - n) % LANES, 1))
    out = []
    for j in range(n):
        lrim = pltpu.roll(left, LANES - j, 1) if j else left
        rrim = pltpu.roll(right, (TY - 1 - j) % LANES, 1)
        out.append(jnp.where(q == 0, lrim, 0.0) + jnp.where(q == TY - 1, rrim, 0.0))
    return out


def sides(ride, refs):
    me, n = lax.axis_index("site"), lax.axis_size("site")
    even = lax.rem(me, 2) == 0
    if ride:
        pair, one, three = refs
        near = jnp.where(even, pair[:, -2 * LANES : -LANES], pair[:, -LANES:])
        row = me // 2
        close = (lax.rem(row, 2) == 1) == even
        far = jnp.where(close, one[:, -LANES:], three[:, -LANES:])
    else:
        near, far = refs[0][...], refs[1][...]
    left = jnp.where(me == 0, 0.0, jnp.where(even, far, near))
    right = jnp.where(me == n - 1, 0.0, jnp.where(even, near, far))
    return left, right


def rims_of(vregs, k):
    first, last = pack_rims(vregs, k)
    even = lax.rem(lax.axis_index("site"), 2) == 0
    return jnp.where(even, last, first), jnp.where(even, first, last)


def vregs_of(array):
    return [array[:, j * LANES : (j + 1) * LANES] for j in range(array.shape[1] // LANES)]


def rims_kernel(k, z_ref, near_ref, far_ref):
    near_ref[...], far_ref[...] = rims_of(vregs_of(z_ref[0]), k)


def stage_kernel(own_ref, got_ref, one_ref, two_ref, three_ref):
    both = own_ref[:, : -2 * LANES] + got_ref[:, : -2 * LANES]
    site = lax.axis_index("site")
    even = lax.rem(site, 2) == 0
    first = jnp.where(even, own_ref[:, -2 * LANES : -LANES], got_ref[:, -2 * LANES : -LANES])
    last = jnp.where(even, got_ref[:, -LANES:], own_ref[:, -LANES:])
    low = lax.rem(site // 2, 2) == 0
    one_ref[:, :-LANES] = both
    one_ref[:, -LANES:] = jnp.where(low, last, first)
    two_ref[...] = both
    three_ref[:, :-LANES] = both
    three_ref[:, -LANES:] = jnp.where(low, first, last)


def ahead_kernel(k, half, z_ref, mom_ref, upper_ref, lower_ref, gain_ref, sf_ref, sl_ref, a_ref, z_own_ref, s_ref, l_ref):
    c = core()
    step = sf_ref[0]
    out = prior_of(vregs_of(z_ref[0]), upper_ref[...], lower_ref[...], k)
    n = half // LANES
    gain = gain_ref[...] * (0.5 * step)
    for j in range(n):
        at = pl.ds(j * LANES, LANES)
        own = jnp.where(c == 0, out[j], out[n + j])
        src = pl.ds(pl.multiple_of(c * half + j * LANES, LANES), LANES)
        a_ref[:, at] = mom_ref[0, :, src] - gain * own
        z_own_ref[:, at] = z_ref[0, :, src]
    s_ref[...] = jnp.full(s_ref.shape, step, f32)
    l_ref[...] = jnp.full(l_ref.shape, sl_ref[0], f32)


def move_kernel(ride, k, half, own_ref, other_ref, a_ref, z_ref, s_ref, gain_ref, *refs):
    *halo, half_ref, moved_ref = refs
    beside = beside_of(*sides(ride, halo), half, k)
    step, gain = s_ref[...], gain_ref[...]
    for j in range(half // LANES):
        at = pl.ds(j * LANES, LANES)
        h = a_ref[:, at] + (0.5 * step) * ((own_ref[:, at] + other_ref[:, at]) + gain * beside[j])
        half_ref[:, at] = h
        moved_ref[:, at] = z_ref[:, at] + step * h


def in_order(own, oth):
    first = core() == 0
    own, oth = vregs_of(own), vregs_of(oth)
    return [jnp.where(first, a, b) for a, b in zip(own, oth)] + [jnp.where(first, b, a) for a, b in zip(own, oth)]


def join_kernel(k, own_ref, oth_ref, near_ref, far_ref):
    near_ref[...], far_ref[...] = rims_of(in_order(own_ref[...], oth_ref[...]), k)


def behind_kernel(k, half, own_ref, oth_ref, h_ref, upper_ref, lower_ref, gain_ref, s_ref, a_ref, e_ref):
    c = core()
    out = prior_of(in_order(own_ref[...], oth_ref[...]), upper_ref[...], lower_ref[...], k)
    n = half // LANES
    gain = gain_ref[...]
    energy = jnp.zeros((k, LANES), f32)
    for j in range(n):
        at = pl.ds(j * LANES, LANES)
        own = gain * jnp.where(c == 0, out[j], out[n + j])
        energy = energy + own_ref[:, at] * own
        a_ref[:, at] = h_ref[:, at] - (0.5 * s_ref[...]) * own
    e_ref[...] = energy


def finish_kernel(ride, k, half, n_terms, shares, *refs):
    terms = refs[:n_terms]
    own_ref, other_ref, a_ref, z_ref, s_ref, gain_ref, pe_ref, newl_ref, halfl_ref, sl_ref = refs[n_terms : n_terms + 10]
    liko_ref, likw_ref, *halo, end_ref, endl_ref, share_ref = refs[n_terms + 10 :]
    beside = beside_of(*sides(ride, halo), half, k)
    step, gain = s_ref[...], gain_ref[...]
    energy = pe_ref[...]
    for j in range(half // LANES):
        at = pl.ds(j * LANES, LANES)
        rim = gain * beside[j]
        e = a_ref[:, at] + (0.5 * step) * ((own_ref[:, at] + other_ref[:, at]) + rim)
        end_ref[:, at] = e
        energy = energy + (e * e - z_ref[:, at] * rim)
    newl = newl_ref[...]
    species = newl.shape[1]
    load = add([t[:, :species] for t in terms])
    step = jnp.tile(sl_ref[...], (1, species // LANES))
    endl = halfl_ref[...] + (0.5 * step) * (load - newl)
    endl_ref[...] = endl
    share = (0.5 / shares[0]) * energy + (0.5 / shares[1]) * fold_lanes(endl * endl + newl * newl)
    share = jnp.sum(share, 0, keepdims=True) + jnp.sum(fold_lanes(liko_ref[...] + likw_ref[...]), 0, keepdims=True)
    share_ref[...] = jnp.broadcast_to(share, share_ref.shape)


def output_kernel(half, own_ref, oth_ref, loadings_ref, full_ref, out_ref):
    c = core()
    own, oth = own_ref[...], oth_ref[...]
    full_ref[0, :, :half] = jnp.where(c == 0, own, oth)
    full_ref[0, :, half:] = jnp.where(c == 0, oth, own)
    out_ref[...] = loadings_ref[...]


def last_kernel(half, entries, own_ref, oth_ref, loadings_ref, shares_ref, full_ref, out_ref, energy_ref):
    output_kernel(half, own_ref, oth_ref, loadings_ref, full_ref, out_ref)
    energy_ref[0] = jnp.sum(shares_ref[...]) / entries


def local(
    counts, factors, loadings, factor_momenta, loading_momenta, precision, factor_step, loading_step
):
    k, cells = factors.shape[1:]
    species = loadings.shape[0]
    half = cells // 2
    sub = 640 if half % 640 == 0 else half
    n_site, n_sp = lax.axis_size("site"), lax.axis_size("sp")
    site, chips = mask_groups(n_site), mask_groups(n_sp)[1:]
    lt, lm = loadings.T, loading_momenta.T
    gain = jnp.broadcast_to(precision[:, None], (k, LANES))
    zero_rim = jnp.zeros((k, LANES), f32)

    ride = rides(n_site)

    def exchange(load):
        if not ride:
            return sum_terms(load, "site", site), ()
        got = swap(load, "site", 1)
        wide, narrow = (k, species + LANES), (k, species)
        stage = call(stage_kernel, [VMEM] * 2, [wide, narrow, wide])(load, got)
        terms = [swap(t, "site", m) for t, m in zip(stage, site[1])]
        return [stage[1], *terms], (got, terms[0], terms[2])

    def upright(low, high):
        if n_site <= TGY:
            return zero_rim, zero_rim
        lead = jnp.zeros((k, LANES - TY), f32)
        upper = jnp.concatenate([lead, from_behind(high, "site", TGY)], 1)
        return upper, jnp.concatenate([from_behind(low, "site", -TGY), lead], 1)

    def sideways(kernel, halo, *arrays):
        if ride:
            return halo
        near, far = call(functools.partial(kernel, k), [VMEM] * len(arrays), [(k, LANES)] * 2)(*arrays)
        return paired(near, "site", 0), paired(far, "site", 1)

    def share(own, oth):
        terms = sum_terms(own + swap(oth, "sp", 1), "sp", chips)
        return terms[0], add(terms[1:])

    rates, grads = (6 * k, species), (2 * k, species)
    load, lg, held, rho, rlo, rhw, rlw = call(
        functools.partial(first_kernel, k, half, sub),
        [HBM, HBM, HBM],
        [(k, species + 2 * LANES), grads, (cells, species)] + [(half, species)] * 4,
        [
            pltpu.VMEM(rates, bf16),
            pltpu.VMEM((1, k, cells), f32),
            pltpu.VMEM((k, species), f32),
            pltpu.VMEM((cells, species), jnp.int32),
            pltpu.SemaphoreType.DMA((cells // sub,)),
            pltpu.SemaphoreType.DMA((2,)),
        ],
        16,
        (1, 3, 4, 5, 6),
    )(*[pltpu.with_memory_space_constraint(x, pltpu.HBM) for x in (factors, lt, counts)])
    load_terms, halo = exchange(load)
    (oth,), (own,) = [
        call(functools.partial(factor_kernel, k, half, sub), [VMEM] * 3, [(k, half)])(lg, rh, rl)
        for rh, rl in ((rho, rlo), (rhw, rlw))
    ]
    own, other = share(own, oth)

    halo = sideways(rims_kernel, halo, factors)
    edges = upright(factors[0, :, :TY], factors[0, :, cells - TY :])
    a1, z_own, svec, lvec = call(
        functools.partial(ahead_kernel, k, half),
        [VMEM] * 5 + [SMEM] * 2,
        [(k, half), (k, half), (k, LANES), (k, LANES)],
    )(factors, factor_momenta, *edges, gain, factor_step, loading_step)
    half_own, moved_own = call(
        functools.partial(move_kernel, ride, k, half), [VMEM] * (6 + len(halo)), [(k, half)] * 2
    )(own, other, a1, z_own, svec, gain, *halo)
    moved_oth = swap(moved_own, "sp", 1)

    newl, halfl, ly, lg = call(
        functools.partial(move_loadings_kernel, len(load_terms)),
        [VMEM] * (len(load_terms) + 3),
        [(k, species)] * 2 + [rates, grads],
        packed=(2, 3),
    )(*load_terms, lt, lm, lvec)
    new_factors, new_loadings = call(
        functools.partial(output_kernel, half), [VMEM] * 3, [(1, k, cells), (k, species)]
    )(moved_own, moved_oth, newl)
    (own, lik_own, *parts_own), (oth, lik_oth, *parts_oth) = [
        call(
            functools.partial(second_kernel, k, half, sub, start),
            [VMEM] * 4,
            [(k, half), (8, species), (half, species), (half, species)],
            limit=8,
            packed=(2, 3),
        )(z, ly, lg, held)
        for start, z in ((half, moved_own), (0, moved_oth))
    ]
    (load,) = call(functools.partial(loading_kernel, k, half, sub), [VMEM] * 6, [(k, species + 2 * LANES)])(
        moved_oth, *parts_oth, moved_own, *parts_own
    )
    load_terms, halo = exchange(load)
    own, other = share(own, oth)

    halo = sideways(join_kernel, halo, moved_own, moved_oth)
    edges = upright(new_factors[0, :, :TY], new_factors[0, :, cells - TY :])
    a2, prior_energy = call(
        functools.partial(behind_kernel, k, half), [VMEM] * 7, [(k, half), (k, LANES)]
    )(moved_own, moved_oth, half_own, *edges, gain, svec)
    n_devices = n_site * n_sp
    end_own, endl, shares = call(
        functools.partial(finish_kernel, ride, k, half, len(load_terms), (n_sp // 2, n_site)),
        [VMEM] * (len(load_terms) + 12 + len(halo)),
        [(k, half), (k, species), (n_devices, LANES)],
    )(*load_terms, own, other, a2, moved_own, svec, gain, prior_energy, newl, halfl, lvec, lik_oth, lik_own, *halo)
    end_oth = swap(end_own, "sp", 1)
    shares = lax.all_to_all(shares, ("site", "sp"), 0, 0, tiled=True)
    new_momenta, end_loadings, energy = call(
        functools.partial(last_kernel, half, n_site * cells * n_sp * species),
        [VMEM] * 4,
        [(1, k, cells), (k, species), (1,)],
    )(end_own, end_oth, endl, shares)
    return new_factors, new_momenta, new_loadings.T, end_loadings.T, energy


def solution(mesh):
    placed = (
        P("site", None, "sp"),
        P("site", None, None),
        P("sp", None),
        P("site", None, None),
        P("sp", None),
        P(),
        P(),
        P(),
    )

    return jax.shard_map(
        local,
        mesh=mesh,
        in_specs=placed,
        out_specs=(P("site", None, None), P("site", None, None), P("sp", None), P("sp", None), P()),
        check_vma=False,
    )
```

```python
import functools

import jax
import jax.numpy as jnp
from jax import lax
from jax.experimental import pallas as pl
from jax.experimental.pallas import tpu as pltpu
from jax.sharding import PartitionSpec as P


TY = 64
TGY = 8
LANES = 128

kappa_sq = 0.25
LOG2E = 1.4426950408889634
LN2 = 0.6931471805599453
f32, bf16 = jnp.float32, jnp.bfloat16


VMEM = pl.BlockSpec(memory_space=pltpu.VMEM)
SMEM = pl.BlockSpec(memory_space=pltpu.SMEM)
HBM = pl.BlockSpec(memory_space=pltpu.HBM)


def swap(block, axis, mask):
    return lax.ppermute(block, axis, [(i, i ^ mask) for i in range(lax.axis_size(axis))])


def from_behind(block, axis, distance):
    devices = range(lax.axis_size(axis))
    route = [(i - distance, i) for i in devices if i - distance in devices]
    return lax.ppermute(block, axis, route)


def paired(block, axis, first):
    n = lax.axis_size(axis)
    route = [(i, i + 1 if (i - first) % 2 == 0 else i - 1) for i in range(n)]
    return lax.ppermute(block, axis, [(i, j) for i, j in route if 0 <= j < n])


def mask_groups(n):
    groups, stride = [], 1
    while stride < n:
        radix = 2 if stride == 1 or n // stride == 2 else 4
        groups.append([stride * g for g in range(1, radix)])
        stride *= radix
    return groups


def rides(n_site):
    return n_site == 8 == TGY


def add(terms):
    return functools.reduce(lambda a, b: a + b, terms)


def sum_terms(block, axis, groups):
    terms = [block]
    for masks in groups:
        total = add(terms)
        terms = [total] + [swap(total, axis, m) for m in masks]
    return terms


def call(kernel, in_specs, outs, scratch=(), limit=4, packed=()):
    return pl.pallas_call(
        kernel,
        in_specs=in_specs,
        out_specs=[SMEM if s == (1,) else VMEM for s in outs],
        out_shape=[jax.ShapeDtypeStruct(s, bf16 if i in packed else f32) for i, s in enumerate(outs)],
        scratch_shapes=list(scratch),
        compiler_params=pltpu.CompilerParams(vmem_limit_bytes=limit << 20),
    )


def core():
    return lax.rem(lax.axis_index("sp"), 2)


def split3(x):
    h = x.astype(bf16)
    r = x - h.astype(f32)
    m = r.astype(bf16)
    return h, m, (r - m.astype(f32)).astype(bf16)


def dotg(a, b, ca, cb):
    return lax.dot_general(a, b, (((ca,), (cb,)), ((), ())), preferred_element_type=f32)


def residuals(zb, c, ly):
    h, m, l = split3(zb)
    y = dotg(jnp.concatenate([h, h, h, m, m, l], 0), ly, 0, 0)
    i = jnp.exp2(y)
    r = c - i
    rh = r.astype(bf16)
    return y, i, rh, (r - rh.astype(f32)).astype(bf16), h, m


def factor_terms(rh, rl, lg, k, axis):
    a = dotg(lg, rh, 1, axis)
    return a[:k] + a[k:] + dotg(lg[k:], rl, 1, 0)


def loading_terms(h, m, rh, rl, k):
    a = dotg(jnp.concatenate([m, h], 0), rh, 1, 0)
    return a[:k] + a[k:] + dotg(h, rl, 1, 0)


def fill_loadings(lt, ly_ref, lg_ref):
    h, m, l = split3(lt * f32(LOG2E))
    ly_ref[...] = jnp.concatenate([h, m, l, h, m, h], 0)
    h, m, _ = split3(lt)
    lg_ref[...] = jnp.concatenate([m, h], 0)


def fold_lanes(x):
    return add([x[:, j * LANES : (j + 1) * LANES] for j in range(x.shape[1] // LANES)])


def rows_to_8(x):
    return jnp.sum(x.reshape(x.shape[0] // 8, 8, x.shape[1]), 0)


DEPTH = 3


def first_kernel(
    k, half, sub, z_hbm, lt_hbm, cnt_ref, load_ref, lg_ref, held_ref, rho_ref, rlo_ref, rhw_ref, rlw_ref,
    ly_ref, z_ref, lt_ref, buf_ref, sem, sems
):
    c = core()
    pieces = [(rho, at) for rho in (1, 0) for at in range(0, half, sub)]

    def place(i):
        rho, at = pieces[i]
        return pl.multiple_of(lax.rem(rho + c, 2) * half + at, LANES)

    def kept(i):
        return pl.ds(i * sub, sub)

    def copy(i):
        return pltpu.make_async_copy(cnt_ref.at[0, pl.ds(place(i), sub)], buf_ref.at[kept(i)], sem.at[i])

    small = [
        pltpu.make_async_copy(lt_hbm, lt_ref, sems.at[0]),
        pltpu.make_async_copy(z_hbm, z_ref, sems.at[1]),
    ]
    for job in small:
        job.start()
    for i in range(min(DEPTH, len(pieces))):
        copy(i).start()
    small[0].wait()
    fill_loadings(lt_ref[...], ly_ref, lg_ref)
    small[1].wait()
    load_ref[:, -2 * LANES : -LANES], load_ref[:, -LANES:] = pack_rims(vregs_of(z_ref[0]), k)
    ly = ly_ref[...]
    loads = []
    for i, (rho, at) in enumerate(pieces):
        copy(i).wait()
        if i + DEPTH < len(pieces):
            copy(i + DEPTH).start()
        cf = buf_ref[kept(i), :].astype(f32)
        held_ref[kept(i), :] = cf
        _, _, rh, rl, h, m = residuals(z_ref[0, :, pl.ds(place(i), sub)], cf, ly)
        loads.append(loading_terms(h, m, rh, rl, k))
        rh_ref, rl_ref = (rho_ref, rlo_ref) if rho else (rhw_ref, rlw_ref)
        rh_ref[:, at : at + sub] = rh.T
        rl_ref[:, at : at + sub] = rl.T
    load_ref[:, : -2 * LANES] = add(loads)


def factor_kernel(k, half, sub, lg_ref, rh_ref, rl_ref, fac_ref):
    lg = lg_ref[...]
    for i in range(half // sub):
        here = pl.ds(i * sub, sub)
        fac_ref[:, here] = factor_terms(rh_ref[:, here], rl_ref[:, here], lg, k, 0)


def move_loadings_kernel(n_terms, *refs):
    terms = refs[:n_terms]
    lt_ref, lm_ref, sl_ref, newl_ref, halfl_ref, ly_ref, lg_ref = refs[n_terms:]
    step = jnp.tile(sl_ref[...], (1, lt_ref.shape[1] // LANES))
    halfl = lm_ref[...] + 0.5 * step * (add([t[:, : lt_ref.shape[1]] for t in terms]) - lt_ref[...])
    newl = lt_ref[...] + step * halfl
    halfl_ref[...] = halfl
    newl_ref[...] = newl
    fill_loadings(newl, ly_ref, lg_ref)


def second_kernel(k, half, sub, start, z_ref, ly_ref, lg_ref, cnt_ref, fac_ref, lik_ref, rh_ref, rl_ref, turned_ref):
    ly, lg = ly_ref[...], lg_ref[...]
    likes, sums = [], []
    for i in range(half // sub):
        rows = pl.ds(i * sub, sub)
        cf = cnt_ref[pl.ds(start + i * sub, sub), :]
        y, inten, rh, rl, _, _ = residuals(z_ref[:, rows], cf, ly)
        rh_ref[rows, :] = rh
        rl_ref[rows, :] = rl
        turned_ref[:, rows] = rl.T
        fac_ref[:, rows] = factor_terms(rh, turned_ref[:, rows], lg, k, 1)
        likes.append(rows_to_8(cf * y))
        sums.append(rows_to_8(inten))
    lik_ref[...] = add(sums) - f32(LN2) * add(likes)


def loading_kernel(k, half, sub, zo_ref, rho_ref, rlo_ref, zw_ref, rhw_ref, rlw_ref, load_ref):
    loads = []
    for z_ref, rh_ref, rl_ref in ((zo_ref, rho_ref, rlo_ref), (zw_ref, rhw_ref, rlw_ref)):
        for i in range(half // sub):
            rows = pl.ds(i * sub, sub)
            h, m, _ = split3(z_ref[:, rows])
            loads.append(loading_terms(h, m, rh_ref[rows, :], rl_ref[rows, :], k))
    load_ref[:, : -2 * LANES] = add(loads)
    load_ref[:, -2 * LANES : -LANES], load_ref[:, -LANES:] = pack_rims(in_order(zw_ref[...], zo_ref[...]), k)


def lane(shape):
    return lax.broadcasted_iota(jnp.int32, shape, len(shape) - 1)


def pack_rims(vregs, k):
    assert len(vregs) <= TY
    q = lax.rem(lane((k, LANES)), TY)
    first = jnp.zeros((k, LANES), f32)
    last = jnp.zeros((k, LANES), f32)
    for j, v in enumerate(vregs):
        first = jnp.where(q == j, pltpu.roll(v, j, 1) if j else v, first)
        last = jnp.where(q == j, pltpu.roll(v, (j - TY + 1) % LANES, 1), last)
    return first, last


def prior_of(vregs, upper, lower, k):
    q = lax.rem(lane((k, LANES)), TY)
    wide = lane((k, LANES))
    n = len(vregs)
    out = []
    for j, v in enumerate(vregs):
        back = jnp.where(q == 0, 0.0, pltpu.roll(v, 1, 1))
        ahead = jnp.where(q == TY - 1, 0.0, pltpu.roll(v, LANES - 1, 1))
        prev = vregs[j - 1] if j else upper
        nxt = vregs[j + 1] if j + 1 < n else lower
        above = jnp.where(wide < TY, pltpu.roll(prev, TY, 1), pltpu.roll(v, TY, 1))
        below = jnp.where(wide >= LANES - TY, pltpu.roll(nxt, LANES - TY, 1), pltpu.roll(v, LANES - TY, 1))
        out.append((kappa_sq + 4.0) * v - (above + below + (back + ahead)))
    return out


def beside_of(left, right, half, k):
    q = lax.rem(lane((k, LANES)), TY)
    n = half // LANES
    low = core() == 0
    left = jnp.where(low, left, pltpu.roll(left, (LANES - n) % LANES, 1))
    right = jnp.where(low, right, pltpu.roll(right, (LANES - n) % LANES, 1))
    out = []
    for j in range(n):
        lrim = pltpu.roll(left, LANES - j, 1) if j else left
        rrim = pltpu.roll(right, (TY - 1 - j) % LANES, 1)
        out.append(jnp.where(q == 0, lrim, 0.0) + jnp.where(q == TY - 1, rrim, 0.0))
    return out


def sides(ride, refs):
    me, n = lax.axis_index("site"), lax.axis_size("site")
    even = lax.rem(me, 2) == 0
    if ride:
        pair, one, three = refs
        near = jnp.where(even, pair[:, -2 * LANES : -LANES], pair[:, -LANES:])
        row = me // 2
        close = (lax.rem(row, 2) == 1) == even
        far = jnp.where(close, one[:, -LANES:], three[:, -LANES:])
    else:
        near, far = refs[0][...], refs[1][...]
    left = jnp.where(me == 0, 0.0, jnp.where(even, far, near))
    right = jnp.where(me == n - 1, 0.0, jnp.where(even, near, far))
    return left, right


def rims_of(vregs, k):
    first, last = pack_rims(vregs, k)
    even = lax.rem(lax.axis_index("site"), 2) == 0
    return jnp.where(even, last, first), jnp.where(even, first, last)


def vregs_of(array):
    return [array[:, j * LANES : (j + 1) * LANES] for j in range(array.shape[1] // LANES)]


def rims_kernel(k, z_ref, near_ref, far_ref):
    near_ref[...], far_ref[...] = rims_of(vregs_of(z_ref[0]), k)


def stage_kernel(own_ref, got_ref, one_ref, two_ref, three_ref):
    both = own_ref[:, : -2 * LANES] + got_ref[:, : -2 * LANES]
    site = lax.axis_index("site")
    even = lax.rem(site, 2) == 0
    first = jnp.where(even, own_ref[:, -2 * LANES : -LANES], got_ref[:, -2 * LANES : -LANES])
    last = jnp.where(even, got_ref[:, -LANES:], own_ref[:, -LANES:])
    low = lax.rem(site // 2, 2) == 0
    one_ref[:, :-LANES] = both
    one_ref[:, -LANES:] = jnp.where(low, last, first)
    two_ref[...] = both
    three_ref[:, :-LANES] = both
    three_ref[:, -LANES:] = jnp.where(low, first, last)


def ahead_kernel(k, half, z_ref, mom_ref, upper_ref, lower_ref, gain_ref, sf_ref, sl_ref, a_ref, z_own_ref, s_ref, l_ref):
    c = core()
    step = sf_ref[0]
    out = prior_of(vregs_of(z_ref[0]), upper_ref[...], lower_ref[...], k)
    n = half // LANES
    gain = gain_ref[...] * (0.5 * step)
    for j in range(n):
        at = pl.ds(j * LANES, LANES)
        own = jnp.where(c == 0, out[j], out[n + j])
        src = pl.ds(pl.multiple_of(c * half + j * LANES, LANES), LANES)
        a_ref[:, at] = mom_ref[0, :, src] - gain * own
        z_own_ref[:, at] = z_ref[0, :, src]
    s_ref[...] = jnp.full(s_ref.shape, step, f32)
    l_ref[...] = jnp.full(l_ref.shape, sl_ref[0], f32)


def move_kernel(ride, k, half, own_ref, other_ref, a_ref, z_ref, s_ref, gain_ref, *refs):
    *halo, half_ref, moved_ref = refs
    beside = beside_of(*sides(ride, halo), half, k)
    step, gain = s_ref[...], gain_ref[...]
    for j in range(half // LANES):
        at = pl.ds(j * LANES, LANES)
        h = a_ref[:, at] + (0.5 * step) * ((own_ref[:, at] + other_ref[:, at]) + gain * beside[j])
        half_ref[:, at] = h
        moved_ref[:, at] = z_ref[:, at] + step * h


def in_order(own, oth):
    first = core() == 0
    own, oth = vregs_of(own), vregs_of(oth)
    return [jnp.where(first, a, b) for a, b in zip(own, oth)] + [jnp.where(first, b, a) for a, b in zip(own, oth)]


def join_kernel(k, own_ref, oth_ref, near_ref, far_ref):
    near_ref[...], far_ref[...] = rims_of(in_order(own_ref[...], oth_ref[...]), k)


def behind_kernel(k, half, own_ref, oth_ref, h_ref, upper_ref, lower_ref, gain_ref, s_ref, a_ref, e_ref):
    c = core()
    out = prior_of(in_order(own_ref[...], oth_ref[...]), upper_ref[...], lower_ref[...], k)
    n = half // LANES
    gain = gain_ref[...]
    energy = jnp.zeros((k, LANES), f32)
    for j in range(n):
        at = pl.ds(j * LANES, LANES)
        own = gain * jnp.where(c == 0, out[j], out[n + j])
        energy = energy + own_ref[:, at] * own
        a_ref[:, at] = h_ref[:, at] - (0.5 * s_ref[...]) * own
    e_ref[...] = energy


def finish_kernel(ride, k, half, n_terms, shares, *refs):
    terms = refs[:n_terms]
    own_ref, other_ref, a_ref, z_ref, s_ref, gain_ref, pe_ref, newl_ref, halfl_ref, sl_ref = refs[n_terms : n_terms + 10]
    liko_ref, likw_ref, *halo, end_ref, endl_ref, share_ref = refs[n_terms + 10 :]
    beside = beside_of(*sides(ride, halo), half, k)
    step, gain = s_ref[...], gain_ref[...]
    energy = pe_ref[...]
    for j in range(half // LANES):
        at = pl.ds(j * LANES, LANES)
        rim = gain * beside[j]
        e = a_ref[:, at] + (0.5 * step) * ((own_ref[:, at] + other_ref[:, at]) + rim)
        end_ref[:, at] = e
        energy = energy + (e * e - z_ref[:, at] * rim)
    newl = newl_ref[...]
    species = newl.shape[1]
    load = add([t[:, :species] for t in terms])
    step = jnp.tile(sl_ref[...], (1, species // LANES))
    endl = halfl_ref[...] + (0.5 * step) * (load - newl)
    endl_ref[...] = endl
    share = (0.5 / shares[0]) * energy + (0.5 / shares[1]) * fold_lanes(endl * endl + newl * newl)
    share = jnp.sum(share, 0, keepdims=True) + jnp.sum(fold_lanes(liko_ref[...] + likw_ref[...]), 0, keepdims=True)
    share_ref[...] = jnp.broadcast_to(share, share_ref.shape)


def output_kernel(half, own_ref, oth_ref, loadings_ref, full_ref, out_ref):
    c = core()
    own, oth = own_ref[...], oth_ref[...]
    full_ref[0, :, :half] = jnp.where(c == 0, own, oth)
    full_ref[0, :, half:] = jnp.where(c == 0, oth, own)
    out_ref[...] = loadings_ref[...]


def last_kernel(half, entries, own_ref, oth_ref, loadings_ref, shares_ref, full_ref, out_ref, energy_ref):
    output_kernel(half, own_ref, oth_ref, loadings_ref, full_ref, out_ref)
    energy_ref[0] = jnp.sum(shares_ref[...]) / entries


def local(
    counts, factors, loadings, factor_momenta, loading_momenta, precision, factor_step, loading_step
):
    k, cells = factors.shape[1:]
    species = loadings.shape[0]
    half = cells // 2
    sub = 640 if half % 640 == 0 else half
    n_site, n_sp = lax.axis_size("site"), lax.axis_size("sp")
    site, chips = mask_groups(n_site), mask_groups(n_sp)[1:]
    lt, lm = loadings.T, loading_momenta.T
    gain = jnp.broadcast_to(precision[:, None], (k, LANES))
    zero_rim = jnp.zeros((k, LANES), f32)

    ride = rides(n_site)

    def exchange(load):
        if not ride:
            return sum_terms(load, "site", site), ()
        got = swap(load, "site", 1)
        wide, narrow = (k, species + LANES), (k, species)
        stage = call(stage_kernel, [VMEM] * 2, [wide, narrow, wide])(load, got)
        terms = [swap(t, "site", m) for t, m in zip(stage, site[1])]
        return [stage[1], *terms], (got, terms[0], terms[2])

    def upright(low, high):
        if n_site <= TGY:
            return zero_rim, zero_rim
        lead = jnp.zeros((k, LANES - TY), f32)
        upper = jnp.concatenate([lead, from_behind(high, "site", TGY)], 1)
        return upper, jnp.concatenate([from_behind(low, "site", -TGY), lead], 1)

    def sideways(kernel, halo, *arrays):
        if ride:
            return halo
        near, far = call(functools.partial(kernel, k), [VMEM] * len(arrays), [(k, LANES)] * 2)(*arrays)
        return paired(near, "site", 0), paired(far, "site", 1)

    def share(own, oth):
        terms = sum_terms(own + swap(oth, "sp", 1), "sp", chips)
        return terms[0], add(terms[1:])

    rates, grads = (6 * k, species), (2 * k, species)
    load, lg, held, rho, rlo, rhw, rlw = call(
        functools.partial(first_kernel, k, half, sub),
        [HBM, HBM, HBM],
        [(k, species + 2 * LANES), grads, (cells, species)] + [(species, half)] * 4,
        [
            pltpu.VMEM(rates, bf16),
            pltpu.VMEM((1, k, cells), f32),
            pltpu.VMEM((k, species), f32),
            pltpu.VMEM((cells, species), jnp.int32),
            pltpu.SemaphoreType.DMA((cells // sub,)),
            pltpu.SemaphoreType.DMA((2,)),
        ],
        16,
        (1, 3, 4, 5, 6),
    )(*[pltpu.with_memory_space_constraint(x, pltpu.HBM) for x in (factors, lt, counts)])
    load_terms, halo = exchange(load)
    (oth,), (own,) = [
        call(functools.partial(factor_kernel, k, half, sub), [VMEM] * 3, [(k, half)])(lg, rh, rl)
        for rh, rl in ((rho, rlo), (rhw, rlw))
    ]
    own, other = share(own, oth)

    halo = sideways(rims_kernel, halo, factors)
    edges = upright(factors[0, :, :TY], factors[0, :, cells - TY :])
    a1, z_own, svec, lvec = call(
        functools.partial(ahead_kernel, k, half),
        [VMEM] * 5 + [SMEM] * 2,
        [(k, half), (k, half), (k, LANES), (k, LANES)],
    )(factors, factor_momenta, *edges, gain, factor_step, loading_step)
    half_own, moved_own = call(
        functools.partial(move_kernel, ride, k, half), [VMEM] * (6 + len(halo)), [(k, half)] * 2
    )(own, other, a1, z_own, svec, gain, *halo)
    moved_oth = swap(moved_own, "sp", 1)

    newl, halfl, ly, lg = call(
        functools.partial(move_loadings_kernel, len(load_terms)),
        [VMEM] * (len(load_terms) + 3),
        [(k, species)] * 2 + [rates, grads],
        packed=(2, 3),
    )(*load_terms, lt, lm, lvec)
    new_factors, new_loadings = call(
        functools.partial(output_kernel, half), [VMEM] * 3, [(1, k, cells), (k, species)]
    )(moved_own, moved_oth, newl)
    (own, lik_own, *parts_own), (oth, lik_oth, *parts_oth) = [
        call(
            functools.partial(second_kernel, k, half, sub, start),
            [VMEM] * 4,
            [(k, half), (8, species), (half, species), (half, species)],
            [pltpu.VMEM((species, half), bf16)],
            limit=12,
            packed=(2, 3),
        )(z, ly, lg, held)
        for start, z in ((half, moved_own), (0, moved_oth))
    ]
    (load,) = call(functools.partial(loading_kernel, k, half, sub), [VMEM] * 6, [(k, species + 2 * LANES)])(
        moved_oth, *parts_oth, moved_own, *parts_own
    )
    load_terms, halo = exchange(load)
    own, other = share(own, oth)

    halo = sideways(join_kernel, halo, moved_own, moved_oth)
    edges = upright(new_factors[0, :, :TY], new_factors[0, :, cells - TY :])
    a2, prior_energy = call(
        functools.partial(behind_kernel, k, half), [VMEM] * 7, [(k, half), (k, LANES)]
    )(moved_own, moved_oth, half_own, *edges, gain, svec)
    n_devices = n_site * n_sp
    end_own, endl, shares = call(
        functools.partial(finish_kernel, ride, k, half, len(load_terms), (n_sp // 2, n_site)),
        [VMEM] * (len(load_terms) + 12 + len(halo)),
        [(k, half), (k, species), (n_devices, LANES)],
    )(*load_terms, own, other, a2, moved_own, svec, gain, prior_energy, newl, halfl, lvec, lik_oth, lik_own, *halo)
    end_oth = swap(end_own, "sp", 1)
    shares = lax.all_to_all(shares, ("site", "sp"), 0, 0, tiled=True)
    new_momenta, end_loadings, energy = call(
        functools.partial(last_kernel, half, n_site * cells * n_sp * species),
        [VMEM] * 4,
        [(1, k, cells), (k, species), (1,)],
    )(end_own, end_oth, endl, shares)
    return new_factors, new_momenta, new_loadings.T, end_loadings.T, energy


def solution(mesh):
    placed = (
        P("site", None, "sp"),
        P("site", None, None),
        P("sp", None),
        P("site", None, None),
        P("sp", None),
        P(),
        P(),
        P(),
    )

    return jax.shard_map(
        local,
        mesh=mesh,
        in_specs=placed,
        out_specs=(P("site", None, None), P("site", None, None), P("sp", None), P("sp", None), P()),
        check_vma=False,
    )
```

```python
import functools

import jax
import jax.numpy as jnp
from jax import lax
from jax.experimental import pallas as pl
from jax.experimental.pallas import tpu as pltpu
from jax.sharding import PartitionSpec as P


TY = 64
TGY = 8
LANES = 128

kappa_sq = 0.25
LOG2E = 1.4426950408889634
LN2 = 0.6931471805599453
f32, bf16 = jnp.float32, jnp.bfloat16


VMEM = pl.BlockSpec(memory_space=pltpu.VMEM)
SMEM = pl.BlockSpec(memory_space=pltpu.SMEM)
HBM = pl.BlockSpec(memory_space=pltpu.HBM)


def swap(block, axis, mask):
    return lax.ppermute(block, axis, [(i, i ^ mask) for i in range(lax.axis_size(axis))])


def from_behind(block, axis, distance):
    devices = range(lax.axis_size(axis))
    route = [(i - distance, i) for i in devices if i - distance in devices]
    return lax.ppermute(block, axis, route)


def paired(block, axis, first):
    n = lax.axis_size(axis)
    route = [(i, i + 1 if (i - first) % 2 == 0 else i - 1) for i in range(n)]
    return lax.ppermute(block, axis, [(i, j) for i, j in route if 0 <= j < n])


def mask_groups(n):
    groups, stride = [], 1
    while stride < n:
        radix = 2 if stride == 1 or n // stride == 2 else 4
        groups.append([stride * g for g in range(1, radix)])
        stride *= radix
    return groups


def rides(n_site):
    return n_site == 8 == TGY


def add(terms):
    return functools.reduce(lambda a, b: a + b, terms)


def sum_terms(block, axis, groups):
    terms = [block]
    for masks in groups:
        total = add(terms)
        terms = [total] + [swap(total, axis, m) for m in masks]
    return terms


def call(kernel, in_specs, outs, scratch=(), limit=4, packed=()):
    return pl.pallas_call(
        kernel,
        in_specs=in_specs,
        out_specs=[SMEM if s == (1,) else VMEM for s in outs],
        out_shape=[jax.ShapeDtypeStruct(s, bf16 if i in packed else f32) for i, s in enumerate(outs)],
        scratch_shapes=list(scratch),
        compiler_params=pltpu.CompilerParams(vmem_limit_bytes=limit << 20),
    )


def core():
    return lax.rem(lax.axis_index("sp"), 2)


def split3(x):
    h = x.astype(bf16)
    r = x - h.astype(f32)
    m = r.astype(bf16)
    return h, m, (r - m.astype(f32)).astype(bf16)


def dotg(a, b, ca, cb):
    return lax.dot_general(a, b, (((ca,), (cb,)), ((), ())), preferred_element_type=f32)


def residuals(zb, c, ly):
    h, m, l = split3(zb)
    y = dotg(jnp.concatenate([h, h, h, m, m, l], 0), ly, 0, 0)
    i = jnp.exp2(y)
    r = c - i
    rh = r.astype(bf16)
    return y, i, rh, (r - rh.astype(f32)).astype(bf16), h, m


def loading_terms(h, m, rh, rl, k):
    a = dotg(jnp.concatenate([m, h], 0), rh, 1, 0)
    return a[:k] + a[k:] + dotg(h, rl, 1, 0)


def fill_loadings(lt, ly_ref, lg_ref):
    h, m, l = split3(lt * f32(LOG2E))
    ly_ref[...] = jnp.concatenate([h, m, l, h, m, h], 0)
    h, m, _ = split3(lt)
    lg_ref[...] = jnp.concatenate([m, h], 0)


def fold_lanes(x):
    return add([x[:, j * LANES : (j + 1) * LANES] for j in range(x.shape[1] // LANES)])


def rows_to_8(x):
    return jnp.sum(x.reshape(x.shape[0] // 8, 8, x.shape[1]), 0)


DEPTH = 3


def first_kernel(
    k, half, sub, z_hbm, lt_hbm, cnt_ref, load_ref, lg_ref, held_ref, rho_ref, rlo_ref, rhw_ref, rlw_ref,
    ly_ref, z_ref, lt_ref, buf_ref, sem, sems
):
    c = core()
    pieces = [(rho, at) for rho in (1, 0) for at in range(0, half, sub)]

    def place(i):
        rho, at = pieces[i]
        return pl.multiple_of(lax.rem(rho + c, 2) * half + at, LANES)

    def kept(i):
        return pl.ds(i * sub, sub)

    def copy(i):
        return pltpu.make_async_copy(cnt_ref.at[0, pl.ds(place(i), sub)], buf_ref.at[kept(i)], sem.at[i])

    small = [
        pltpu.make_async_copy(lt_hbm, lt_ref, sems.at[0]),
        pltpu.make_async_copy(z_hbm, z_ref, sems.at[1]),
    ]
    for job in small:
        job.start()
    for i in range(min(DEPTH, len(pieces))):
        copy(i).start()
    small[0].wait()
    fill_loadings(lt_ref[...], ly_ref, lg_ref)
    small[1].wait()
    load_ref[:, -2 * LANES : -LANES], load_ref[:, -LANES:] = pack_rims(vregs_of(z_ref[0]), k)
    ly = ly_ref[...]
    loads = []
    for i, (rho, at) in enumerate(pieces):
        copy(i).wait()
        if i + DEPTH < len(pieces):
            copy(i + DEPTH).start()
        cf = buf_ref[kept(i), :].astype(f32)
        held_ref[kept(i), :] = cf
        _, _, rh, rl, h, m = residuals(z_ref[0, :, pl.ds(place(i), sub)], cf, ly)
        loads.append(loading_terms(h, m, rh, rl, k))
        rh_ref, rl_ref = (rho_ref, rlo_ref) if rho else (rhw_ref, rlw_ref)
        rh_ref[pl.ds(at, sub), :] = rh
        rl_ref[pl.ds(at, sub), :] = rl
    load_ref[:, : -2 * LANES] = add(loads)


def factor_kernel(k, half, sub, lg_ref, rh_ref, rl_ref, fac_ref, turned_ref):
    lg = lg_ref[...]
    for i in range(half // sub):
        rows = pl.ds(i * sub, sub)
        turned_ref[:, rows] = rl_ref[rows, :].T
        a = dotg(lg, rh_ref[rows, :], 1, 1)
        fac_ref[:, rows] = a[:k] + a[k:] + dotg(lg[k:], turned_ref[:, rows], 1, 0)


def move_loadings_kernel(n_terms, *refs):
    terms = refs[:n_terms]
    lt_ref, lm_ref, sl_ref, newl_ref, halfl_ref, ly_ref, lg_ref = refs[n_terms:]
    step = jnp.tile(sl_ref[...], (1, lt_ref.shape[1] // LANES))
    halfl = lm_ref[...] + 0.5 * step * (add([t[:, : lt_ref.shape[1]] for t in terms]) - lt_ref[...])
    newl = lt_ref[...] + step * halfl
    halfl_ref[...] = halfl
    newl_ref[...] = newl
    fill_loadings(newl, ly_ref, lg_ref)


def second_kernel(k, half, sub, start, z_ref, ly_ref, cnt_ref, *refs):
    *before, load_ref, lik_ref, rh_ref, rl_ref = refs
    ly = ly_ref[...]
    loads, likes, sums = [], [], []
    for i in range(half // sub):
        rows = pl.ds(i * sub, sub)
        cf = cnt_ref[pl.ds(start + i * sub, sub), :]
        y, inten, rh, rl, h, m = residuals(z_ref[:, rows], cf, ly)
        rh_ref[rows, :] = rh
        rl_ref[rows, :] = rl
        loads.append(loading_terms(h, m, rh, rl, k))
        likes.append(rows_to_8(cf * y))
        sums.append(rows_to_8(inten))
    lik_ref[...] = add(sums) - f32(LN2) * add(likes)
    if not before:
        load_ref[...] = add(loads)
        return
    part_ref, zw_ref = before
    load_ref[:, : -2 * LANES] = add(loads) + part_ref[...]
    load_ref[:, -2 * LANES : -LANES], load_ref[:, -LANES:] = pack_rims(in_order(zw_ref[...], z_ref[...]), k)


def lane(shape):
    return lax.broadcasted_iota(jnp.int32, shape, len(shape) - 1)


def pack_rims(vregs, k):
    assert len(vregs) <= TY
    q = lax.rem(lane((k, LANES)), TY)
    first = jnp.zeros((k, LANES), f32)
    last = jnp.zeros((k, LANES), f32)
    for j, v in enumerate(vregs):
        first = jnp.where(q == j, pltpu.roll(v, j, 1) if j else v, first)
        last = jnp.where(q == j, pltpu.roll(v, (j - TY + 1) % LANES, 1), last)
    return first, last


def prior_of(vregs, upper, lower, k):
    q = lax.rem(lane((k, LANES)), TY)
    wide = lane((k, LANES))
    n = len(vregs)
    out = []
    for j, v in enumerate(vregs):
        back = jnp.where(q == 0, 0.0, pltpu.roll(v, 1, 1))
        ahead = jnp.where(q == TY - 1, 0.0, pltpu.roll(v, LANES - 1, 1))
        prev = vregs[j - 1] if j else upper
        nxt = vregs[j + 1] if j + 1 < n else lower
        above = jnp.where(wide < TY, pltpu.roll(prev, TY, 1), pltpu.roll(v, TY, 1))
        below = jnp.where(wide >= LANES - TY, pltpu.roll(nxt, LANES - TY, 1), pltpu.roll(v, LANES - TY, 1))
        out.append((kappa_sq + 4.0) * v - (above + below + (back + ahead)))
    return out


def beside_of(left, right, half, k):
    q = lax.rem(lane((k, LANES)), TY)
    n = half // LANES
    low = core() == 0
    left = jnp.where(low, left, pltpu.roll(left, (LANES - n) % LANES, 1))
    right = jnp.where(low, right, pltpu.roll(right, (LANES - n) % LANES, 1))
    out = []
    for j in range(n):
        lrim = pltpu.roll(left, LANES - j, 1) if j else left
        rrim = pltpu.roll(right, (TY - 1 - j) % LANES, 1)
        out.append(jnp.where(q == 0, lrim, 0.0) + jnp.where(q == TY - 1, rrim, 0.0))
    return out


def sides(ride, refs):
    me, n = lax.axis_index("site"), lax.axis_size("site")
    even = lax.rem(me, 2) == 0
    if ride:
        pair, one, three = refs
        near = jnp.where(even, pair[:, -2 * LANES : -LANES], pair[:, -LANES:])
        row = me // 2
        close = (lax.rem(row, 2) == 1) == even
        far = jnp.where(close, one[:, -LANES:], three[:, -LANES:])
    else:
        near, far = refs[0][...], refs[1][...]
    left = jnp.where(me == 0, 0.0, jnp.where(even, far, near))
    right = jnp.where(me == n - 1, 0.0, jnp.where(even, near, far))
    return left, right


def rims_of(vregs, k):
    first, last = pack_rims(vregs, k)
    even = lax.rem(lax.axis_index("site"), 2) == 0
    return jnp.where(even, last, first), jnp.where(even, first, last)


def vregs_of(array):
    return [array[:, j * LANES : (j + 1) * LANES] for j in range(array.shape[1] // LANES)]


def rims_kernel(k, z_ref, near_ref, far_ref):
    near_ref[...], far_ref[...] = rims_of(vregs_of(z_ref[0]), k)


def stage_kernel(own_ref, got_ref, one_ref, two_ref, three_ref):
    both = own_ref[:, : -2 * LANES] + got_ref[:, : -2 * LANES]
    site = lax.axis_index("site")
    even = lax.rem(site, 2) == 0
    first = jnp.where(even, own_ref[:, -2 * LANES : -LANES], got_ref[:, -2 * LANES : -LANES])
    last = jnp.where(even, got_ref[:, -LANES:], own_ref[:, -LANES:])
    low = lax.rem(site // 2, 2) == 0
    one_ref[:, :-LANES] = both
    one_ref[:, -LANES:] = jnp.where(low, last, first)
    two_ref[...] = both
    three_ref[:, :-LANES] = both
    three_ref[:, -LANES:] = jnp.where(low, first, last)


def ahead_kernel(k, half, z_ref, mom_ref, upper_ref, lower_ref, gain_ref, sf_ref, sl_ref, a_ref, z_own_ref, s_ref, l_ref):
    c = core()
    step = sf_ref[0]
    out = prior_of(vregs_of(z_ref[0]), upper_ref[...], lower_ref[...], k)
    n = half // LANES
    gain = gain_ref[...] * (0.5 * step)
    for j in range(n):
        at = pl.ds(j * LANES, LANES)
        own = jnp.where(c == 0, out[j], out[n + j])
        src = pl.ds(pl.multiple_of(c * half + j * LANES, LANES), LANES)
        a_ref[:, at] = mom_ref[0, :, src] - gain * own
        z_own_ref[:, at] = z_ref[0, :, src]
    s_ref[...] = jnp.full(s_ref.shape, step, f32)
    l_ref[...] = jnp.full(l_ref.shape, sl_ref[0], f32)


def move_kernel(ride, k, half, own_ref, other_ref, a_ref, z_ref, s_ref, gain_ref, *refs):
    *halo, half_ref, moved_ref = refs
    beside = beside_of(*sides(ride, halo), half, k)
    step, gain = s_ref[...], gain_ref[...]
    for j in range(half // LANES):
        at = pl.ds(j * LANES, LANES)
        h = a_ref[:, at] + (0.5 * step) * ((own_ref[:, at] + other_ref[:, at]) + gain * beside[j])
        half_ref[:, at] = h
        moved_ref[:, at] = z_ref[:, at] + step * h


def in_order(own, oth):
    first = core() == 0
    own, oth = vregs_of(own), vregs_of(oth)
    return [jnp.where(first, a, b) for a, b in zip(own, oth)] + [jnp.where(first, b, a) for a, b in zip(own, oth)]


def join_kernel(k, own_ref, oth_ref, near_ref, far_ref):
    near_ref[...], far_ref[...] = rims_of(in_order(own_ref[...], oth_ref[...]), k)


def behind_kernel(k, half, own_ref, oth_ref, h_ref, upper_ref, lower_ref, gain_ref, s_ref, a_ref, e_ref):
    c = core()
    out = prior_of(in_order(own_ref[...], oth_ref[...]), upper_ref[...], lower_ref[...], k)
    n = half // LANES
    gain = gain_ref[...]
    energy = jnp.zeros((k, LANES), f32)
    for j in range(n):
        at = pl.ds(j * LANES, LANES)
        own = gain * jnp.where(c == 0, out[j], out[n + j])
        energy = energy + own_ref[:, at] * own
        a_ref[:, at] = h_ref[:, at] - (0.5 * s_ref[...]) * own
    e_ref[...] = energy


def finish_kernel(ride, k, half, n_terms, shares, *refs):
    terms = refs[:n_terms]
    own_ref, other_ref, a_ref, z_ref, s_ref, gain_ref, pe_ref, newl_ref, halfl_ref, sl_ref = refs[n_terms : n_terms + 10]
    liko_ref, likw_ref, *halo, end_ref, endl_ref, share_ref = refs[n_terms + 10 :]
    beside = beside_of(*sides(ride, halo), half, k)
    step, gain = s_ref[...], gain_ref[...]
    energy = pe_ref[...]
    for j in range(half // LANES):
        at = pl.ds(j * LANES, LANES)
        rim = gain * beside[j]
        e = a_ref[:, at] + (0.5 * step) * ((own_ref[:, at] + other_ref[:, at]) + rim)
        end_ref[:, at] = e
        energy = energy + (e * e - z_ref[:, at] * rim)
    newl = newl_ref[...]
    species = newl.shape[1]
    load = add([t[:, :species] for t in terms])
    step = jnp.tile(sl_ref[...], (1, species // LANES))
    endl = halfl_ref[...] + (0.5 * step) * (load - newl)
    endl_ref[...] = endl
    share = (0.5 / shares[0]) * energy + (0.5 / shares[1]) * fold_lanes(endl * endl + newl * newl)
    share = jnp.sum(share, 0, keepdims=True) + jnp.sum(fold_lanes(liko_ref[...] + likw_ref[...]), 0, keepdims=True)
    share_ref[...] = jnp.broadcast_to(share, share_ref.shape)


def output_kernel(half, own_ref, oth_ref, loadings_ref, full_ref, out_ref):
    c = core()
    own, oth = own_ref[...], oth_ref[...]
    full_ref[0, :, :half] = jnp.where(c == 0, own, oth)
    full_ref[0, :, half:] = jnp.where(c == 0, oth, own)
    out_ref[...] = loadings_ref[...]


def last_kernel(half, entries, own_ref, oth_ref, loadings_ref, shares_ref, full_ref, out_ref, energy_ref):
    output_kernel(half, own_ref, oth_ref, loadings_ref, full_ref, out_ref)
    energy_ref[0] = jnp.sum(shares_ref[...]) / entries


def local(
    counts, factors, loadings, factor_momenta, loading_momenta, precision, factor_step, loading_step
):
    k, cells = factors.shape[1:]
    species = loadings.shape[0]
    half = cells // 2
    sub = 640 if half % 640 == 0 else half
    n_site, n_sp = lax.axis_size("site"), lax.axis_size("sp")
    site, chips = mask_groups(n_site), mask_groups(n_sp)[1:]
    lt, lm = loadings.T, loading_momenta.T
    gain = jnp.broadcast_to(precision[:, None], (k, LANES))
    zero_rim = jnp.zeros((k, LANES), f32)

    ride = rides(n_site)

    def exchange(load):
        if not ride:
            return sum_terms(load, "site", site), ()
        got = swap(load, "site", 1)
        wide, narrow = (k, species + LANES), (k, species)
        stage = call(stage_kernel, [VMEM] * 2, [wide, narrow, wide])(load, got)
        terms = [swap(t, "site", m) for t, m in zip(stage, site[1])]
        return [stage[1], *terms], (got, terms[0], terms[2])

    def upright(low, high):
        if n_site <= TGY:
            return zero_rim, zero_rim
        lead = jnp.zeros((k, LANES - TY), f32)
        upper = jnp.concatenate([lead, from_behind(high, "site", TGY)], 1)
        return upper, jnp.concatenate([from_behind(low, "site", -TGY), lead], 1)

    def sideways(kernel, halo, *arrays):
        if ride:
            return halo
        near, far = call(functools.partial(kernel, k), [VMEM] * len(arrays), [(k, LANES)] * 2)(*arrays)
        return paired(near, "site", 0), paired(far, "site", 1)

    def share(own, oth):
        terms = sum_terms(own + swap(oth, "sp", 1), "sp", chips)
        return terms[0], add(terms[1:])

    rates, grads = (6 * k, species), (2 * k, species)
    load, lg, held, rho, rlo, rhw, rlw = call(
        functools.partial(first_kernel, k, half, sub),
        [HBM, HBM, HBM],
        [(k, species + 2 * LANES), grads, (cells, species)] + [(half, species)] * 4,
        [
            pltpu.VMEM(rates, bf16),
            pltpu.VMEM((1, k, cells), f32),
            pltpu.VMEM((k, species), f32),
            pltpu.VMEM((cells, species), jnp.int32),
            pltpu.SemaphoreType.DMA((cells // sub,)),
            pltpu.SemaphoreType.DMA((2,)),
        ],
        16,
        (1, 3, 4, 5, 6),
    )(*[pltpu.with_memory_space_constraint(x, pltpu.HBM) for x in (factors, lt, counts)])
    load_terms, halo = exchange(load)

    def factors_of(lg, rh, rl):
        kernel = functools.partial(factor_kernel, k, half, sub)
        scratch = [pltpu.VMEM((species, half), bf16)]
        return call(kernel, [VMEM] * 3, [(k, half)], scratch, limit=6)(lg, rh, rl)[0]

    oth = factors_of(lg, rho, rlo)
    own = factors_of(lg, rhw, rlw)
    own, other = share(own, oth)

    halo = sideways(rims_kernel, halo, factors)
    edges = upright(factors[0, :, :TY], factors[0, :, cells - TY :])
    a1, z_own, svec, lvec = call(
        functools.partial(ahead_kernel, k, half),
        [VMEM] * 5 + [SMEM] * 2,
        [(k, half), (k, half), (k, LANES), (k, LANES)],
    )(factors, factor_momenta, *edges, gain, factor_step, loading_step)
    half_own, moved_own = call(
        functools.partial(move_kernel, ride, k, half), [VMEM] * (6 + len(halo)), [(k, half)] * 2
    )(own, other, a1, z_own, svec, gain, *halo)
    moved_oth = swap(moved_own, "sp", 1)

    newl, halfl, ly, lg = call(
        functools.partial(move_loadings_kernel, len(load_terms)),
        [VMEM] * (len(load_terms) + 3),
        [(k, species)] * 2 + [rates, grads],
        packed=(2, 3),
    )(*load_terms, lt, lm, lvec)
    new_factors, new_loadings = call(
        functools.partial(output_kernel, half), [VMEM] * 3, [(1, k, cells), (k, species)]
    )(moved_own, moved_oth, newl)

    def second(start, z, before, load_shape):
        return call(
            functools.partial(second_kernel, k, half, sub, start),
            [VMEM] * (3 + len(before)),
            [load_shape, (8, species), (half, species), (half, species)],
            limit=8,
            packed=(2, 3),
        )(z, ly, held, *before)

    load, lik_own, rhw, rlw = second(half, moved_own, (), (k, species))
    load, lik_oth, rho, rlo = second(0, moved_oth, (load, moved_own), (k, species + 2 * LANES))
    oth = factors_of(lg, rho, rlo)
    own = factors_of(lg, rhw, rlw)
    load_terms, halo = exchange(load)
    own, other = share(own, oth)

    halo = sideways(join_kernel, halo, moved_own, moved_oth)
    edges = upright(new_factors[0, :, :TY], new_factors[0, :, cells - TY :])
    a2, prior_energy = call(
        functools.partial(behind_kernel, k, half), [VMEM] * 7, [(k, half), (k, LANES)]
    )(moved_own, moved_oth, half_own, *edges, gain, svec)
    n_devices = n_site * n_sp
    end_own, endl, shares = call(
        functools.partial(finish_kernel, ride, k, half, len(load_terms), (n_sp // 2, n_site)),
        [VMEM] * (len(load_terms) + 12 + len(halo)),
        [(k, half), (k, species), (n_devices, LANES)],
    )(*load_terms, own, other, a2, moved_own, svec, gain, prior_energy, newl, halfl, lvec, lik_oth, lik_own, *halo)
    end_oth = swap(end_own, "sp", 1)
    shares = lax.all_to_all(shares, ("site", "sp"), 0, 0, tiled=True)
    new_momenta, end_loadings, energy = call(
        functools.partial(last_kernel, half, n_site * cells * n_sp * species),
        [VMEM] * 4,
        [(1, k, cells), (k, species), (1,)],
    )(end_own, end_oth, endl, shares)
    return new_factors, new_momenta, new_loadings.T, end_loadings.T, energy


def solution(mesh):
    placed = (
        P("site", None, "sp"),
        P("site", None, None),
        P("sp", None),
        P("site", None, None),
        P("sp", None),
        P(),
        P(),
        P(),
    )

    return jax.shard_map(
        local,
        mesh=mesh,
        in_specs=placed,
        out_specs=(P("site", None, None), P("site", None, None), P("sp", None), P("sp", None), P()),
        check_vma=False,
    )
```

```python
import functools

import jax
import jax.numpy as jnp
from jax import lax
from jax.experimental import pallas as pl
from jax.experimental.pallas import tpu as pltpu
from jax.sharding import PartitionSpec as P


TY = 64
TGY = 8
LANES = 128

kappa_sq = 0.25
LOG2E = 1.4426950408889634
LN2 = 0.6931471805599453
f32, bf16 = jnp.float32, jnp.bfloat16


VMEM = pl.BlockSpec(memory_space=pltpu.VMEM)
SMEM = pl.BlockSpec(memory_space=pltpu.SMEM)
HBM = pl.BlockSpec(memory_space=pltpu.HBM)


def swap(block, axis, mask):
    return lax.ppermute(block, axis, [(i, i ^ mask) for i in range(lax.axis_size(axis))])


def from_behind(block, axis, distance):
    devices = range(lax.axis_size(axis))
    route = [(i - distance, i) for i in devices if i - distance in devices]
    return lax.ppermute(block, axis, route)


def paired(block, axis, first):
    n = lax.axis_size(axis)
    route = [(i, i + 1 if (i - first) % 2 == 0 else i - 1) for i in range(n)]
    return lax.ppermute(block, axis, [(i, j) for i, j in route if 0 <= j < n])


def split_swap(block, masks):
    n_site, n_sp = lax.axis_size("site"), lax.axis_size("sp")
    route = [(i * n_sp + j, (i ^ masks[j % 2]) * n_sp + j) for i in range(n_site) for j in range(n_sp)]
    return lax.ppermute(block, ("site", "sp"), route)


def mask_groups(n):
    groups, stride = [], 1
    while stride < n:
        radix = 2 if stride == 1 or n // stride == 2 else 4
        groups.append([stride * g for g in range(1, radix)])
        stride *= radix
    return groups


def rides(n_site):
    return n_site == 8 == TGY


def add(terms):
    return functools.reduce(lambda a, b: a + b, terms)


def sum_terms(block, axis, groups):
    terms = [block]
    for masks in groups:
        total = add(terms)
        terms = [total] + [swap(total, axis, m) for m in masks]
    return terms


def call(kernel, in_specs, outs, scratch=(), limit=4, packed=()):
    return pl.pallas_call(
        kernel,
        in_specs=in_specs,
        out_specs=[SMEM if s == (1,) else VMEM for s in outs],
        out_shape=[jax.ShapeDtypeStruct(s, bf16 if i in packed else f32) for i, s in enumerate(outs)],
        scratch_shapes=list(scratch),
        compiler_params=pltpu.CompilerParams(vmem_limit_bytes=limit << 20),
    )


def core():
    return lax.rem(lax.axis_index("sp"), 2)


def split3(x):
    h = x.astype(bf16)
    r = x - h.astype(f32)
    m = r.astype(bf16)
    return h, m, (r - m.astype(f32)).astype(bf16)


def dotg(a, b, ca, cb):
    return lax.dot_general(a, b, (((ca,), (cb,)), ((), ())), preferred_element_type=f32)


def residuals(zb, c, ly):
    h, m, l = split3(zb)
    y = dotg(jnp.concatenate([h, h, h, m, m, l], 0), ly, 0, 0)
    i = jnp.exp2(y)
    r = c - i
    rh = r.astype(bf16)
    return y, i, rh, (r - rh.astype(f32)).astype(bf16), h, m


def loading_terms(h, m, rh, rl, k):
    a = dotg(jnp.concatenate([m, h], 0), rh, 1, 0)
    return a[:k] + a[k:] + dotg(h, rl, 1, 0)


def fill_loadings(lt, ly_ref, lg_ref):
    h, m, l = split3(lt * f32(LOG2E))
    ly_ref[...] = jnp.concatenate([h, m, l, h, m, h], 0)
    h, m, _ = split3(lt)
    lg_ref[...] = jnp.concatenate([m, h], 0)


def fold_lanes(x):
    return add([x[:, j * LANES : (j + 1) * LANES] for j in range(x.shape[1] // LANES)])


def rows_to_8(x):
    return jnp.sum(x.reshape(x.shape[0] // 8, 8, x.shape[1]), 0)


DEPTH = 3


def first_kernel(
    k, half, sub, z_hbm, lt_hbm, cnt_ref, load_ref, lg_ref, held_ref, rho_ref, rlo_ref, rhw_ref, rlw_ref,
    ly_ref, z_ref, lt_ref, buf_ref, sem, sems
):
    c = core()
    pieces = [(rho, at) for rho in (1, 0) for at in range(0, half, sub)]

    def place(i):
        rho, at = pieces[i]
        return pl.multiple_of(lax.rem(rho + c, 2) * half + at, LANES)

    def kept(i):
        return pl.ds(i * sub, sub)

    def copy(i):
        return pltpu.make_async_copy(cnt_ref.at[0, pl.ds(place(i), sub)], buf_ref.at[kept(i)], sem.at[i])

    small = [
        pltpu.make_async_copy(lt_hbm, lt_ref, sems.at[0]),
        pltpu.make_async_copy(z_hbm, z_ref, sems.at[1]),
    ]
    for job in small:
        job.start()
    for i in range(min(DEPTH, len(pieces))):
        copy(i).start()
    small[0].wait()
    fill_loadings(lt_ref[...], ly_ref, lg_ref)
    small[1].wait()
    load_ref[:, -2 * LANES : -LANES], load_ref[:, -LANES:] = pack_rims(vregs_of(z_ref[0]), k)
    ly = ly_ref[...]
    loads = []
    for i, (rho, at) in enumerate(pieces):
        copy(i).wait()
        if i + DEPTH < len(pieces):
            copy(i + DEPTH).start()
        cf = buf_ref[kept(i), :].astype(f32)
        held_ref[kept(i), :] = cf
        _, _, rh, rl, h, m = residuals(z_ref[0, :, pl.ds(place(i), sub)], cf, ly)
        loads.append(loading_terms(h, m, rh, rl, k))
        rh_ref, rl_ref = (rho_ref, rlo_ref) if rho else (rhw_ref, rlw_ref)
        rh_ref[pl.ds(at, sub), :] = rh
        rl_ref[pl.ds(at, sub), :] = rl
    load_ref[:, : -2 * LANES] = add(loads)


def factor_kernel(k, half, sub, lg_ref, rh_ref, rl_ref, fac_ref, turned_ref):
    lg = lg_ref[...]
    for i in range(half // sub):
        rows = pl.ds(i * sub, sub)
        turned_ref[:, rows] = rl_ref[rows, :].T
        a = dotg(lg, rh_ref[rows, :], 1, 1)
        fac_ref[:, rows] = a[:k] + a[k:] + dotg(lg[k:], turned_ref[:, rows], 1, 0)


def move_loadings_kernel(n_terms, *refs):
    terms = refs[:n_terms]
    lt_ref, lm_ref, sl_ref, newl_ref, halfl_ref, ly_ref, lg_ref = refs[n_terms:]
    step = jnp.tile(sl_ref[...], (1, lt_ref.shape[1] // LANES))
    halfl = lm_ref[...] + 0.5 * step * (add([t[:, : lt_ref.shape[1]] for t in terms]) - lt_ref[...])
    newl = lt_ref[...] + step * halfl
    halfl_ref[...] = halfl
    newl_ref[...] = newl
    fill_loadings(newl, ly_ref, lg_ref)


def second_kernel(k, half, sub, start, z_ref, ly_ref, cnt_ref, *refs):
    *before, load_ref, lik_ref, rh_ref, rl_ref = refs
    ly = ly_ref[...]
    loads, likes, sums = [], [], []
    for i in range(half // sub):
        rows = pl.ds(i * sub, sub)
        cf = cnt_ref[pl.ds(start + i * sub, sub), :]
        y, inten, rh, rl, h, m = residuals(z_ref[:, rows], cf, ly)
        rh_ref[rows, :] = rh
        rl_ref[rows, :] = rl
        loads.append(loading_terms(h, m, rh, rl, k))
        likes.append(rows_to_8(cf * y))
        sums.append(rows_to_8(inten))
    lik_ref[...] = add(sums) - f32(LN2) * add(likes)
    if not before:
        load_ref[...] = add(loads)
        return
    part_ref, zw_ref = before
    load_ref[:, : -2 * LANES] = add(loads) + part_ref[...]
    load_ref[:, -2 * LANES : -LANES], load_ref[:, -LANES:] = pack_rims(in_order(zw_ref[...], z_ref[...]), k)


def lane(shape):
    return lax.broadcasted_iota(jnp.int32, shape, len(shape) - 1)


def pack_rims(vregs, k):
    assert len(vregs) <= TY
    q = lax.rem(lane((k, LANES)), TY)
    first = jnp.zeros((k, LANES), f32)
    last = jnp.zeros((k, LANES), f32)
    for j, v in enumerate(vregs):
        first = jnp.where(q == j, pltpu.roll(v, j, 1) if j else v, first)
        last = jnp.where(q == j, pltpu.roll(v, (j - TY + 1) % LANES, 1), last)
    return first, last


def prior_of(vregs, upper, lower, k):
    q = lax.rem(lane((k, LANES)), TY)
    wide = lane((k, LANES))
    n = len(vregs)
    out = []
    for j, v in enumerate(vregs):
        back = jnp.where(q == 0, 0.0, pltpu.roll(v, 1, 1))
        ahead = jnp.where(q == TY - 1, 0.0, pltpu.roll(v, LANES - 1, 1))
        prev = vregs[j - 1] if j else upper
        nxt = vregs[j + 1] if j + 1 < n else lower
        above = jnp.where(wide < TY, pltpu.roll(prev, TY, 1), pltpu.roll(v, TY, 1))
        below = jnp.where(wide >= LANES - TY, pltpu.roll(nxt, LANES - TY, 1), pltpu.roll(v, LANES - TY, 1))
        out.append((kappa_sq + 4.0) * v - (above + below + (back + ahead)))
    return out


def beside_of(left, right, half, k):
    q = lax.rem(lane((k, LANES)), TY)
    n = half // LANES
    low = core() == 0
    left = jnp.where(low, left, pltpu.roll(left, (LANES - n) % LANES, 1))
    right = jnp.where(low, right, pltpu.roll(right, (LANES - n) % LANES, 1))
    out = []
    for j in range(n):
        lrim = pltpu.roll(left, LANES - j, 1) if j else left
        rrim = pltpu.roll(right, (TY - 1 - j) % LANES, 1)
        out.append(jnp.where(q == 0, lrim, 0.0) + jnp.where(q == TY - 1, rrim, 0.0))
    return out


def sides(ride, refs):
    me, n = lax.axis_index("site"), lax.axis_size("site")
    even = lax.rem(me, 2) == 0
    if ride:
        pair, one, three = refs
        near = jnp.where(even, pair[:, -2 * LANES : -LANES], pair[:, -LANES:])
        row = me // 2
        close = (lax.rem(row, 2) == 1) == even
        far = jnp.where(close == (core() == 0), one[:, -LANES:], three[:, -LANES:])
    else:
        near, far = refs[0][...], refs[1][...]
    left = jnp.where(me == 0, 0.0, jnp.where(even, far, near))
    right = jnp.where(me == n - 1, 0.0, jnp.where(even, near, far))
    return left, right


def rims_of(vregs, k):
    first, last = pack_rims(vregs, k)
    even = lax.rem(lax.axis_index("site"), 2) == 0
    return jnp.where(even, last, first), jnp.where(even, first, last)


def vregs_of(array):
    return [array[:, j * LANES : (j + 1) * LANES] for j in range(array.shape[1] // LANES)]


def rims_kernel(k, z_ref, near_ref, far_ref):
    near_ref[...], far_ref[...] = rims_of(vregs_of(z_ref[0]), k)


def stage_kernel(own_ref, got_ref, one_ref, two_ref, three_ref):
    both = own_ref[:, : -2 * LANES] + got_ref[:, : -2 * LANES]
    site = lax.axis_index("site")
    even = lax.rem(site, 2) == 0
    first = jnp.where(even, own_ref[:, -2 * LANES : -LANES], got_ref[:, -2 * LANES : -LANES])
    last = jnp.where(even, got_ref[:, -LANES:], own_ref[:, -LANES:])
    low = (lax.rem(site // 2, 2) == 0) == (core() == 0)
    one_ref[:, :-LANES] = both
    one_ref[:, -LANES:] = jnp.where(low, last, first)
    two_ref[...] = both
    three_ref[:, :-LANES] = both
    three_ref[:, -LANES:] = jnp.where(low, first, last)


def ahead_kernel(k, half, z_ref, mom_ref, upper_ref, lower_ref, gain_ref, sf_ref, sl_ref, a_ref, z_own_ref, s_ref, l_ref):
    c = core()
    step = sf_ref[0]
    out = prior_of(vregs_of(z_ref[0]), upper_ref[...], lower_ref[...], k)
    n = half // LANES
    gain = gain_ref[...] * (0.5 * step)
    for j in range(n):
        at = pl.ds(j * LANES, LANES)
        own = jnp.where(c == 0, out[j], out[n + j])
        src = pl.ds(pl.multiple_of(c * half + j * LANES, LANES), LANES)
        a_ref[:, at] = mom_ref[0, :, src] - gain * own
        z_own_ref[:, at] = z_ref[0, :, src]
    s_ref[...] = jnp.full(s_ref.shape, step, f32)
    l_ref[...] = jnp.full(l_ref.shape, sl_ref[0], f32)


def move_kernel(ride, k, half, own_ref, other_ref, a_ref, z_ref, s_ref, gain_ref, *refs):
    *halo, half_ref, moved_ref = refs
    beside = beside_of(*sides(ride, halo), half, k)
    step, gain = s_ref[...], gain_ref[...]
    for j in range(half // LANES):
        at = pl.ds(j * LANES, LANES)
        h = a_ref[:, at] + (0.5 * step) * ((own_ref[:, at] + other_ref[:, at]) + gain * beside[j])
        half_ref[:, at] = h
        moved_ref[:, at] = z_ref[:, at] + step * h


def in_order(own, oth):
    first = core() == 0
    own, oth = vregs_of(own), vregs_of(oth)
    return [jnp.where(first, a, b) for a, b in zip(own, oth)] + [jnp.where(first, b, a) for a, b in zip(own, oth)]


def join_kernel(k, own_ref, oth_ref, near_ref, far_ref):
    near_ref[...], far_ref[...] = rims_of(in_order(own_ref[...], oth_ref[...]), k)


def behind_kernel(k, half, own_ref, oth_ref, h_ref, upper_ref, lower_ref, gain_ref, s_ref, a_ref, e_ref):
    c = core()
    out = prior_of(in_order(own_ref[...], oth_ref[...]), upper_ref[...], lower_ref[...], k)
    n = half // LANES
    gain = gain_ref[...]
    energy = jnp.zeros((k, LANES), f32)
    for j in range(n):
        at = pl.ds(j * LANES, LANES)
        own = gain * jnp.where(c == 0, out[j], out[n + j])
        energy = energy + own_ref[:, at] * own
        a_ref[:, at] = h_ref[:, at] - (0.5 * s_ref[...]) * own
    e_ref[...] = energy


def finish_kernel(ride, k, half, n_terms, shares, *refs):
    terms = refs[:n_terms]
    own_ref, other_ref, a_ref, z_ref, s_ref, gain_ref, pe_ref, newl_ref, halfl_ref, sl_ref = refs[n_terms : n_terms + 10]
    liko_ref, likw_ref, *halo, end_ref, endl_ref, share_ref = refs[n_terms + 10 :]
    beside = beside_of(*sides(ride, halo), half, k)
    step, gain = s_ref[...], gain_ref[...]
    energy = pe_ref[...]
    for j in range(half // LANES):
        at = pl.ds(j * LANES, LANES)
        rim = gain * beside[j]
        e = a_ref[:, at] + (0.5 * step) * ((own_ref[:, at] + other_ref[:, at]) + rim)
        end_ref[:, at] = e
        energy = energy + (e * e - z_ref[:, at] * rim)
    newl = newl_ref[...]
    species = newl.shape[1]
    load = add([t[:, :species] for t in terms])
    step = jnp.tile(sl_ref[...], (1, species // LANES))
    endl = halfl_ref[...] + (0.5 * step) * (load - newl)
    endl_ref[...] = endl
    share = (0.5 / shares[0]) * energy + (0.5 / shares[1]) * fold_lanes(endl * endl + newl * newl)
    share = jnp.sum(share, 0, keepdims=True) + jnp.sum(fold_lanes(liko_ref[...] + likw_ref[...]), 0, keepdims=True)
    share_ref[...] = jnp.broadcast_to(share, share_ref.shape)


def output_kernel(half, own_ref, oth_ref, loadings_ref, full_ref, out_ref):
    c = core()
    own, oth = own_ref[...], oth_ref[...]
    full_ref[0, :, :half] = jnp.where(c == 0, own, oth)
    full_ref[0, :, half:] = jnp.where(c == 0, oth, own)
    out_ref[...] = loadings_ref[...]


def last_kernel(half, entries, own_ref, oth_ref, loadings_ref, shares_ref, full_ref, out_ref, energy_ref):
    output_kernel(half, own_ref, oth_ref, loadings_ref, full_ref, out_ref)
    energy_ref[0] = jnp.sum(shares_ref[...]) / entries


def local(
    counts, factors, loadings, factor_momenta, loading_momenta, precision, factor_step, loading_step
):
    k, cells = factors.shape[1:]
    species = loadings.shape[0]
    half = cells // 2
    sub = 640 if half % 640 == 0 else half
    n_site, n_sp = lax.axis_size("site"), lax.axis_size("sp")
    site, chips = mask_groups(n_site), mask_groups(n_sp)[1:]
    lt, lm = loadings.T, loading_momenta.T
    gain = jnp.broadcast_to(precision[:, None], (k, LANES))
    zero_rim = jnp.zeros((k, LANES), f32)

    ride = rides(n_site)

    def exchange(load):
        if not ride:
            return sum_terms(load, "site", site), ()
        got = swap(load, "site", 1)
        wide, narrow = (k, species + LANES), (k, species)
        stage = call(stage_kernel, [VMEM] * 2, [wide, narrow, wide])(load, got)
        masks = zip(site[1], site[1][::-1])
        terms = [split_swap(t, m) for t, m in zip(stage, masks)]
        return [stage[1], *terms], (got, terms[0], terms[2])

    def upright(low, high):
        if n_site <= TGY:
            return zero_rim, zero_rim
        lead = jnp.zeros((k, LANES - TY), f32)
        upper = jnp.concatenate([lead, from_behind(high, "site", TGY)], 1)
        return upper, jnp.concatenate([from_behind(low, "site", -TGY), lead], 1)

    def sideways(kernel, halo, *arrays):
        if ride:
            return halo
        near, far = call(functools.partial(kernel, k), [VMEM] * len(arrays), [(k, LANES)] * 2)(*arrays)
        return paired(near, "site", 0), paired(far, "site", 1)

    def share(own, oth):
        terms = sum_terms(own + swap(oth, "sp", 1), "sp", chips)
        return terms[0], add(terms[1:])

    rates, grads = (6 * k, species), (2 * k, species)
    load, lg, held, rho, rlo, rhw, rlw = call(
        functools.partial(first_kernel, k, half, sub),
        [HBM, HBM, HBM],
        [(k, species + 2 * LANES), grads, (cells, species)] + [(half, species)] * 4,
        [
            pltpu.VMEM(rates, bf16),
            pltpu.VMEM((1, k, cells), f32),
            pltpu.VMEM((k, species), f32),
            pltpu.VMEM((cells, species), jnp.int32),
            pltpu.SemaphoreType.DMA((cells // sub,)),
            pltpu.SemaphoreType.DMA((2,)),
        ],
        16,
        (1, 3, 4, 5, 6),
    )(*[pltpu.with_memory_space_constraint(x, pltpu.HBM) for x in (factors, lt, counts)])
    load_terms, halo = exchange(load)

    def factors_of(lg, rh, rl):
        kernel = functools.partial(factor_kernel, k, half, sub)
        scratch = [pltpu.VMEM((species, half), bf16)]
        return call(kernel, [VMEM] * 3, [(k, half)], scratch, limit=6)(lg, rh, rl)[0]

    oth = factors_of(lg, rho, rlo)
    own = factors_of(lg, rhw, rlw)
    own, other = share(own, oth)

    halo = sideways(rims_kernel, halo, factors)
    edges = upright(factors[0, :, :TY], factors[0, :, cells - TY :])
    a1, z_own, svec, lvec = call(
        functools.partial(ahead_kernel, k, half),
        [VMEM] * 5 + [SMEM] * 2,
        [(k, half), (k, half), (k, LANES), (k, LANES)],
    )(factors, factor_momenta, *edges, gain, factor_step, loading_step)
    half_own, moved_own = call(
        functools.partial(move_kernel, ride, k, half), [VMEM] * (6 + len(halo)), [(k, half)] * 2
    )(own, other, a1, z_own, svec, gain, *halo)
    moved_oth = swap(moved_own, "sp", 1)

    newl, halfl, ly, lg = call(
        functools.partial(move_loadings_kernel, len(load_terms)),
        [VMEM] * (len(load_terms) + 3),
        [(k, species)] * 2 + [rates, grads],
        packed=(2, 3),
    )(*load_terms, lt, lm, lvec)
    new_factors, new_loadings = call(
        functools.partial(output_kernel, half), [VMEM] * 3, [(1, k, cells), (k, species)]
    )(moved_own, moved_oth, newl)

    def second(start, z, before, load_shape):
        return call(
            functools.partial(second_kernel, k, half, sub, start),
            [VMEM] * (3 + len(before)),
            [load_shape, (8, species), (half, species), (half, species)],
            limit=8,
            packed=(2, 3),
        )(z, ly, held, *before)

    load, lik_own, rhw, rlw = second(half, moved_own, (), (k, species))
    load, lik_oth, rho, rlo = second(0, moved_oth, (load, moved_own), (k, species + 2 * LANES))
    oth = factors_of(lg, rho, rlo)
    own = factors_of(lg, rhw, rlw)
    load_terms, halo = exchange(load)
    own, other = share(own, oth)

    halo = sideways(join_kernel, halo, moved_own, moved_oth)
    edges = upright(new_factors[0, :, :TY], new_factors[0, :, cells - TY :])
    a2, prior_energy = call(
        functools.partial(behind_kernel, k, half), [VMEM] * 7, [(k, half), (k, LANES)]
    )(moved_own, moved_oth, half_own, *edges, gain, svec)
    n_devices = n_site * n_sp
    end_own, endl, shares = call(
        functools.partial(finish_kernel, ride, k, half, len(load_terms), (n_sp // 2, n_site)),
        [VMEM] * (len(load_terms) + 12 + len(halo)),
        [(k, half), (k, species), (n_devices, LANES)],
    )(*load_terms, own, other, a2, moved_own, svec, gain, prior_energy, newl, halfl, lvec, lik_oth, lik_own, *halo)
    end_oth = swap(end_own, "sp", 1)
    shares = lax.all_to_all(shares, ("site", "sp"), 0, 0, tiled=True)
    new_momenta, end_loadings, energy = call(
        functools.partial(last_kernel, half, n_site * cells * n_sp * species),
        [VMEM] * 4,
        [(1, k, cells), (k, species), (1,)],
    )(end_own, end_oth, endl, shares)
    return new_factors, new_momenta, new_loadings.T, end_loadings.T, energy


def solution(mesh):
    placed = (
        P("site", None, "sp"),
        P("site", None, None),
        P("sp", None),
        P("site", None, None),
        P("sp", None),
        P(),
        P(),
        P(),
    )

    return jax.shard_map(
        local,
        mesh=mesh,
        in_specs=placed,
        out_specs=(P("site", None, None), P("site", None, None), P("sp", None), P("sp", None), P()),
        check_vma=False,
    )
```
